128 devices in a mesh: req: 4 (over y), seq: 32 (over x, z, core).
Axes of the slice: x: 4, y: 4, z: 4, core: 2. Of those that a mesh axis runs over, the one named last changes fastest.
Arguments:
- hidden_in: bfloat16 [4, 4096, 1600], P('req', 'seq'), may hold values from -6 to 6
- mamba_in: bfloat16 [4, 4096, 3200], P('req', 'seq'), may hold values from -6 to 6
- conv_weight: float32 [4, 3200], replicated, may hold values from -3 to 3
- conv_bias: float32 [3200], replicated, may hold values from -3 to 3
- x_proj: bfloat16 [3200, 132], replicated, may hold values from -0.109375 to 0.109375
- dt_proj: bfloat16 [100, 3200], replicated, may hold values from -0.625 to 0.625
- dt_bias: float32 [3200], replicated, may hold values from -2 to 0.5
- decay_rate: float32 [3200], replicated, may hold values from 2.4414063e-05 to 0.05
- skip_gain: float32 [3200], replicated, may hold values from 0.5 to 1.5
- out_proj: bfloat16 [3200, 1600], replicated, may hold values from -0.109375 to 0.109375
- norm_gain: float32 [1600], replicated, may hold values from 0.3 to 1.7
- mlp_gate: bfloat16 [1600, 5504], P(None, 'req'), may hold values from -0.15625 to 0.15625
- mlp_up: bfloat16 [1600, 5504], P(None, 'req'), may hold values from -0.15625 to 0.15625
- mlp_down: bfloat16 [5504, 1600], P('req'), may hold values from -0.078125 to 0.078125
- cache_state: float32 [4, 32, 16, 3200], P('req', 'seq'), may hold values from -6 to 6
- cache_edge: bfloat16 [4, 32, 3, 3200], P('req', 'seq'), may hold values from -6 to 6
- req_lengths: int32 [4, 4], P('req'), may hold values from 1 to 3072, 4096 in all within a row
- cont_flag: int32 [4, 4], P('req'), may hold values from 0 to 1, as said below
- cache_source: int32 [4, 4], P('req'), may hold values from 0 to 31, as said below
- owner_slot: int32 [4, 4], P('req'), may hold values from 0 to 31, as said below
Outputs:
- block_out: bfloat16 [4, 4096, 1600], P('req', 'seq')
- new_state: float32 [4, 32, 16, 3200], P('req', 'seq')
- new_edge: bfloat16 [4, 32, 3, 3200], P('req', 'seq')
The draws below stay inside these ranges and needn't reach their ends.
Inputs may be any that keep to these rules, and one draw needn't show every extreme that they name: `req_lengths`: each row sums to 4096; its largest entry is exactly 3072. `owner_slot`: the 4 entries of a row are distinct; slots 0 and 31 each own a request of every group. `cont_flag`: request 0 of every group continues; request 1 of group 0 does not; the others continue with probability one half. `cache_source`: request 0 reads slot 16 in groups 0, 4, 8 ..., slot 31 in groups 1, 5 ..., slot 0 in groups 2, 6 ..., slot 1 in groups 3, 7 ...; other requests read any slot.
All inputs are finite; a program needn't handle non-finite values.
Results may differ from the reference program's by a relative error of at most 0.007.
Values may be sent and summed in bfloat16 or wider, within the bound.
A program may use at most 256 MiB of HBM per device.

```python
import math
import jax
import jax.numpy as jnp
import numpy as np
from jax import lax

D = 1600
INNER = 3200
STATE = 16
CONV = 4
DT_RANK = 100
FF = 5504
TOK_DEV = 128
REQS = 4
GROUP_TOK = 4096
EDGE = 3
N_REQ = 4
N_SEQ = 32


def draw_owner_slot(key, part):
    slot_count = GROUP_TOK // TOK_DEV
    row_keys = jax.random.split(key, N_REQ)

    def one_row(row_key):
        first_key, second_key = jax.random.split(row_key)
        middle = (jax.random.permutation(first_key, slot_count - 2) + 1).astype(jnp.int32)
        chosen = jnp.concatenate([jnp.array([0, slot_count - 1], dtype=jnp.int32), middle[:REQS - 2]])
        return jax.random.permutation(second_key, chosen).astype(jnp.int32)
    return jax.vmap(one_row)(row_keys).astype(jnp.int32)


def draw_cont_flag(key, part):
    flags = jax.random.randint(jax.random.fold_in(key, 11), (N_REQ, REQS), 0, 2).astype(jnp.int32)
    flags = flags.at[:, 0].set(1)
    flags = flags.at[0, 1].set(0)
    return flags.astype(jnp.int32)


def draw_cache_source(key, part):
    slot_count = GROUP_TOK // TOK_DEV
    sources = jax.random.randint(jax.random.fold_in(key, 23), (N_REQ, REQS), 0, slot_count).astype(jnp.int32)
    group_ids = jnp.arange(N_REQ, dtype=jnp.int32) % 4
    fixed = jnp.where(group_ids == 0, slot_count // 2, jnp.where(group_ids == 1, slot_count - 1, jnp.where(group_ids == 2, 0, 1))).astype(jnp.int32)
    return sources.at[:, 0].set(fixed).astype(jnp.int32)


def shard_levels(stream_key, dims, cuts, low, largest):
    factor_of = 1.0
    for dim, blocks in cuts:
        heights = jax.random.uniform(jax.random.fold_in(jax.random.fold_in(stream_key, 6), dim), (blocks,), jnp.float32, low / len(cuts), largest / len(cuts))
        factor_of = factor_of * jnp.repeat(jnp.exp(heights), dims[dim] // blocks).reshape((-1,) + (1,) * (len(dims) - 1 - dim))
    return factor_of


def split_up(number_of, total, most, skew):
    loads = [(1 << 20) // math.isqrt(standing ** skew) + 1 for standing in range(2, number_of + 1)]
    rest, given = total - most - (number_of - 1), [1] * (number_of - 1)
    while rest > 0:
        movable = [i for i in range(number_of - 1) if given[i] < most]
        mass, left = sum([loads[i] for i in movable]), rest
        for i in movable:
            addition = min(most - given[i], max(1, left * loads[i] // mass), rest)
            given[i] = given[i] + addition
            rest = rest - addition
    return np.array([most] + given)


def uneven_parts(stream_key, amount, total, reach, slope):
    if amount == 2:
        one = jax.random.randint(stream_key, (), max(1, total - reach), min(reach, total - 1) + 1)
        return jnp.stack([one, total - one])
    sizes = jnp.asarray(split_up(amount, total, reach, slope), jnp.int32)
    twos = (amount - 1) // 2
    source_of, receiver = sizes[1:1 + 2 * twos:2], sizes[2:2 + 2 * twos:2]
    margin = jnp.minimum(source_of - 1, reach - receiver)
    moved = jax.random.randint(jax.random.fold_in(stream_key, 1), (twos,), 0, 1 << 20) % (margin + 1)
    sizes = sizes.at[1:1 + 2 * twos:2].set(source_of - moved).at[2:2 + 2 * twos:2].set(receiver + moved)
    return sizes[jax.random.permutation(jax.random.fold_in(stream_key, 2), amount)]


def gaussian(rng, extent, spread, bound, cuts=(), kind=jnp.bfloat16):
    values = jax.random.normal(rng, extent, jnp.float32) * spread
    if len(cuts) > 0:
        values = shard_levels(rng, extent, cuts, -0.22, 0.18) * values
    return jnp.clip(values, min=-bound, max=bound).astype(kind)


def setup_inputs(seed: int = 0) -> dict:
    key_list = jax.random.split(jax.random.key(seed), 21)
    return {
        "hidden_in": gaussian(key_list[0], (N_REQ, GROUP_TOK, D), 1.0, 6.0, ((0, 4), (1, 32))),
        "mamba_in": gaussian(key_list[1], (N_REQ, GROUP_TOK, INNER), 1.0, 6.0, ((0, 4), (1, 32))),
        "conv_weight": gaussian(key_list[2], (CONV, INNER), 0.5, 3.0, (), jnp.float32),
        "conv_bias": gaussian(key_list[3], (INNER,), 0.5, 3.0, (), jnp.float32),
        "x_proj": gaussian(key_list[4], (INNER, DT_RANK + 2 * STATE), INNER ** -0.5, 0.109375),
        "dt_proj": gaussian(key_list[5], (DT_RANK, INNER), DT_RANK ** -0.5, 0.625),
        "dt_bias": jnp.clip(jax.random.uniform(key_list[6], (INNER,), jnp.float32, -2.0, 0.5), -2.0, 0.5),
        "decay_rate": jnp.clip(jnp.exp(jax.random.uniform(key_list[7], (INNER,), jnp.float32, math.log(2.441406286379788e-05), math.log(0.05))), 2.441406286379788e-05, 0.05),
        "skip_gain": jnp.clip(jax.random.uniform(key_list[8], (INNER,), jnp.float32, 0.5, 1.5), 0.5, 1.5),
        "out_proj": gaussian(key_list[9], (INNER, D), INNER ** -0.5, 0.109375),
        "norm_gain": jnp.clip(jax.random.uniform(key_list[10], (D,), jnp.float32, 0.3, 1.7), 0.3, 1.7),
        "mlp_gate": gaussian(key_list[11], (D, FF), D ** -0.5, 0.15625, ((1, 4),)),
        "mlp_up": gaussian(key_list[12], (D, FF), D ** -0.5, 0.15625, ((1, 4),)),
        "mlp_down": gaussian(key_list[13], (FF, D), FF ** -0.5, 0.078125, ((0, 4),)),
        "cache_state": gaussian(key_list[14], (N_REQ, N_SEQ, STATE, INNER), 1.0, 6.0, ((0, 4), (1, 32)), jnp.float32),
        "cache_edge": gaussian(key_list[15], (N_REQ, N_SEQ, EDGE, INNER), 1.0, 6.0, ((0, 4), (1, 32))),
        "req_lengths": jax.vmap(lambda own: uneven_parts(own, REQS, TOK_DEV * N_SEQ, TOK_DEV * N_SEQ * 3 // 4, 2))(jax.random.split(key_list[16], N_REQ)).reshape((N_REQ, REQS)).astype(jnp.int32),
        "cont_flag": draw_cont_flag(jax.random.fold_in(key_list[20], 71), 0),
        "cache_source": draw_cache_source(jax.random.fold_in(key_list[20], 71), 0),
        "owner_slot": draw_owner_slot(jax.random.fold_in(key_list[20], 71), 0),
    }


HIGHEST_PREC = lax.Precision.HIGHEST
NORM_EPS = 1e-06

def request_layout(length_row, first_pos, row_count):
    length_row = length_row.astype(jnp.int32)
    end_marks = jnp.cumsum(length_row).astype(jnp.int32)
    start_marks = (end_marks - length_row).astype(jnp.int32)
    position = (first_pos + jnp.arange(row_count, dtype=jnp.int32)).astype(jnp.int32)
    request_id = lax.optimization_barrier(jnp.sum((position[:, None] >= end_marks[None, :]).astype(jnp.int32), axis=1)).astype(jnp.int32)
    member = jnp.arange(length_row.shape[0], dtype=jnp.int32)[None, :] == request_id[:, None]
    begin = lax.optimization_barrier(jnp.sum(jnp.where(member, start_marks[None, :], 0), axis=1)).astype(jnp.int32)
    finish = lax.optimization_barrier(jnp.sum(jnp.where(member, end_marks[None, :], 0), axis=1)).astype(jnp.int32)
    offset = (position - begin).astype(jnp.int32)
    is_last = position + 1 == finish
    return (member, offset, is_last)

def conv_window(extended, member, offset, edges, continuing):
    row_count = member.shape[0]
    request_count = member.shape[1]
    edge_rows = edges.shape[1]
    active = member.astype(jnp.float32) * continuing.astype(jnp.float32)[None, :]
    flat_edges = edges.reshape(request_count * edge_rows, edges.shape[2])
    window = []
    for lag_back in range(edge_rows, 0, -1):
        near_rows = extended[edge_rows - lag_back:edge_rows - lag_back + row_count].astype(jnp.float32)
        edge_slot = offset - lag_back + edge_rows
        chooser = active[:, :, None] * (jnp.arange(edge_rows, dtype=jnp.int32)[None, None, :] == edge_slot[:, None, None]).astype(jnp.float32)
        far_rows = jnp.dot(chooser.reshape(row_count, request_count * edge_rows), flat_edges, precision=HIGHEST_PREC)
        window.append(jnp.where((offset >= lag_back)[:, None], near_rows, far_rows))
    window.append(extended[edge_rows:].astype(jnp.float32))
    return window

def conv_apply(window, conv_weight, conv_bias):
    result = conv_bias[None, :] + conv_weight[0][None, :] * window[0]
    for tap_index in range(1, len(window)):
        result = result + conv_weight[tap_index][None, :] * window[tap_index]
    return jax.nn.silu(result).astype(jnp.bfloat16)

def selective_terms(mixed_in, x_proj, dt_proj, dt_bias, state_size):
    projected = jnp.dot(mixed_in, x_proj, preferred_element_type=jnp.float32)
    rank_size = dt_proj.shape[0]
    dt_low = projected[:, :rank_size].astype(jnp.bfloat16)
    b_coef = projected[:, rank_size:rank_size + state_size]
    c_coef = projected[:, rank_size + state_size:rank_size + 2 * state_size]
    step_size = jax.nn.softplus(jnp.dot(dt_low, dt_proj, preferred_element_type=jnp.float32) + dt_bias[None, :])
    return (b_coef, c_coef, step_size)

def norm_input(ssm_out, hidden_rows, out_proj, norm_gain):
    middle = hidden_rows.astype(jnp.float32) + jnp.dot(ssm_out, out_proj, preferred_element_type=jnp.float32)
    inverse_rms = lax.rsqrt(lax.optimization_barrier(jnp.mean(middle * middle, axis=1, keepdims=True)) + NORM_EPS)
    normed = (middle * inverse_rms * norm_gain[None, :]).astype(jnp.bfloat16)
    return (middle, normed)

def reference(hidden_in, mamba_in, conv_weight, conv_bias, x_proj, dt_proj, dt_bias, decay_rate, skip_gain, out_proj, norm_gain, mlp_gate, mlp_up, mlp_down, cache_state, cache_edge, req_lengths, cont_flag, cache_source, owner_slot):
    rate_matrix = (jnp.arange(STATE, dtype=jnp.int32) + 1).astype(jnp.float32)[:, None] * decay_rate[None, :]
    outputs = []
    states_out = []
    edges_out = []
    for group in range(N_REQ):
        token_rows = mamba_in[group]
        row_count = token_rows.shape[0]
        inner_size = token_rows.shape[1]
        edge_rows = cache_edge.shape[2]
        member, offset, is_last = request_layout(req_lengths[group], 0, row_count)
        continuing = cont_flag[group]
        keep_flag = continuing.astype(jnp.float32)
        start_state = keep_flag[:, None, None] * cache_state[group][cache_source[group]]
        start_edge = keep_flag[:, None, None] * cache_edge[group][cache_source[group]].astype(jnp.float32)
        extended = jnp.concatenate([jnp.zeros((edge_rows, inner_size), token_rows.dtype), token_rows], axis=0)
        window = conv_window(extended, member, offset, start_edge, continuing)
        mixed_in = conv_apply(window, conv_weight, conv_bias)
        b_coef, c_coef, step_size = selective_terms(mixed_in, x_proj, dt_proj, dt_bias, STATE)
        mixed_f = mixed_in.astype(jnp.float32)
        request_id = lax.optimization_barrier(jnp.sum(member.astype(jnp.int32) * jnp.arange(REQS, dtype=jnp.int32)[None, :], axis=1)).astype(jnp.int32)
        is_first = offset == 0

        def advance(carry, item):
            held, finals = carry
            step_t, b_t, c_t, input_t, first_t, request_t, last_t = item
            decay = jnp.exp(-step_t[None, :] * rate_matrix)
            before = jnp.where(first_t, start_state[request_t], held)
            held = decay * before + step_t[None, :] * b_t[:, None] * input_t[None, :]
            output_t = lax.optimization_barrier(jnp.sum(c_t[:, None] * held, axis=0))
            finals = finals.at[request_t].add(jnp.where(last_t, held, jnp.zeros_like(held)))
            return ((held, finals), output_t)
        carry_init = (jnp.zeros((STATE, inner_size), jnp.float32), jnp.zeros((REQS, STATE, inner_size), jnp.float32))
        (_, finals), ssm_core = lax.scan(advance, carry_init, (step_size, b_coef, c_coef, mixed_f, is_first, request_id, is_last))
        ssm_out = (ssm_core + skip_gain[None, :] * mixed_f).astype(jnp.bfloat16)
        middle, normed = norm_input(ssm_out, hidden_in[group], out_proj, norm_gain)
        gate_v = jnp.dot(normed, mlp_gate, preferred_element_type=jnp.float32)
        up_v = jnp.dot(normed, mlp_up, preferred_element_type=jnp.float32)
        hidden = (jax.nn.silu(gate_v) * up_v).astype(jnp.bfloat16)
        block_rows = (middle + jnp.dot(hidden, mlp_down, preferred_element_type=jnp.float32)).astype(jnp.bfloat16)
        outputs.append(block_rows)
        end_marks = jnp.cumsum(req_lengths[group].astype(jnp.int32)).astype(jnp.int32)
        window_tail = jnp.stack(window[1:], axis=1)
        final_edge = window_tail[end_marks - 1]
        owners = owner_slot[group]
        slot_state = jnp.zeros((N_SEQ, STATE, inner_size), jnp.float32).at[owners].set(finals)
        slot_edge = jnp.zeros((N_SEQ, edge_rows, inner_size), jnp.float32).at[owners].set(final_edge)
        states_out.append(slot_state)
        edges_out.append(slot_edge.astype(jnp.bfloat16))
    return (jnp.stack(outputs, axis=0), jnp.stack(states_out, axis=0), jnp.stack(edges_out, axis=0))
```

```python
import functools

import jax
import jax.numpy as jnp
from jax import lax
from jax.experimental import pallas as pl
from jax.experimental.pallas import tpu as pltpu
from jax.sharding import PartitionSpec as P

STATE = 16
EDGE = 3
NORM_EPS = 1e-06
LANES = 128
FAR = 1e30
HIGHEST_PREC = lax.Precision.HIGHEST
VMEM = pltpu.VMEM
SMEM = pltpu.SMEM


def vspec():
    return pl.BlockSpec(memory_space=VMEM)


def sspec():
    return pl.BlockSpec(memory_space=SMEM)


def col_block(width):
    return 640 if width % 640 == 0 else LANES


def segment(info, r, rows):
    begin = jnp.int32(0)
    for q in range(r):
        begin = begin + info[q]
    end = begin + info[r]
    first = info[16]
    low = jnp.clip(begin - first, 0, rows)
    high = jnp.clip(end - first, 0, rows)
    fresh = begin >= first
    ends = (end > first) & (end <= first + rows)
    return begin, low, high, fresh, ends


def token_stage(
    info,
    x_ref,
    halo_ref,
    edge_ref,
    start_ref,
    conv_w_ref,
    conv_b_ref,
    x_proj_ref,
    dt_proj_ref,
    dt_bias_ref,
    decay_ref,
    mixed_ref,
    step_ref,
    proj_ref,
    end_ref,
    sum_ref,
    last_edge_ref,
    ext,
    mixed_b,
    suffix,
    b_wide,
):
    rows, inner = x_ref.shape
    width = col_block(inner)
    rank = dt_proj_ref.shape[0]
    ext[pl.ds(0, 16), :] = halo_ref[...].astype(jnp.float32)
    ext[pl.ds(16, rows), :] = x_ref[...].astype(jnp.float32)
    requests = start_ref.shape[0]
    first_pos = info[16]
    position = first_pos + lax.broadcasted_iota(jnp.int32, (rows, LANES), 0)
    marks = [segment(info, r, rows) for r in range(requests)]
    begin = jnp.zeros((rows, LANES), jnp.int32)
    request = jnp.zeros((rows, LANES), jnp.int32)
    last_begin, last_req = jnp.int32(0), jnp.int32(0)
    for r in range(1, requests):
        reached = position >= marks[r][0]
        begin = jnp.where(reached, marks[r][0], begin)
        request = jnp.where(reached, r, request)
        inside = first_pos + rows - 1 >= marks[r][0]
        last_begin = jnp.where(inside, marks[r][0], last_begin)
        last_req = jnp.where(inside, r, last_req)
    offset = position - begin
    in_last = (position >= last_begin).astype(jnp.float32)
    edge_id = lax.broadcasted_iota(jnp.int32, (rows, 16), 1)
    hots = []
    for lag in (1, 2, 3):
        want = request * EDGE + EDGE + offset - lag
        hit = (edge_id == want[:, :16]) & (offset[:, :16] < lag)
        hots.append(hit.astype(jnp.float32).astype(jnp.bfloat16))

    keep = {}
    for lag in (1, 2, 3):
        keep[lag] = jnp.concatenate([offset] * (width // LANES), axis=1) >= lag
    for first in range(0, inner, width):
        cols = pl.ds(first, width)
        edges = edge_ref[:, cols]
        total = conv_b_ref[:, cols] + conv_w_ref[pl.ds(3, 1), cols] * ext[pl.ds(16, rows), cols]
        for lag in (1, 2, 3):
            near = ext[pl.ds(16 - lag, rows), cols]
            far = jnp.dot(hots[lag - 1], edges, preferred_element_type=jnp.float32)
            row = jnp.where(keep[lag], near, far)
            total = total + conv_w_ref[pl.ds(3 - lag, 1), cols] * row
        mixed = (total / (1.0 + jnp.exp(-total))).astype(jnp.bfloat16)
        mixed_b[:, cols] = mixed
        mixed_ref[:, cols] = mixed.astype(jnp.float32)

    proj = jnp.dot(mixed_b[...], x_proj_ref[...], preferred_element_type=jnp.float32)
    proj_ref[...] = proj
    for s in range(STATE):
        b_wide[s] = jnp.broadcast_to(proj[:, rank + s : rank + s + 1], (rows, LANES))
    dt_low = proj[:, :rank].astype(jnp.bfloat16)
    row_id = lax.broadcasted_iota(jnp.int32, (rows, rows), 0)
    col_id = lax.broadcasted_iota(jnp.int32, (rows, rows), 1)
    later = (col_id > row_id).astype(jnp.bfloat16)
    for first in range(0, inner, width):
        cols = pl.ds(first, width)
        v = jnp.dot(dt_low, dt_proj_ref[:, cols], preferred_element_type=jnp.float32)
        v = v + dt_bias_ref[:, cols]
        step = jnp.maximum(v, 0.0) + jnp.log1p(jnp.exp(-jnp.abs(v)))
        step_ref[:, cols] = step
        high = step.astype(jnp.bfloat16)
        rest = step - high.astype(jnp.float32)
        mid = rest.astype(jnp.bfloat16)
        low = (rest - mid.astype(jnp.float32)).astype(jnp.bfloat16)
        after = (
            jnp.dot(later, high, preferred_element_type=jnp.float32)
            + jnp.dot(later, mid, preferred_element_type=jnp.float32)
            + jnp.dot(later, low, preferred_element_type=jnp.float32)
        )
        suffix[:, cols] = after

    starts_here = (last_begin >= first_pos).astype(jnp.int32)
    flag = jnp.full((1, LANES), starts_here, jnp.int32).astype(jnp.float32)
    power = (lax.broadcasted_iota(jnp.int32, (STATE, LANES), 0) + 1).astype(jnp.float32)

    def one_tile(j, carry):
        cols = pl.ds(pl.multiple_of(j * LANES, LANES), LANES)
        rate = decay_ref[:, cols]
        acc = [jnp.zeros((8, LANES), jnp.float32) for _ in range(STATE)]
        since = jnp.zeros((8, LANES), jnp.float32)
        for tile in range(rows // 8):
            here = pl.ds(tile * 8, 8)
            fade = jnp.exp(-rate * suffix[here, cols])
            step = step_ref[here, cols] * in_last[tile * 8 : tile * 8 + 8]
            since = since + step
            push = step * mixed_ref[here, cols]
            for s in range(STATE):
                push = push * fade
                acc[s] = acc[s] + push * b_wide[s, here, :]
        ends = jnp.concatenate([jnp.sum(a, axis=0, keepdims=True) for a in acc], axis=0)
        since = jnp.sum(since, axis=0, keepdims=True)
        seed = jnp.exp(-(rate * since) * power) * start_ref[last_req, :, cols].astype(jnp.float32)
        end_ref[:, cols] = ends + flag * seed
        sum_ref[:, cols] = jnp.where(flag > 0.5, FAR, since)
        return carry

    lax.fori_loop(0, inner // LANES, one_tile, 0)
    row_of = lax.broadcasted_iota(jnp.int32, (16, LANES), 0)
    from_of = lax.broadcasted_iota(jnp.int32, (16, LANES), 1)
    near_at = jnp.full((16, LANES), -1, jnp.int32)
    far_at = jnp.full((16, LANES), -1, jnp.int32)
    for r in range(requests):
        _, _, high, _, ends = marks[r]
        size = info[r]
        for j in range(EDGE):
            lag = EDGE - 1 - j
            near = jnp.where(ends & (size > lag), high + 15 - lag, -1)
            far = jnp.where(ends & (size <= lag), r * EDGE + EDGE + size - 1 - lag, -1)
            near_at = jnp.where(row_of == r * EDGE + j, near, near_at)
            far_at = jnp.where(row_of == r * EDGE + j, far, far_at)

    def hot_rows(at, count):
        return (from_of[:, :count] == at[:, :count]).astype(jnp.float32).astype(jnp.bfloat16)

    for first in range(0, inner, width):
        cols = pl.ds(first, width)
        last_edge_ref[:, cols] = (
            jnp.dot(hot_rows(near_at - 16, rows), x_ref[:, cols], preferred_element_type=jnp.float32)
            + jnp.dot(hot_rows(near_at, 16), halo_ref[:, cols], preferred_element_type=jnp.float32)
            + jnp.dot(hot_rows(far_at, 16), edge_ref[:, cols], preferred_element_type=jnp.float32)
        )


def token_call(info, args, rows, inner, proj_width):
    f32 = jnp.float32
    return pl.pallas_call(
        token_stage,
        out_shape=(
            jax.ShapeDtypeStruct((rows, inner), f32),
            jax.ShapeDtypeStruct((rows, inner), f32),
            jax.ShapeDtypeStruct((rows, proj_width), f32),
            jax.ShapeDtypeStruct((STATE, inner), f32),
            jax.ShapeDtypeStruct((1, inner), f32),
            jax.ShapeDtypeStruct((16, inner), f32),
        ),
        in_specs=[sspec()] + [vspec()] * len(args),
        out_specs=tuple([vspec()] * 6),
        scratch_shapes=[
            VMEM((rows + 16, inner), f32),
            VMEM((rows, inner), jnp.bfloat16),
            VMEM((rows, inner), f32),
            VMEM((STATE, rows, LANES), f32),
        ],
        compiler_params=pltpu.CompilerParams(vmem_limit_bytes=40 << 20),
        cost_estimate=pl.CostEstimate(
            flops=400_000_000, bytes_accessed=8_000_000, transcendentals=2_000_000
        ),
        name="token_stage",
    )(info, *args)


def scan_stage(
    info,
    mixed_ref,
    step_ref,
    proj_ref,
    enter_ref,
    start_ref,
    decay_ref,
    skip_ref,
    hidden_ref,
    gain_ref,
    out_w_hbm,
    middle_ref,
    normed_ref,
    final_ref,
    bc_wide,
    y_ref,
    ssm_b,
    out_w,
    w_sem,
):
    rows, inner = mixed_ref.shape
    width = col_block(inner)
    tiles = width // LANES
    rank = proj_ref.shape[1] - 2 * STATE
    fetch = pltpu.make_async_copy(out_w_hbm, out_w, w_sem)
    fetch.start()

    turned = jnp.transpose(proj_ref[:, rank : rank + 2 * STATE])
    for t in range(rows):
        bc_wide[t] = jnp.broadcast_to(turned[:, t : t + 1], (2 * STATE, LANES))
    final_ref[...] = jnp.zeros_like(final_ref)
    power = (lax.broadcasted_iota(jnp.int32, (8, LANES), 0) + 1).astype(jnp.float32)

    def wide_step(t, i, step, push, fade8, state, rates):
        b_low, b_high = bc_wide[t, 0:8], bc_wide[t, 8:16]
        c_low, c_high = bc_wide[t, 16:24], bc_wide[t, 24:32]
        outs, new = [], []
        for j in range(tiles):
            s_row, p_row, f_row = (
                jnp.broadcast_to(part[j][i : i + 1], (8, LANES)) for part in (step, push, fade8)
            )
            d_low = jnp.exp(s_row * rates[j])
            d_high = d_low * f_row
            low = d_low * state[2 * j] + b_low * p_row
            high = d_high * state[2 * j + 1] + b_high * p_row
            new += [low, high]
            outs.append(jnp.sum(c_low * low + c_high * high, axis=0, keepdims=True))
        return outs, tuple(new)

    def one_block(g, carry):
        base = pl.multiple_of(g * width, LANES)
        tile_cols = [pl.ds(pl.multiple_of(base + j * LANES, LANES), LANES) for j in range(tiles)]
        rates = [-decay_ref[:, c] * power for c in tile_cols]
        decays = [decay_ref[:, c] for c in tile_cols]

        def load(row, count):
            step = [step_ref[pl.ds(row, count), c] for c in tile_cols]
            push = [s * mixed_ref[pl.ds(row, count), c] for s, c in zip(step, tile_cols)]
            fade8 = [jnp.exp(-8.0 * (s * d)) for s, d in zip(step, decays)]
            return step, push, fade8

        def eight(block, state, limits=None):
            row = pl.multiple_of(block * 8, 8)
            step, push, fade8 = load(row, 8)
            kept = [[] for _ in range(tiles)]
            for i in range(8):
                outs, new = wide_step(row + i, i, step, push, fade8, state, rates)
                if limits is not None:
                    active = (row + i >= limits[0]) & (row + i < limits[1])
                    new = tuple(jnp.where(active, a, b) for a, b in zip(new, state))
                state = new
                for j in range(tiles):
                    kept[j].append(outs[j])
            for j in range(tiles):
                y = jnp.concatenate(kept[j], axis=0)
                if limits is not None:
                    at = row + lax.broadcasted_iota(jnp.int32, (8, LANES), 0)
                    y = jnp.where(
                        (at >= limits[0]) & (at < limits[1]), y, y_ref[pl.ds(row, 8), tile_cols[j]]
                    )
                y_ref[pl.ds(row, 8), tile_cols[j]] = y
            return state

        for r in range(final_ref.shape[0]):
            _, begin, end, new, ends = segment(info, r, rows)

            @pl.when(end > begin)
            def _():
                state = []
                for c in tile_cols:
                    for half in (pl.ds(0, 8), pl.ds(8, 8)):
                        old = enter_ref[half, c]
                        seed = start_ref[r, half, c].astype(jnp.float32)
                        state.append(jnp.where(new, seed, old))
                state = tuple(state)
                part = functools.partial(eight, limits=(begin, end))
                low, low_up, high = begin // 8, (begin + 7) // 8, end // 8
                state = lax.fori_loop(low, low_up, part, state)
                state = lax.fori_loop(low_up, jnp.maximum(high, low_up), eight, state)
                tail = jnp.where((high >= low_up) & (end % 8 > 0), high + 1, high)
                state = lax.fori_loop(high, tail, part, state)

                @pl.when(ends)
                def _():
                    for j, c in enumerate(tile_cols):
                        final_ref[r, pl.ds(0, 8), c] = state[2 * j]
                        final_ref[r, pl.ds(8, 8), c] = state[2 * j + 1]

        y = y_ref[:, pl.ds(base, width)]
        y = y + skip_ref[:, pl.ds(base, width)] * mixed_ref[:, pl.ds(base, width)]
        ssm_b[:, pl.ds(base, width)] = y.astype(jnp.bfloat16)
        return carry

    lax.fori_loop(0, inner // width, one_block, 0)
    fetch.wait()
    middle = hidden_ref[...].astype(jnp.float32)
    for first in range(0, inner, width):
        middle = middle + jnp.dot(
            ssm_b[:, first : first + width],
            out_w[first : first + width],
            preferred_element_type=jnp.float32,
        )
    middle_ref[...] = middle
    scale = lax.rsqrt(jnp.mean(middle * middle, axis=1, keepdims=True) + NORM_EPS)
    normed_ref[...] = (middle * scale * gain_ref[...]).astype(jnp.bfloat16)


def scan_call(info, args, out_w, rows, inner, model, requests):
    f32 = jnp.float32
    return pl.pallas_call(
        scan_stage,
        out_shape=(
            jax.ShapeDtypeStruct((rows, model), f32),
            jax.ShapeDtypeStruct((rows, model), jnp.bfloat16),
            jax.ShapeDtypeStruct((requests, STATE, inner), f32),
        ),
        in_specs=[sspec()] + [vspec()] * len(args) + [pl.BlockSpec(memory_space=pl.ANY)],
        out_specs=tuple([vspec()] * 3),
        scratch_shapes=[
            VMEM((rows, 2 * STATE, LANES), f32),
            VMEM((rows, inner), f32),
            VMEM((rows, inner), jnp.bfloat16),
            VMEM((inner, model), jnp.bfloat16),
            pltpu.SemaphoreType.DMA,
        ],
        compiler_params=pltpu.CompilerParams(vmem_limit_bytes=48 << 20),
        cost_estimate=pl.CostEstimate(
            flops=1_400_000_000, bytes_accessed=18_000_000, transcendentals=4_000_000
        ),
        name="scan_stage",
    )(info, *args, out_w)


def passed_along(block, axis, distance):
    devices = range(lax.axis_size(axis))
    route = [(i - distance, i) for i in devices if i - distance in devices]
    return lax.ppermute(block, axis, route)


def picked(array, chooser):
    return jnp.einsum("rj,jsc->rsc", chooser, array, precision=HIGHEST_PREC)


def shards(
    hidden_in,
    mamba_in,
    conv_weight,
    conv_bias,
    x_proj,
    dt_proj,
    dt_bias,
    decay_rate,
    skip_gain,
    out_proj,
    norm_gain,
    mlp_gate,
    mlp_up,
    mlp_down,
    cache_state,
    cache_edge,
    req_lengths,
    cont_flag,
    cache_source,
    owner_slot,
):
    rows, inner = mamba_in.shape[1:]
    model = hidden_in.shape[2]
    requests = req_lengths.shape[1]
    devices = lax.axis_size("seq")
    place = lax.axis_index("seq")
    info = jnp.concatenate(
        [
            req_lengths[0],
            cont_flag[0],
            cache_source[0],
            owner_slot[0],
            jnp.reshape(place * rows, (1,)).astype(jnp.int32),
        ]
    )
    bf16 = jnp.bfloat16
    states = lax.all_gather(cache_state[0, 0].astype(bf16), "seq")
    edges = lax.all_gather(cache_edge[0, 0], "seq")
    chooser = (
        cont_flag[0][:, None]
        * (cache_source[0][:, None] == jnp.arange(devices)[None, :]).astype(jnp.int32)
    ).astype(jnp.float32)
    start_state = picked(states.astype(jnp.float32), chooser)
    start_edge = picked(edges.astype(jnp.float32), chooser).astype(bf16)
    start_edge = start_edge.reshape(requests * EDGE, inner)
    start_edge = jnp.pad(start_edge, ((0, 16 - requests * EDGE), (0, 0)))
    halo = passed_along(mamba_in[0, rows - 16 :], "seq", 1)
    mixed, step, proj, end_state, step_sum, last_edge = token_call(
        info,
        (
            mamba_in[0],
            halo,
            start_edge,
            start_state,
            conv_weight,
            conv_bias[None],
            x_proj,
            dt_proj,
            dt_bias[None],
            decay_rate[None],
        ),
        rows,
        inner,
        x_proj.shape[1],
    )
    all_end = lax.all_gather(end_state, "seq")
    all_sum = lax.all_gather(step_sum[0], "seq")
    rates = (jnp.arange(STATE) + 1).astype(jnp.float32)[:, None] * decay_rate[None, :]
    enter = jnp.zeros_like(end_state)

    def lap(k, before):
        after = jnp.exp(-rates * all_sum[k][None]) * before + all_end[k]
        return jnp.where(k < place, after, before)

    enter = lax.fori_loop(0, devices, lap, enter)
    middle, normed, finals = scan_call(
        info,
        (
            mixed,
            step,
            proj,
            enter,
            start_state,
            decay_rate[None],
            skip_gain[None],
            hidden_in[0],
            norm_gain[None],
        ),
        out_proj,
        rows,
        inner,
        model,
        requests,
    )
    sums = jnp.concatenate([finals.reshape(requests * STATE, inner), last_edge], axis=0)
    sums = lax.psum(sums.astype(bf16), "seq")
    owned = (owner_slot[0] == place).astype(bf16)
    new_state = jnp.einsum("r,rsc->sc", owned, sums[: requests * STATE].reshape(finals.shape))
    last = sums[requests * STATE :][: requests * EDGE].reshape(requests, EDGE, inner)
    new_edge = jnp.einsum("r,rsc->sc", owned, last)
    piece = lax.all_gather(normed, "req", axis=0, tiled=True)
    gate_v = jnp.dot(piece, mlp_gate, preferred_element_type=jnp.float32)
    up_v = jnp.dot(piece, mlp_up, preferred_element_type=jnp.float32)
    hidden = (jax.nn.silu(gate_v) * up_v).astype(bf16)
    mlp_out = lax.psum_scatter(
        jnp.dot(hidden, mlp_down, preferred_element_type=jnp.float32).astype(bf16),
        "req",
        scatter_dimension=0,
        tiled=True,
    ).astype(jnp.float32)
    block_rows = (middle + mlp_out).astype(bf16)
    return (
        block_rows[None],
        new_state.astype(jnp.float32)[None, None],
        new_edge.astype(bf16)[None, None],
    )


def solution(mesh):
    grouped = P("req", "seq", None)
    slots = P("req", "seq", None, None)
    return jax.shard_map(
        shards,
        mesh=mesh,
        in_specs=(grouped, grouped)
        + (P(),) * 9
        + (P(None, "req"), P(None, "req"), P("req", None), slots, slots)
        + (P("req", None),) * 4,
        out_specs=(grouped, slots, slots),
        check_vma=False,
    )
```

```python
import functools

import jax
import jax.numpy as jnp
from jax import lax
from jax.experimental import pallas as pl
from jax.experimental.pallas import tpu as pltpu
from jax.sharding import PartitionSpec as P

STATE = 16
EDGE = 3
NORM_EPS = 1e-06
LANES = 128
FAR = 1e30
HIGHEST_PREC = lax.Precision.HIGHEST
VMEM = pltpu.VMEM
SMEM = pltpu.SMEM


def vspec():
    return pl.BlockSpec(memory_space=VMEM)


def sspec():
    return pl.BlockSpec(memory_space=SMEM)


def col_block(width):
    return 640 if width % 640 == 0 else LANES


MESH_ID = pl.DeviceIdType.MESH


def layout_of(devices):
    depth = 4 if devices >= 32 else 2
    return devices // (2 * depth), depth


def half_width(inner):
    return -(-inner // (2 * LANES)) * LANES


def near_devices(devices):
    across, depth = layout_of(devices)
    me = lax.axis_index("seq")
    core, z, x = me % 2, (me // 2) % depth, me // (2 * depth)
    partner = me + 1 - 2 * core
    z_peers = [x * 2 * depth + ((z + d) % depth) * 2 + core for d in range(1, depth)]
    x_peers = [((x + d) % across) * 2 * depth + z * 2 + core for d in range(1, across)]
    return me, core, z, x, partner, z_peers, x_peers


def my_lanes(core, inner):
    half = half_width(inner)
    return pl.ds(pl.multiple_of(core * (inner - half), LANES), half)


def send(src, dst, sems, index, peer):
    return pltpu.make_async_remote_copy(
        src_ref=src,
        dst_ref=dst,
        send_sem=sems.at[0, index],
        recv_sem=sems.at[1, index],
        device_id={"seq": peer},
        device_id_type=MESH_ID,
    )


def greet(axis_peers):
    barrier = pltpu.get_barrier_semaphore()
    for axis, peer in axis_peers:
        pl.semaphore_signal(barrier, inc=1, device_id={axis: peer}, device_id_type=MESH_ID)
    pl.semaphore_wait(barrier, len(axis_peers))


class Spread:
    def __init__(self, devices, inner, count, split, refs):
        self.devices, self.inner, self.count, self.split = devices, inner, count, split
        self.across, self.depth = layout_of(devices)
        self.part = count // self.depth if split else count
        (
            self.mine,
            self.from_core,
            self.acc,
            self.from_z,
            self.from_x,
            self.from_z2,
            self.other,
            self.sems,
        ) = refs
        _, self.core, self.z, self.x, self.partner, self.z_peers, self.x_peers = near_devices(
            devices
        )
        self.lanes = my_lanes(self.core, inner)
        self.far_lanes = my_lanes(1 - self.core, inner)
        self.copies = []

    @staticmethod
    def scratch(devices, inner, count, split):
        across, depth = layout_of(devices)
        part = count // depth if split else count
        half = half_width(inner)
        b = jnp.bfloat16
        return [
            VMEM((count, 16, inner), b),
            VMEM((count, 16, half), b),
            VMEM((count, 16, half), b),
            VMEM((depth - 1, part, 16, half), b),
            VMEM((across - 1, part, 16, half), b),
            VMEM((depth - 1, part, 16, half), b),
            VMEM((count, 16, half), b),
            pltpu.SemaphoreType.DMA((2, 2 + 2 * (depth - 1) + (across - 1))),
        ]

    def own_part(self, shift=0):
        if not self.split:
            return pl.ds(0, self.part)
        return pl.ds(((self.z + shift) % self.depth) * self.part, self.part)

    def begin(self, copies):
        self.copies = copies
        for copy in copies:
            copy.start()

    def end(self):
        for copy in self.copies:
            copy.wait()

    def start_core(self):
        self.begin(
            [send(self.mine.at[:, :, self.far_lanes], self.from_core, self.sems, 0, self.partner)]
        )

    def finish_core(self):
        self.end()
        total = self.mine[:, :, self.lanes].astype(jnp.float32) + self.from_core[...].astype(
            jnp.float32
        )
        self.acc[...] = total.astype(jnp.bfloat16)

    def start_z(self):
        self.begin(
            [
                send(self.acc.at[self.own_part(d + 1)], self.from_z.at[d], self.sems, 1 + d, peer)
                for d, peer in enumerate(self.z_peers)
            ]
        )

    def finish_z(self):
        self.end()
        here = self.own_part()
        total = self.acc[here].astype(jnp.float32)
        for d in range(self.depth - 1):
            total = total + self.from_z[d].astype(jnp.float32)
        self.acc[here] = total.astype(jnp.bfloat16)

    def start_x(self):
        base = self.depth
        self.begin(
            [
                send(self.acc.at[self.own_part()], self.from_x.at[d], self.sems, base + d, peer)
                for d, peer in enumerate(self.x_peers)
            ]
        )

    def finish_x(self):
        self.end()
        here = self.own_part()
        total = self.acc[here].astype(jnp.float32)
        for d in range(self.across - 1):
            total = total + self.from_x[d].astype(jnp.float32)
        self.acc[here] = total.astype(jnp.bfloat16)

    def start_z2(self):
        if not self.split:
            return
        base = self.depth + self.across - 1
        self.begin(
            [
                send(self.acc.at[self.own_part()], self.from_z2.at[d], self.sems, base + d, peer)
                for d, peer in enumerate(self.z_peers)
            ]
        )

    def finish_z2(self):
        if not self.split:
            return
        self.end()
        for d in range(self.depth - 1):
            self.acc[self.own_part(-(d + 1))] = self.from_z2[d]

    def start_core2(self):
        last = 2 * (self.depth - 1) + self.across
        self.begin([send(self.acc, self.other, self.sems, last, self.partner)])

    def finish_core2(self, out_ref):
        self.end()
        out_ref[:, :, self.lanes] = self.acc[...]
        out_ref[:, :, self.far_lanes] = self.other[...]


def segment(info, r, rows):
    begin = jnp.int32(0)
    for q in range(r):
        begin = begin + info[q]
    end = begin + info[r]
    first = info[16]
    low = jnp.clip(begin - first, 0, rows)
    high = jnp.clip(end - first, 0, rows)
    fresh = begin >= first
    ends = (end > first) & (end <= first + rows)
    return begin, low, high, fresh, ends


def front_stage(
    devices,
    info,
    x_ref,
    cache_ref,
    cache_edge_ref,
    conv_w_ref,
    conv_b_ref,
    x_proj_ref,
    dt_proj_ref,
    dt_bias_ref,
    decay_ref,
    mixed_ref,
    step_ref,
    proj_ref,
    enter_ref,
    last_edge_ref,
    start_ref,
    ext,
    mixed_b,
    suffix,
    b_wide,
    halo_ref,
    edge3_ref,
    end_ref,
    sum_ref,
    halo_sems,
    pair_h,
    pair_s,
    own_h,
    own_s,
    z_h,
    z_s,
    x_h,
    x_s,
    half_out,
    half_in,
    pre_sems,
    *spread_refs,
):
    rows, inner = x_ref.shape
    requests = start_ref.shape[0]
    me, core, z, x, partner, z_peers, x_peers = near_devices(devices)
    after, before = (me + 1) % devices, (me + devices - 1) % devices
    greet([("seq", p) for p in [partner, after, before] + z_peers + x_peers])
    halo_copy = send(x_ref.at[pl.ds(rows - 16, 16)], halo_ref, halo_sems, 0, after)
    halo_copy.start()
    per = len(Spread.scratch(devices, inner, 1, False))
    edge_sum = Spread(devices, inner, 1, False, spread_refs[:per])
    state_sum = Spread(devices, inner, requests, True, spread_refs[per:])
    spot = lax.broadcasted_iota(jnp.int32, (16, inner), 0)
    edge_rows = cache_edge_ref[...].astype(jnp.float32)
    placed = jnp.zeros((16, inner), jnp.float32)
    for r in range(requests):
        take = (info[8 + r] == me) & (info[4 + r] > 0)
        for j in range(EDGE):
            placed = jnp.where((spot == r * EDGE + j) & take, edge_rows[j : j + 1], placed)
    edge_sum.mine[0] = placed.astype(jnp.bfloat16)
    edge_sum.start_core()
    for r in range(requests):
        take = (info[8 + r] == me) & (info[4 + r] > 0)
        state_sum.mine[r] = jnp.where(take, cache_ref[...], 0.0).astype(jnp.bfloat16)
    state_sum.start_core()
    ext[pl.ds(16, rows), :] = x_ref[...].astype(jnp.float32)
    edge_sum.finish_core()
    edge_sum.start_z()
    state_sum.finish_core()
    state_sum.start_z()
    edge_sum.finish_z()
    edge_sum.start_x()
    state_sum.finish_z()
    state_sum.start_x()
    edge_sum.finish_x()
    edge_sum.start_core2()
    edge_sum.finish_core2(edge3_ref)
    edge_ref = edge3_ref.at[0]
    halo_copy.wait()
    width = col_block(inner)
    rank = dt_proj_ref.shape[0]
    ext[pl.ds(0, 16), :] = halo_ref[...].astype(jnp.float32)
    first_pos = info[16]
    position = first_pos + lax.broadcasted_iota(jnp.int32, (rows, LANES), 0)
    marks = [segment(info, r, rows) for r in range(requests)]
    begin = jnp.zeros((rows, LANES), jnp.int32)
    request = jnp.zeros((rows, LANES), jnp.int32)
    last_begin, last_req = jnp.int32(0), jnp.int32(0)
    for r in range(1, requests):
        reached = position >= marks[r][0]
        begin = jnp.where(reached, marks[r][0], begin)
        request = jnp.where(reached, r, request)
        inside = first_pos + rows - 1 >= marks[r][0]
        last_begin = jnp.where(inside, marks[r][0], last_begin)
        last_req = jnp.where(inside, r, last_req)
    offset = position - begin
    in_last = (position >= last_begin).astype(jnp.float32)
    edge_id = lax.broadcasted_iota(jnp.int32, (rows, 16), 1)
    hots = []
    for lag in (1, 2, 3):
        want = request * EDGE + EDGE + offset - lag
        hit = (edge_id == want[:, :16]) & (offset[:, :16] < lag)
        hots.append(hit.astype(jnp.float32).astype(jnp.bfloat16))

    keep = {}
    for lag in (1, 2, 3):
        keep[lag] = jnp.concatenate([offset] * (width // LANES), axis=1) >= lag
    for first in range(0, inner, width):
        cols = pl.ds(first, width)
        edges = edge_ref[:, cols]
        total = conv_b_ref[:, cols] + conv_w_ref[pl.ds(3, 1), cols] * ext[pl.ds(16, rows), cols]
        for lag in (1, 2, 3):
            near = ext[pl.ds(16 - lag, rows), cols]
            far = jnp.dot(hots[lag - 1], edges, preferred_element_type=jnp.float32)
            row = jnp.where(keep[lag], near, far)
            total = total + conv_w_ref[pl.ds(3 - lag, 1), cols] * row
        mixed = (total / (1.0 + jnp.exp(-total))).astype(jnp.bfloat16)
        mixed_b[:, cols] = mixed
        mixed_ref[:, cols] = mixed.astype(jnp.float32)

    proj = lax.dot_general(
        mixed_b[...],
        x_proj_ref[...],
        (((1,), (1,)), ((), ())),
        preferred_element_type=jnp.float32,
    )
    state_sum.finish_x()
    state_sum.start_z2()
    proj_ref[...] = proj
    for s in range(STATE):
        b_wide[s] = jnp.broadcast_to(proj[:, rank + s : rank + s + 1], (rows, LANES))
    dt_low = proj[:, :rank].astype(jnp.bfloat16)
    row_id = lax.broadcasted_iota(jnp.int32, (rows, rows), 0)
    col_id = lax.broadcasted_iota(jnp.int32, (rows, rows), 1)
    later = (col_id > row_id).astype(jnp.bfloat16)
    for first in range(0, inner, width):
        cols = pl.ds(first, width)
        v = jnp.dot(dt_low, dt_proj_ref[:, cols], preferred_element_type=jnp.float32)
        v = v + dt_bias_ref[:, cols]
        step = jnp.maximum(v, 0.0) + jnp.log1p(jnp.exp(-jnp.abs(v)))
        step_ref[:, cols] = step
        high = step.astype(jnp.bfloat16)
        rest = step - high.astype(jnp.float32)
        mid = rest.astype(jnp.bfloat16)
        low = (rest - mid.astype(jnp.float32)).astype(jnp.bfloat16)
        after = (
            jnp.dot(later, high, preferred_element_type=jnp.float32)
            + jnp.dot(later, mid, preferred_element_type=jnp.float32)
            + jnp.dot(later, low, preferred_element_type=jnp.float32)
        )
        suffix[:, cols] = after

    state_sum.finish_z2()
    state_sum.start_core2()
    state_sum.finish_core2(start_ref)
    starts_here = (last_begin >= first_pos).astype(jnp.int32)
    flag = jnp.full((1, LANES), starts_here, jnp.int32).astype(jnp.float32)
    power = (lax.broadcasted_iota(jnp.int32, (STATE, LANES), 0) + 1).astype(jnp.float32)

    def one_tile(j, carry):
        cols = pl.ds(pl.multiple_of(j * LANES, LANES), LANES)
        rate = decay_ref[:, cols]
        acc = [jnp.zeros((8, LANES), jnp.float32) for _ in range(STATE)]
        since = jnp.zeros((8, LANES), jnp.float32)
        for tile in range(rows // 8):
            here = pl.ds(tile * 8, 8)
            fade = jnp.exp(-rate * suffix[here, cols])
            step = step_ref[here, cols] * in_last[tile * 8 : tile * 8 + 8]
            since = since + step
            push = step * mixed_ref[here, cols]
            for s in range(STATE):
                push = push * fade
                acc[s] = acc[s] + push * b_wide[s, here, :]
        ends = jnp.concatenate([jnp.sum(a, axis=0, keepdims=True) for a in acc], axis=0)
        since = jnp.sum(since, axis=0, keepdims=True)
        seed = jnp.exp(-(rate * since) * power) * start_ref[last_req, :, cols].astype(jnp.float32)
        end_ref[:, cols] = ends + flag * seed
        sum_ref[:, cols] = jnp.where(flag > 0.5, FAR, since)
        return carry

    lax.fori_loop(0, inner // LANES, one_tile, 0)
    power16 = (lax.broadcasted_iota(jnp.int32, (STATE, LANES), 0) + 1).astype(jnp.float32)
    half = half_width(inner)
    tiles = half // LANES
    base = core * (inner - half)
    own_h[...] = end_ref[...].astype(jnp.bfloat16)
    for j in range(inner // LANES):
        own_s[pl.ds(j, 1), :] = sum_ref[:, pl.ds(j * LANES, LANES)]
    pair = [
        send(own_h, pair_h, pre_sems, 0, partner),
        send(own_s, pair_s, pre_sems, 1, partner),
    ]
    for copy in pair:
        copy.start()
    across, depth = layout_of(devices)
    first_core = core == 0

    def lane(j):
        return pl.ds(pl.multiple_of(base + j * LANES, LANES), LANES)

    def f32(value):
        return value.astype(jnp.float32)

    for copy in pair:
        copy.wait()
    z_sum = []
    for j in range(tiles):
        rate = decay_ref[:, lane(j)] * power16
        mine, theirs = own_h[:, lane(j)], pair_h[:, lane(j)]
        shift = (inner - half) // LANES
        s_mine = jnp.where(first_core, own_s[j : j + 1], own_s[j + shift : j + shift + 1])
        s_pair = jnp.where(first_core, pair_s[j : j + 1], pair_s[j + shift : j + shift + 1])
        h0 = f32(jnp.where(first_core, f32(mine), f32(theirs)))
        h1 = f32(jnp.where(first_core, f32(theirs), f32(mine)))
        s1 = jnp.where(first_core, s_pair, s_mine)
        z_h[0, :, pl.ds(j * LANES, LANES)] = (jnp.exp(-rate * s1) * h0 + h1).astype(jnp.bfloat16)
        z_s[0, pl.ds(j, 1), :] = s_mine + s_pair
    copies = []
    for d, peer in enumerate(z_peers):
        copies.append(send(z_h.at[0], z_h.at[d + 1], pre_sems, 2 + 2 * d, peer))
        copies.append(send(z_s.at[0], z_s.at[d + 1], pre_sems, 3 + 2 * d, peer))
    for copy in copies:
        copy.start()
    for copy in copies:
        copy.wait()
    prefix = []
    for j in range(tiles):
        cols = pl.ds(j * LANES, LANES)
        rate = decay_ref[:, lane(j)] * power16
        total = jnp.zeros((STATE, LANES), jnp.float32)
        part = jnp.zeros((STATE, LANES), jnp.float32)
        total_s = jnp.zeros((1, LANES), jnp.float32)
        part_s = jnp.zeros((1, LANES), jnp.float32)
        for k in range(depth):
            slot = (z - k + depth) % depth
            s_k = z_s[slot, pl.ds(j, 1), :]
            h_k = f32(z_h[slot, :, cols])
            fade = jnp.exp(-rate * s_k)
            total = fade * total + h_k
            part = jnp.where(k < z, fade * part + h_k, part)
            total_s = total_s + s_k
            part_s = jnp.where(k < z, part_s + s_k, part_s)
        x_h[0, :, cols] = total.astype(jnp.bfloat16)
        x_s[0, pl.ds(j, 1), :] = total_s
        prefix.append((part, part_s))
    copies = []
    first = 2 + 2 * (depth - 1)
    for d, peer in enumerate(x_peers):
        copies.append(send(x_h.at[0], x_h.at[d + 1], pre_sems, first + 2 * d, peer))
        copies.append(send(x_s.at[0], x_s.at[d + 1], pre_sems, first + 1 + 2 * d, peer))
    for copy in copies:
        copy.start()
    for copy in copies:
        copy.wait()
    for j in range(tiles):
        cols = pl.ds(j * LANES, LANES)
        rate = decay_ref[:, lane(j)] * power16
        part = jnp.zeros((STATE, LANES), jnp.float32)
        for k in range(across):
            slot = (x - k + across) % across
            value = jnp.exp(-rate * x_s[slot, pl.ds(j, 1), :]) * part + f32(x_h[slot, :, cols])
            part = jnp.where(k < x, value, part)
        inner_part, inner_s = prefix[j]
        half_out[:, cols] = jnp.exp(-rate * inner_s) * part + inner_part
    last = first + 2 * (across - 1)
    swap = send(half_out, half_in, pre_sems, last, partner)
    swap.start()
    swap.wait()
    enter_ref[:, my_lanes(core, inner)] = half_out[...]
    enter_ref[:, my_lanes(1 - core, inner)] = half_in[...]
    for j in range(inner // LANES):
        cols = pl.ds(j * LANES, LANES)
        rate = decay_ref[:, cols] * power16
        chip = enter_ref[:, cols]
        second = jnp.exp(-rate * pair_s[j : j + 1]) * chip + f32(pair_h[:, cols])
        enter_ref[:, cols] = jnp.where(first_core, chip, second)

    row_of = lax.broadcasted_iota(jnp.int32, (16, LANES), 0)
    from_of = lax.broadcasted_iota(jnp.int32, (16, LANES), 1)
    near_at = jnp.full((16, LANES), -1, jnp.int32)
    far_at = jnp.full((16, LANES), -1, jnp.int32)
    for r in range(requests):
        _, _, high, _, ends = marks[r]
        size = info[r]
        for j in range(EDGE):
            lag = EDGE - 1 - j
            near = jnp.where(ends & (size > lag), high + 15 - lag, -1)
            far = jnp.where(ends & (size <= lag), r * EDGE + EDGE + size - 1 - lag, -1)
            near_at = jnp.where(row_of == r * EDGE + j, near, near_at)
            far_at = jnp.where(row_of == r * EDGE + j, far, far_at)

    def hot_rows(at, count):
        return (from_of[:, :count] == at[:, :count]).astype(jnp.float32).astype(jnp.bfloat16)

    for first in range(0, inner, width):
        cols = pl.ds(first, width)
        last_edge_ref[:, cols] = (
            jnp.dot(hot_rows(near_at - 16, rows), x_ref[:, cols], preferred_element_type=jnp.float32)
            + jnp.dot(hot_rows(near_at, 16), halo_ref[:, cols], preferred_element_type=jnp.float32)
            + jnp.dot(hot_rows(far_at, 16), edge_ref[:, cols], preferred_element_type=jnp.float32)
        )


def front_call(devices, info, args, rows, inner, proj_width, requests):
    f32, bf16 = jnp.float32, jnp.bfloat16
    across, depth = layout_of(devices)
    half = half_width(inner)
    s_rows = -(-(inner // LANES) // 8) * 8
    return pl.pallas_call(
        functools.partial(front_stage, devices),
        out_shape=(
            jax.ShapeDtypeStruct((rows, inner), f32),
            jax.ShapeDtypeStruct((rows, inner), f32),
            jax.ShapeDtypeStruct((rows, proj_width), f32),
            jax.ShapeDtypeStruct((STATE, inner), f32),
            jax.ShapeDtypeStruct((16, inner), f32),
            jax.ShapeDtypeStruct((requests, STATE, inner), bf16),
        ),
        in_specs=[sspec()] + [vspec()] * len(args),
        out_specs=tuple([vspec()] * 6),
        scratch_shapes=[
            VMEM((rows + 16, inner), f32),
            VMEM((rows, inner), bf16),
            VMEM((rows, inner), f32),
            VMEM((STATE, rows, LANES), f32),
            VMEM((16, inner), bf16),
            VMEM((1, 16, inner), bf16),
            VMEM((STATE, inner), f32),
            VMEM((1, inner), f32),
            pltpu.SemaphoreType.DMA((2, 1)),
            VMEM((STATE, inner), bf16),
            VMEM((s_rows, LANES), f32),
            VMEM((STATE, inner), bf16),
            VMEM((s_rows, LANES), f32),
            VMEM((depth, STATE, half), bf16),
            VMEM((depth, 16, LANES), f32),
            VMEM((across, STATE, half), bf16),
            VMEM((across, 16, LANES), f32),
            VMEM((STATE, half), f32),
            VMEM((STATE, half), f32),
            pltpu.SemaphoreType.DMA((2, 3 + 2 * (depth + across - 2))),
        ]
        + Spread.scratch(devices, inner, 1, False)
        + Spread.scratch(devices, inner, requests, True),
        compiler_params=pltpu.CompilerParams(
            vmem_limit_bytes=48 << 20, collective_id=0, has_side_effects=True
        ),
        cost_estimate=pl.CostEstimate(
            flops=400_000_000, bytes_accessed=8_000_000, transcendentals=2_000_000
        ),
        name="front_stage",
    )(info, *args)


def scan_stage(
    info,
    mixed_ref,
    step_ref,
    proj_ref,
    enter_ref,
    start_ref,
    decay_ref,
    skip_ref,
    hidden_ref,
    gain_ref,
    out_w_hbm,
    middle_ref,
    normed_ref,
    final_ref,
    bc_wide,
    y_ref,
    ssm_b,
    out_w,
    w_sem,
):
    rows, inner = mixed_ref.shape
    width = col_block(inner)
    tiles = width // LANES
    rank = proj_ref.shape[1] - 2 * STATE
    fetch = pltpu.make_async_copy(out_w_hbm, out_w, w_sem)
    fetch.start()

    turned = jnp.transpose(proj_ref[:, rank : rank + 2 * STATE])
    for t in range(rows):
        bc_wide[t] = jnp.broadcast_to(turned[:, t : t + 1], (2 * STATE, LANES))
    final_ref[...] = jnp.zeros_like(final_ref)
    power = (lax.broadcasted_iota(jnp.int32, (8, LANES), 0) + 1).astype(jnp.float32)

    def wide_step(t, i, step, push, fade8, state, rates):
        b_low, b_high = bc_wide[t, 0:8], bc_wide[t, 8:16]
        c_low, c_high = bc_wide[t, 16:24], bc_wide[t, 24:32]
        outs, new = [], []
        for j in range(tiles):
            s_row, p_row, f_row = (
                jnp.broadcast_to(part[j][i : i + 1], (8, LANES)) for part in (step, push, fade8)
            )
            d_low = jnp.exp(s_row * rates[j])
            d_high = d_low * f_row
            low = d_low * state[2 * j] + b_low * p_row
            high = d_high * state[2 * j + 1] + b_high * p_row
            new += [low, high]
            outs.append(jnp.sum(c_low * low + c_high * high, axis=0, keepdims=True))
        return outs, tuple(new)

    def one_block(g, carry):
        base = pl.multiple_of(g * width, LANES)
        tile_cols = [pl.ds(pl.multiple_of(base + j * LANES, LANES), LANES) for j in range(tiles)]
        rates = [-decay_ref[:, c] * power for c in tile_cols]
        decays = [decay_ref[:, c] for c in tile_cols]

        def load(row, count):
            step = [step_ref[pl.ds(row, count), c] for c in tile_cols]
            push = [s * mixed_ref[pl.ds(row, count), c] for s, c in zip(step, tile_cols)]
            fade8 = [jnp.exp(-8.0 * (s * d)) for s, d in zip(step, decays)]
            return step, push, fade8

        def eight(block, state, limits=None):
            row = pl.multiple_of(block * 8, 8)
            step, push, fade8 = load(row, 8)
            kept = [[] for _ in range(tiles)]
            for i in range(8):
                outs, new = wide_step(row + i, i, step, push, fade8, state, rates)
                if limits is not None:
                    active = (row + i >= limits[0]) & (row + i < limits[1])
                    new = tuple(jnp.where(active, a, b) for a, b in zip(new, state))
                state = new
                for j in range(tiles):
                    kept[j].append(outs[j])
            for j in range(tiles):
                y = jnp.concatenate(kept[j], axis=0)
                if limits is not None:
                    at = row + lax.broadcasted_iota(jnp.int32, (8, LANES), 0)
                    y = jnp.where(
                        (at >= limits[0]) & (at < limits[1]), y, y_ref[pl.ds(row, 8), tile_cols[j]]
                    )
                y_ref[pl.ds(row, 8), tile_cols[j]] = y
            return state

        for r in range(final_ref.shape[0]):
            _, begin, end, new, ends = segment(info, r, rows)

            @pl.when(end > begin)
            def _():
                state = []
                for c in tile_cols:
                    for half in (pl.ds(0, 8), pl.ds(8, 8)):
                        old = enter_ref[half, c]
                        seed = start_ref[r, half, c].astype(jnp.float32)
                        state.append(jnp.where(new, seed, old))
                state = tuple(state)
                part = functools.partial(eight, limits=(begin, end))
                low, low_up, high = begin // 8, (begin + 7) // 8, end // 8
                state = lax.fori_loop(low, low_up, part, state)
                state = lax.fori_loop(low_up, jnp.maximum(high, low_up), eight, state)
                tail = jnp.where((high >= low_up) & (end % 8 > 0), high + 1, high)
                state = lax.fori_loop(high, tail, part, state)

                @pl.when(ends)
                def _():
                    for j, c in enumerate(tile_cols):
                        final_ref[r, pl.ds(0, 8), c] = state[2 * j]
                        final_ref[r, pl.ds(8, 8), c] = state[2 * j + 1]

        y = y_ref[:, pl.ds(base, width)]
        y = y + skip_ref[:, pl.ds(base, width)] * mixed_ref[:, pl.ds(base, width)]
        ssm_b[:, pl.ds(base, width)] = y.astype(jnp.bfloat16)
        return carry

    lax.fori_loop(0, inner // width, one_block, 0)
    fetch.wait()
    middle = jnp.transpose(hidden_ref[...].astype(jnp.float32))
    for first in range(0, inner, width):
        middle = middle + lax.dot_general(
            ssm_b[:, first : first + width],
            out_w[:, first : first + width],
            (((1,), (1,)), ((), ())),
            preferred_element_type=jnp.float32,
        )
    middle_ref[...] = middle
    scale = lax.rsqrt(jnp.mean(middle * middle, axis=1, keepdims=True) + NORM_EPS)
    normed_ref[...] = (middle * scale * gain_ref[...]).astype(jnp.bfloat16)


def scan_call(info, args, out_w, rows, inner, model, requests):
    f32 = jnp.float32
    return pl.pallas_call(
        scan_stage,
        out_shape=(
            jax.ShapeDtypeStruct((rows, model), f32),
            jax.ShapeDtypeStruct((rows, model), jnp.bfloat16),
            jax.ShapeDtypeStruct((requests, STATE, inner), f32),
        ),
        in_specs=[sspec()] + [vspec()] * len(args) + [pl.BlockSpec(memory_space=pl.ANY)],
        out_specs=tuple([vspec()] * 3),
        scratch_shapes=[
            VMEM((rows, 2 * STATE, LANES), f32),
            VMEM((rows, inner), f32),
            VMEM((rows, inner), jnp.bfloat16),
            VMEM((model, inner), jnp.bfloat16),
            pltpu.SemaphoreType.DMA,
        ],
        compiler_params=pltpu.CompilerParams(vmem_limit_bytes=48 << 20),
        cost_estimate=pl.CostEstimate(
            flops=1_400_000_000, bytes_accessed=18_000_000, transcendentals=4_000_000
        ),
        name="scan_stage",
    )(info, *args, out_w)


def mlp_stage(
    devices,
    info,
    normed_ref,
    middle_ref,
    final_ref,
    last_edge_ref,
    gate_hbm,
    up_hbm,
    down_hbm,
    out_ref,
    new_state_ref,
    new_edge_ref,
    gate_w,
    up_w,
    down_w,
    w_sems,
    near,
    far,
    near_out,
    far_out,
    own_out,
    low_in,
    high_in,
    far_in,
    ring_sems,
    full,
    *spread_refs,
):
    rows, model = normed_ref.shape
    half = rows // 2
    inner = final_ref.shape[2]
    requests = final_ref.shape[0]
    me, _, _, _, partner, z_peers, x_peers = near_devices(devices)
    ring = lax.axis_size("req")
    here = lax.axis_index("req")
    above, below = (here + 1) % ring, (here + ring - 1) % ring
    fetches = [
        pltpu.make_async_copy(gate_hbm, gate_w, w_sems.at[0]),
        pltpu.make_async_copy(up_hbm, up_w, w_sems.at[1]),
        pltpu.make_async_copy(down_hbm, down_w, w_sems.at[2]),
    ]
    for copy in fetches:
        copy.start()
    greet(
        [("req", above), ("req", below)] + [("seq", p) for p in [partner] + z_peers + x_peers]
    )

    def hop(src, dst, index, peer):
        return pltpu.make_async_remote_copy(
            src_ref=src,
            dst_ref=dst,
            send_sem=ring_sems.at[0, index],
            recv_sem=ring_sems.at[1, index],
            device_id={"req": peer},
            device_id_type=MESH_ID,
        )

    first, second = pl.ds(0, half), pl.ds(half, half)
    third, fourth = pl.ds(2 * half, half), pl.ds(3 * half, half)
    up_a = hop(normed_ref.at[first], near.at[first], 0, above)
    down_b = hop(normed_ref.at[second], near.at[fourth], 1, below)
    up_a.start()
    down_b.start()
    finals = Spread(devices, inner, requests + requests, True, spread_refs)
    for r in range(requests):
        finals.mine[2 * r] = final_ref[r].astype(jnp.bfloat16)
        edges = last_edge_ref[pl.ds(r * EDGE, EDGE), :]
        rest = jnp.zeros((16 - EDGE, inner), jnp.float32)
        finals.mine[2 * r + 1] = jnp.concatenate([edges, rest], axis=0).astype(jnp.bfloat16)
    finals.start_core()

    def hidden_units(value):
        gate = jnp.dot(value, gate_w[...], preferred_element_type=jnp.float32)
        up = jnp.dot(value, up_w[...], preferred_element_type=jnp.float32)
        hidden = (gate / (1.0 + jnp.exp(-gate)) * up).astype(jnp.bfloat16)
        return lax.dot_general(
            hidden, down_w[...], (((1,), (1,)), ((), ())), preferred_element_type=jnp.float32
        )

    for copy in fetches:
        copy.wait()
    up_a.wait_recv()
    up_a2 = hop(near.at[first], far.at[first], 2, above)
    up_a2.start()
    down_b.wait_recv()
    down_b2 = hop(near.at[fourth], far.at[second], 3, below)
    down_b2.start()
    up_b = hop(normed_ref.at[second], near.at[second], 4, above)
    down_a = hop(normed_ref.at[first], near.at[third], 5, below)
    up_b.start()
    down_a.start()
    own_out[...] = hidden_units(normed_ref[...])
    finals.finish_core()
    finals.start_z()
    up_a2.wait_recv()
    down_b2.wait_recv()
    far_out[...] = hidden_units(far[...]).astype(jnp.bfloat16)
    far_up = hop(far_out.at[first], far_in.at[first], 6, above)
    far_down = hop(far_out.at[second], far_in.at[second], 7, below)
    far_up.start()
    far_down.start()
    finals.finish_z()
    finals.start_x()
    up_b.wait_recv()
    down_a.wait_recv()
    near_out[...] = hidden_units(near[...]).astype(jnp.bfloat16)
    back_down = hop(near_out.at[first], high_in.at[first], 8, below)
    back_up = hop(near_out.at[fourth], low_in.at[second], 9, above)
    back_down.start()
    back_up.start()
    finals.finish_x()
    finals.start_z2()

    def joined(rows_at, extra):
        return (
            near_out[rows_at].astype(jnp.float32) + far_in[extra].astype(jnp.float32)
        ).astype(jnp.bfloat16)

    far_up.wait_recv()
    near_out[third] = joined(third, first)
    last_up = hop(near_out.at[third], low_in.at[first], 10, above)
    last_up.start()
    far_down.wait_recv()
    near_out[second] = joined(second, second)
    last_down = hop(near_out.at[second], high_in.at[second], 11, below)
    last_down.start()
    finals.finish_z2()
    finals.start_core2()
    finals.finish_core2(full)
    state = jnp.zeros((STATE, inner), jnp.float32)
    edge = jnp.zeros((16, inner), jnp.float32)
    for r in range(requests):
        owned = info[12 + r] == me
        state = jnp.where(owned, full[2 * r].astype(jnp.float32), state)
        edge = jnp.where(owned, full[2 * r + 1].astype(jnp.float32), edge)
    new_state_ref[...] = state
    new_edge_ref[...] = edge[:EDGE].astype(jnp.bfloat16)
    own_out[...] = own_out[...] + middle_ref[...]
    back_down.wait_recv()
    back_up.wait_recv()
    last_up.wait_recv()
    last_down.wait_recv()
    total = own_out[...] + low_in[...].astype(jnp.float32) + high_in[...].astype(jnp.float32)
    out_ref[...] = jnp.transpose(total).astype(jnp.bfloat16)
    for copy in (
        up_a, down_b, up_a2, down_b2, up_b, down_a,
        far_up, far_down, back_down, back_up, last_up, last_down,
    ):
        copy.wait_send()


def mlp_call(devices, info, args, weights, rows, model, inner, requests):
    f32, bf16 = jnp.float32, jnp.bfloat16
    hidden = weights[0].shape[1]
    return pl.pallas_call(
        functools.partial(mlp_stage, devices),
        out_shape=(
            jax.ShapeDtypeStruct((model, rows), bf16),
            jax.ShapeDtypeStruct((STATE, inner), f32),
            jax.ShapeDtypeStruct((EDGE, inner), bf16),
        ),
        in_specs=[sspec()]
        + [vspec()] * len(args)
        + [pl.BlockSpec(memory_space=pl.ANY)] * len(weights),
        out_specs=tuple([vspec()] * 3),
        scratch_shapes=[
            VMEM((model, hidden), bf16),
            VMEM((model, hidden), bf16),
            VMEM((model, hidden), bf16),
            pltpu.SemaphoreType.DMA((3,)),
            VMEM((2 * rows, model), bf16),
            VMEM((rows, model), bf16),
            VMEM((2 * rows, model), bf16),
            VMEM((rows, model), bf16),
            VMEM((rows, model), f32),
            VMEM((rows, model), bf16),
            VMEM((rows, model), bf16),
            VMEM((rows, model), bf16),
            pltpu.SemaphoreType.DMA((2, 12)),
            VMEM((2 * requests, 16, inner), bf16),
        ]
        + Spread.scratch(devices, inner, 2 * requests, True),
        compiler_params=pltpu.CompilerParams(
            vmem_limit_bytes=56 << 20, collective_id=1, has_side_effects=True
        ),
        cost_estimate=pl.CostEstimate(
            flops=7_000_000_000, bytes_accessed=16_000_000, transcendentals=1_000_000
        ),
        name="mlp_stage",
    )(info, *args, *weights)


def shards(
    hidden_in,
    mamba_in,
    conv_weight,
    conv_bias,
    x_proj,
    dt_proj,
    dt_bias,
    decay_rate,
    skip_gain,
    out_proj,
    norm_gain,
    mlp_gate,
    mlp_up,
    mlp_down,
    cache_state,
    cache_edge,
    req_lengths,
    cont_flag,
    cache_source,
    owner_slot,
):
    rows, inner = mamba_in.shape[1:]
    model = hidden_in.shape[2]
    requests = req_lengths.shape[1]
    devices = lax.axis_size("seq")
    place = lax.axis_index("seq")
    info = jnp.concatenate(
        [
            req_lengths[0],
            cont_flag[0],
            cache_source[0],
            owner_slot[0],
            jnp.reshape(place * rows, (1,)).astype(jnp.int32),
        ]
    )
    mixed, step, proj, enter, last_edge, start_state = front_call(
        devices,
        info,
        (
            mamba_in[0],
            cache_state[0, 0],
            cache_edge[0, 0],
            conv_weight,
            conv_bias[None],
            x_proj.T,
            dt_proj,
            dt_bias[None],
            decay_rate[None],
        ),
        rows,
        inner,
        x_proj.shape[1],
        requests,
    )
    middle, normed, finals = scan_call(
        info,
        (
            mixed,
            step,
            proj,
            enter,
            start_state,
            decay_rate[None],
            skip_gain[None],
            hidden_in[0].T,
            norm_gain[None],
        ),
        out_proj.T,
        rows,
        inner,
        model,
        requests,
    )
    block_out, new_state, new_edge = mlp_call(
        devices,
        info,
        (normed, middle, finals, last_edge),
        (mlp_gate, mlp_up, mlp_down.T),
        rows,
        model,
        inner,
        requests,
    )
    return block_out.T[None], new_state[None, None], new_edge[None, None]


def solution(mesh):
    grouped = P("req", "seq", None)
    slots = P("req", "seq", None, None)
    return jax.shard_map(
        shards,
        mesh=mesh,
        in_specs=(grouped, grouped)
        + (P(),) * 9
        + (P(None, "req"), P(None, "req"), P("req", None), slots, slots)
        + (P("req", None),) * 4,
        out_specs=(grouped, slots, slots),
        check_vma=False,
    )
```

```python
import functools

import jax
import jax.numpy as jnp
from jax import lax
from jax.experimental import pallas as pl
from jax.experimental.pallas import tpu as pltpu
from jax.sharding import PartitionSpec as P

STATE = 16
EDGE = 3
NORM_EPS = 1e-06
LANES = 128
FAR = 1e30
HIGHEST_PREC = lax.Precision.HIGHEST
VMEM = pltpu.VMEM
SMEM = pltpu.SMEM


def vspec():
    return pl.BlockSpec(memory_space=VMEM)


def hspec():
    return pl.BlockSpec(memory_space=pltpu.HBM)


def sspec():
    return pl.BlockSpec(memory_space=SMEM)


def col_block(width):
    return 640 if width % 640 == 0 else LANES


MESH_ID = pl.DeviceIdType.MESH


def layout_of(devices):
    depth = 4 if devices >= 32 else 2
    return devices // (2 * depth), depth


def half_width(inner):
    return -(-inner // (2 * LANES)) * LANES


def near_devices(devices):
    across, depth = layout_of(devices)
    me = lax.axis_index("seq")
    core, z, x = me % 2, (me // 2) % depth, me // (2 * depth)
    partner = me + 1 - 2 * core
    z_peers = [x * 2 * depth + ((z + d) % depth) * 2 + core for d in range(1, depth)]
    x_peers = [((x + d) % across) * 2 * depth + z * 2 + core for d in range(1, across)]
    return me, core, z, x, partner, z_peers, x_peers


def my_lanes(core, inner):
    half = half_width(inner)
    return pl.ds(pl.multiple_of(core * (inner - half), LANES), half)


def send(src, dst, sems, index, peer):
    return pltpu.make_async_remote_copy(
        src_ref=src,
        dst_ref=dst,
        send_sem=sems.at[0, index],
        recv_sem=sems.at[1, index],
        device_id={"seq": peer},
        device_id_type=MESH_ID,
    )


def greet(axis_peers):
    barrier = pltpu.get_barrier_semaphore()
    for axis, peer in axis_peers:
        pl.semaphore_signal(barrier, inc=1, device_id={axis: peer}, device_id_type=MESH_ID)
    pl.semaphore_wait(barrier, len(axis_peers))


class Spread:
    def __init__(self, devices, inner, count, split, refs):
        self.devices, self.inner, self.count, self.split = devices, inner, count, split
        self.across, self.depth = layout_of(devices)
        self.part = count // self.depth if split else count
        (
            self.mine,
            self.from_core,
            self.acc,
            self.from_z,
            self.from_x,
            self.from_z2,
            self.other,
            self.sems,
        ) = refs
        _, self.core, self.z, self.x, self.partner, self.z_peers, self.x_peers = near_devices(
            devices
        )
        self.lanes = my_lanes(self.core, inner)
        self.far_lanes = my_lanes(1 - self.core, inner)
        self.copies = []

    @staticmethod
    def scratch(devices, inner, count, split):
        across, depth = layout_of(devices)
        part = count // depth if split else count
        half = half_width(inner)
        b = jnp.bfloat16
        return [
            VMEM((count, 16, inner), b),
            VMEM((count, 16, half), b),
            VMEM((count, 16, half), b),
            VMEM((depth - 1, part, 16, half), b),
            VMEM((across - 1, part, 16, half), b),
            VMEM((depth - 1, part, 16, half), b),
            VMEM((count, 16, half), b),
            pltpu.SemaphoreType.DMA((2, 2 + 2 * (depth - 1) + (across - 1))),
        ]

    def own_part(self, shift=0):
        if not self.split:
            return pl.ds(0, self.part)
        return pl.ds(((self.z + shift) % self.depth) * self.part, self.part)

    def begin(self, copies):
        self.copies = copies
        for copy in copies:
            copy.start()

    def end(self):
        for copy in self.copies:
            copy.wait()

    def start_core(self):
        self.begin(
            [send(self.mine.at[:, :, self.far_lanes], self.from_core, self.sems, 0, self.partner)]
        )

    def finish_core(self):
        self.end()
        total = self.mine[:, :, self.lanes].astype(jnp.float32) + self.from_core[...].astype(
            jnp.float32
        )
        self.acc[...] = total.astype(jnp.bfloat16)

    def start_z(self):
        self.begin(
            [
                send(self.acc.at[self.own_part(d + 1)], self.from_z.at[d], self.sems, 1 + d, peer)
                for d, peer in enumerate(self.z_peers)
            ]
        )

    def finish_z(self):
        self.end()
        here = self.own_part()
        total = self.acc[here].astype(jnp.float32)
        for d in range(self.depth - 1):
            total = total + self.from_z[d].astype(jnp.float32)
        self.acc[here] = total.astype(jnp.bfloat16)

    def start_x(self):
        base = self.depth
        self.begin(
            [
                send(self.acc.at[self.own_part()], self.from_x.at[d], self.sems, base + d, peer)
                for d, peer in enumerate(self.x_peers)
            ]
        )

    def finish_x(self):
        self.end()
        here = self.own_part()
        total = self.acc[here].astype(jnp.float32)
        for d in range(self.across - 1):
            total = total + self.from_x[d].astype(jnp.float32)
        self.acc[here] = total.astype(jnp.bfloat16)

    def start_z2(self):
        if not self.split:
            return
        base = self.depth + self.across - 1
        self.begin(
            [
                send(self.acc.at[self.own_part()], self.from_z2.at[d], self.sems, base + d, peer)
                for d, peer in enumerate(self.z_peers)
            ]
        )

    def finish_z2(self):
        if not self.split:
            return
        self.end()
        for d in range(self.depth - 1):
            self.acc[self.own_part(-(d + 1))] = self.from_z2[d]

    def start_core2(self):
        last = 2 * (self.depth - 1) + self.across
        self.begin([send(self.acc, self.other, self.sems, last, self.partner)])

    def finish_core2(self, out_ref):
        self.end()
        out_ref[:, :, self.lanes] = self.acc[...]
        out_ref[:, :, self.far_lanes] = self.other[...]


def segment(info, r, rows):
    begin = jnp.int32(0)
    for q in range(r):
        begin = begin + info[q]
    end = begin + info[r]
    first = info[16]
    low = jnp.clip(begin - first, 0, rows)
    high = jnp.clip(end - first, 0, rows)
    fresh = begin >= first
    ends = (end > first) & (end <= first + rows)
    return begin, low, high, fresh, ends


def front_stage(
    devices,
    info,
    taps_ref,
    conv_b_flat,
    dt_bias_flat,
    decay_flat,
    skip_flat,
    gain_flat,
    x_hbm,
    cache_hbm,
    cache_edge_hbm,
    x_proj_hbm,
    dt_proj_hbm,
    mixed_ref,
    step_ref,
    proj_ref,
    enter_ref,
    last_edge_ref,
    start_ref,
    param_ref,
    x_ref,
    cache_ref,
    cache_edge_ref,
    x_proj_ref,
    dt_proj_ref,
    fetch_sems,
    ext,
    mixed_b,
    suffix,
    b_wide,
    halo_ref,
    edge3_ref,
    end_ref,
    sum_ref,
    halo_sems,
    pair_h,
    pair_s,
    own_h,
    own_s,
    z_h,
    z_s,
    x_h,
    x_s,
    half_out,
    half_in,
    pre_sems,
    *spread_refs,
):
    fetches = [
        pltpu.make_async_copy(src, dst, fetch_sems.at[i])
        for i, (src, dst) in enumerate(
            (
                (x_hbm, x_ref),
                (cache_edge_hbm, cache_edge_ref),
                (cache_hbm, cache_ref),
                (x_proj_hbm, x_proj_ref),
                (dt_proj_hbm, dt_proj_ref),
            )
        )
    ]
    for copy in fetches:
        copy.start()
    param_ref[pl.ds(0, 4), :] = taps_ref[...]
    for i, flat in enumerate((conv_b_flat, dt_bias_flat, decay_flat, skip_flat, gain_flat)):
        size = flat.shape[0]
        param_ref[pl.ds(4 + i, 1), pl.ds(0, size)] = flat[...].reshape(1, size)
    conv_w_ref = param_ref.at[pl.ds(0, 4)]
    conv_b_ref = param_ref.at[pl.ds(4, 1)]
    dt_bias_ref = param_ref.at[pl.ds(5, 1)]
    decay_ref = param_ref.at[pl.ds(6, 1)]
    rows, inner = x_ref.shape
    requests = start_ref.shape[0]
    me, core, z, x, partner, z_peers, x_peers = near_devices(devices)
    after, before = (me + 1) % devices, (me + devices - 1) % devices
    greet([("seq", p) for p in [partner, after, before] + z_peers + x_peers])
    halo_copy = send(x_ref.at[pl.ds(rows - 16, 16)], halo_ref, halo_sems, 0, after)
    fetches[0].wait()
    halo_copy.start()
    fetches[1].wait()
    per = len(Spread.scratch(devices, inner, 1, False))
    edge_sum = Spread(devices, inner, 1, False, spread_refs[:per])
    state_sum = Spread(devices, inner, requests, True, spread_refs[per:])
    spot = lax.broadcasted_iota(jnp.int32, (16, inner), 0)
    edge_rows = cache_edge_ref[...].astype(jnp.float32)
    placed = jnp.zeros((16, inner), jnp.float32)
    for r in range(requests):
        take = (info[8 + r] == me) & (info[4 + r] > 0)
        for j in range(EDGE):
            placed = jnp.where((spot == r * EDGE + j) & take, edge_rows[j : j + 1], placed)
    edge_sum.mine[0] = placed.astype(jnp.bfloat16)
    edge_sum.start_core()
    fetches[2].wait()
    for r in range(requests):
        take = (info[8 + r] == me) & (info[4 + r] > 0)
        state_sum.mine[r] = jnp.where(take, cache_ref[...], 0.0).astype(jnp.bfloat16)
    state_sum.start_core()
    ext[pl.ds(16, rows), :] = x_ref[...].astype(jnp.float32)
    fetches[3].wait()
    fetches[4].wait()
    edge_sum.finish_core()
    edge_sum.start_z()
    state_sum.finish_core()
    state_sum.start_z()
    edge_sum.finish_z()
    edge_sum.start_x()
    state_sum.finish_z()
    state_sum.start_x()
    edge_sum.finish_x()
    edge_sum.start_core2()
    edge_sum.finish_core2(edge3_ref)
    edge_ref = edge3_ref.at[0]
    halo_copy.wait()
    width = col_block(inner)
    rank = dt_proj_ref.shape[0]
    ext[pl.ds(0, 16), :] = halo_ref[...].astype(jnp.float32)
    first_pos = info[16]
    position = first_pos + lax.broadcasted_iota(jnp.int32, (rows, LANES), 0)
    marks = [segment(info, r, rows) for r in range(requests)]
    begin = jnp.zeros((rows, LANES), jnp.int32)
    request = jnp.zeros((rows, LANES), jnp.int32)
    last_begin, last_req = jnp.int32(0), jnp.int32(0)
    for r in range(1, requests):
        reached = position >= marks[r][0]
        begin = jnp.where(reached, marks[r][0], begin)
        request = jnp.where(reached, r, request)
        inside = first_pos + rows - 1 >= marks[r][0]
        last_begin = jnp.where(inside, marks[r][0], last_begin)
        last_req = jnp.where(inside, r, last_req)
    offset = position - begin
    in_last = (position >= last_begin).astype(jnp.float32)
    edge_id = lax.broadcasted_iota(jnp.int32, (rows, 16), 1)
    hots = []
    for lag in (1, 2, 3):
        want = request * EDGE + EDGE + offset - lag
        hit = (edge_id == want[:, :16]) & (offset[:, :16] < lag)
        hots.append(hit.astype(jnp.float32).astype(jnp.bfloat16))

    keep = {}
    for lag in (1, 2, 3):
        keep[lag] = jnp.concatenate([offset] * (width // LANES), axis=1) >= lag
    for first in range(0, inner, width):
        cols = pl.ds(first, width)
        edges = edge_ref[:, cols]
        total = conv_b_ref[:, cols] + conv_w_ref[pl.ds(3, 1), cols] * ext[pl.ds(16, rows), cols]
        for lag in (1, 2, 3):
            near = ext[pl.ds(16 - lag, rows), cols]
            far = jnp.dot(hots[lag - 1], edges, preferred_element_type=jnp.float32)
            row = jnp.where(keep[lag], near, far)
            total = total + conv_w_ref[pl.ds(3 - lag, 1), cols] * row
        mixed = (total / (1.0 + jnp.exp(-total))).astype(jnp.bfloat16)
        mixed_b[:, cols] = mixed
        mixed_ref[:, cols] = mixed.astype(jnp.float32)

    proj = lax.dot_general(
        mixed_b[...],
        x_proj_ref[...],
        (((1,), (1,)), ((), ())),
        preferred_element_type=jnp.float32,
    )
    state_sum.finish_x()
    state_sum.start_z2()
    proj_ref[...] = proj
    for s in range(STATE):
        b_wide[s] = jnp.broadcast_to(proj[:, rank + s : rank + s + 1], (rows, LANES))
    dt_low = proj[:, :rank].astype(jnp.bfloat16)
    row_id = lax.broadcasted_iota(jnp.int32, (rows, rows), 0)
    col_id = lax.broadcasted_iota(jnp.int32, (rows, rows), 1)
    later = (col_id > row_id).astype(jnp.bfloat16)
    for first in range(0, inner, width):
        cols = pl.ds(first, width)
        v = jnp.dot(dt_low, dt_proj_ref[:, cols], preferred_element_type=jnp.float32)
        v = v + dt_bias_ref[:, cols]
        step = jnp.maximum(v, 0.0) + jnp.log1p(jnp.exp(-jnp.abs(v)))
        step_ref[:, cols] = step
        high = step.astype(jnp.bfloat16)
        rest = step - high.astype(jnp.float32)
        mid = rest.astype(jnp.bfloat16)
        low = (rest - mid.astype(jnp.float32)).astype(jnp.bfloat16)
        after = (
            jnp.dot(later, high, preferred_element_type=jnp.float32)
            + jnp.dot(later, mid, preferred_element_type=jnp.float32)
            + jnp.dot(later, low, preferred_element_type=jnp.float32)
        )
        suffix[:, cols] = after

    state_sum.finish_z2()
    state_sum.start_core2()
    state_sum.finish_core2(start_ref)
    starts_here = (last_begin >= first_pos).astype(jnp.int32)
    flag = jnp.full((1, LANES), starts_here, jnp.int32).astype(jnp.float32)
    power = (lax.broadcasted_iota(jnp.int32, (STATE, LANES), 0) + 1).astype(jnp.float32)

    def one_tile(j, carry):
        cols = pl.ds(pl.multiple_of(j * LANES, LANES), LANES)
        rate = decay_ref[:, cols]
        acc = [jnp.zeros((8, LANES), jnp.float32) for _ in range(STATE)]
        since = jnp.zeros((8, LANES), jnp.float32)
        for tile in range(rows // 8):
            here = pl.ds(tile * 8, 8)
            fade = jnp.exp(-rate * suffix[here, cols])
            step = step_ref[here, cols] * in_last[tile * 8 : tile * 8 + 8]
            since = since + step
            push = step * mixed_ref[here, cols]
            for s in range(STATE):
                push = push * fade
                acc[s] = acc[s] + push * b_wide[s, here, :]
        ends = jnp.concatenate([jnp.sum(a, axis=0, keepdims=True) for a in acc], axis=0)
        since = jnp.sum(since, axis=0, keepdims=True)
        seed = jnp.exp(-(rate * since) * power) * start_ref[last_req, :, cols].astype(jnp.float32)
        end_ref[:, cols] = ends + flag * seed
        sum_ref[:, cols] = jnp.where(flag > 0.5, FAR, since)
        return carry

    lax.fori_loop(0, inner // LANES, one_tile, 0)
    power16 = (lax.broadcasted_iota(jnp.int32, (STATE, LANES), 0) + 1).astype(jnp.float32)
    half = half_width(inner)
    tiles = half // LANES
    base = core * (inner - half)
    own_h[...] = end_ref[...].astype(jnp.bfloat16)
    for j in range(inner // LANES):
        own_s[pl.ds(j, 1), :] = sum_ref[:, pl.ds(j * LANES, LANES)]
    pair = [
        send(own_h, pair_h, pre_sems, 0, partner),
        send(own_s, pair_s, pre_sems, 1, partner),
    ]
    for copy in pair:
        copy.start()
    across, depth = layout_of(devices)
    first_core = core == 0

    def lane(j):
        return pl.ds(pl.multiple_of(base + j * LANES, LANES), LANES)

    def f32(value):
        return value.astype(jnp.float32)

    for copy in pair:
        copy.wait()
    z_sum = []
    for j in range(tiles):
        rate = decay_ref[:, lane(j)] * power16
        mine, theirs = own_h[:, lane(j)], pair_h[:, lane(j)]
        shift = (inner - half) // LANES
        s_mine = jnp.where(first_core, own_s[j : j + 1], own_s[j + shift : j + shift + 1])
        s_pair = jnp.where(first_core, pair_s[j : j + 1], pair_s[j + shift : j + shift + 1])
        h0 = f32(jnp.where(first_core, f32(mine), f32(theirs)))
        h1 = f32(jnp.where(first_core, f32(theirs), f32(mine)))
        s1 = jnp.where(first_core, s_pair, s_mine)
        z_h[0, :, pl.ds(j * LANES, LANES)] = (jnp.exp(-rate * s1) * h0 + h1).astype(jnp.bfloat16)
        z_s[0, pl.ds(j, 1), :] = s_mine + s_pair
    copies = []
    for d, peer in enumerate(z_peers):
        copies.append(send(z_h.at[0], z_h.at[d + 1], pre_sems, 2 + 2 * d, peer))
        copies.append(send(z_s.at[0], z_s.at[d + 1], pre_sems, 3 + 2 * d, peer))
    for copy in copies:
        copy.start()
    for copy in copies:
        copy.wait()
    prefix = []
    for j in range(tiles):
        cols = pl.ds(j * LANES, LANES)
        rate = decay_ref[:, lane(j)] * power16
        total = jnp.zeros((STATE, LANES), jnp.float32)
        part = jnp.zeros((STATE, LANES), jnp.float32)
        total_s = jnp.zeros((1, LANES), jnp.float32)
        part_s = jnp.zeros((1, LANES), jnp.float32)
        for k in range(depth):
            slot = (z - k + depth) % depth
            s_k = z_s[slot, pl.ds(j, 1), :]
            h_k = f32(z_h[slot, :, cols])
            fade = jnp.exp(-rate * s_k)
            total = fade * total + h_k
            part = jnp.where(k < z, fade * part + h_k, part)
            total_s = total_s + s_k
            part_s = jnp.where(k < z, part_s + s_k, part_s)
        x_h[0, :, cols] = total.astype(jnp.bfloat16)
        x_s[0, pl.ds(j, 1), :] = total_s
        prefix.append((part, part_s))
    copies = []
    first = 2 + 2 * (depth - 1)
    for d, peer in enumerate(x_peers):
        copies.append(send(x_h.at[0], x_h.at[d + 1], pre_sems, first + 2 * d, peer))
        copies.append(send(x_s.at[0], x_s.at[d + 1], pre_sems, first + 1 + 2 * d, peer))
    for copy in copies:
        copy.start()
    for copy in copies:
        copy.wait()
    for j in range(tiles):
        cols = pl.ds(j * LANES, LANES)
        rate = decay_ref[:, lane(j)] * power16
        part = jnp.zeros((STATE, LANES), jnp.float32)
        for k in range(across):
            slot = (x - k + across) % across
            value = jnp.exp(-rate * x_s[slot, pl.ds(j, 1), :]) * part + f32(x_h[slot, :, cols])
            part = jnp.where(k < x, value, part)
        inner_part, inner_s = prefix[j]
        half_out[:, cols] = jnp.exp(-rate * inner_s) * part + inner_part
    last = first + 2 * (across - 1)
    swap = send(half_out, half_in, pre_sems, last, partner)
    swap.start()
    swap.wait()
    enter_ref[:, my_lanes(core, inner)] = half_out[...]
    enter_ref[:, my_lanes(1 - core, inner)] = half_in[...]
    for j in range(inner // LANES):
        cols = pl.ds(j * LANES, LANES)
        rate = decay_ref[:, cols] * power16
        chip = enter_ref[:, cols]
        second = jnp.exp(-rate * pair_s[j : j + 1]) * chip + f32(pair_h[:, cols])
        enter_ref[:, cols] = jnp.where(first_core, chip, second)

    row_of = lax.broadcasted_iota(jnp.int32, (16, LANES), 0)
    from_of = lax.broadcasted_iota(jnp.int32, (16, LANES), 1)
    near_at = jnp.full((16, LANES), -1, jnp.int32)
    far_at = jnp.full((16, LANES), -1, jnp.int32)
    for r in range(requests):
        _, _, high, _, ends = marks[r]
        size = info[r]
        for j in range(EDGE):
            lag = EDGE - 1 - j
            near = jnp.where(ends & (size > lag), high + 15 - lag, -1)
            far = jnp.where(ends & (size <= lag), r * EDGE + EDGE + size - 1 - lag, -1)
            near_at = jnp.where(row_of == r * EDGE + j, near, near_at)
            far_at = jnp.where(row_of == r * EDGE + j, far, far_at)

    def hot_rows(at, count):
        return (from_of[:, :count] == at[:, :count]).astype(jnp.float32).astype(jnp.bfloat16)

    for first in range(0, inner, width):
        cols = pl.ds(first, width)
        last_edge_ref[:, cols] = (
            jnp.dot(hot_rows(near_at - 16, rows), x_ref[:, cols], preferred_element_type=jnp.float32)
            + jnp.dot(hot_rows(near_at, 16), halo_ref[:, cols], preferred_element_type=jnp.float32)
            + jnp.dot(hot_rows(far_at, 16), edge_ref[:, cols], preferred_element_type=jnp.float32)
        )


def front_call(devices, info, args, rows, inner, proj_width, requests):
    f32, bf16 = jnp.float32, jnp.bfloat16
    across, depth = layout_of(devices)
    half = half_width(inner)
    s_rows = -(-(inner // LANES) // 8) * 8
    return pl.pallas_call(
        functools.partial(front_stage, devices),
        out_shape=(
            jax.ShapeDtypeStruct((rows, inner), f32),
            jax.ShapeDtypeStruct((rows, inner), f32),
            jax.ShapeDtypeStruct((rows, proj_width), f32),
            jax.ShapeDtypeStruct((STATE, inner), f32),
            jax.ShapeDtypeStruct((16, inner), f32),
            jax.ShapeDtypeStruct((requests, STATE, inner), bf16),
            jax.ShapeDtypeStruct((16, inner), f32),
        ),
        in_specs=[sspec()] + [vspec()] * 6 + [hspec()] * (len(args) - 6),
        out_specs=tuple([vspec()] * 7),
        scratch_shapes=[
            VMEM((rows, inner), bf16),
            VMEM((STATE, inner), f32),
            VMEM((EDGE, inner), bf16),
            VMEM((proj_width, inner), bf16),
            VMEM((proj_width - 2 * STATE, inner), bf16),
            pltpu.SemaphoreType.DMA((5,)),
            VMEM((rows + 16, inner), f32),
            VMEM((rows, inner), bf16),
            VMEM((rows, inner), f32),
            VMEM((STATE, rows, LANES), f32),
            VMEM((16, inner), bf16),
            VMEM((1, 16, inner), bf16),
            VMEM((STATE, inner), f32),
            VMEM((1, inner), f32),
            pltpu.SemaphoreType.DMA((2, 1)),
            VMEM((STATE, inner), bf16),
            VMEM((s_rows, LANES), f32),
            VMEM((STATE, inner), bf16),
            VMEM((s_rows, LANES), f32),
            VMEM((depth, STATE, half), bf16),
            VMEM((depth, 16, LANES), f32),
            VMEM((across, STATE, half), bf16),
            VMEM((across, 16, LANES), f32),
            VMEM((STATE, half), f32),
            VMEM((STATE, half), f32),
            pltpu.SemaphoreType.DMA((2, 3 + 2 * (depth + across - 2))),
        ]
        + Spread.scratch(devices, inner, 1, False)
        + Spread.scratch(devices, inner, requests, True),
        compiler_params=pltpu.CompilerParams(
            vmem_limit_bytes=61 << 20, collective_id=0, has_side_effects=True
        ),
        cost_estimate=pl.CostEstimate(
            flops=400_000_000, bytes_accessed=8_000_000, transcendentals=2_000_000
        ),
        name="front_stage",
    )(info, *args)


def scan_stage(
    info,
    mixed_ref,
    step_ref,
    proj_ref,
    enter_ref,
    start_ref,
    param_ref,
    hidden_hbm,
    out_w_hbm,
    middle_ref,
    normed_ref,
    final_ref,
    bc_wide,
    y_ref,
    ssm_b,
    out_w,
    hidden_ref,
    w_sem,
    hidden_sem,
):
    rows, inner = mixed_ref.shape
    width = col_block(inner)
    tiles = width // LANES
    rank = proj_ref.shape[1] - 2 * STATE
    fetch = pltpu.make_async_copy(out_w_hbm, out_w, w_sem)
    fetch.start()
    fetch_hidden = pltpu.make_async_copy(hidden_hbm, hidden_ref, hidden_sem)
    fetch_hidden.start()
    model = hidden_ref.shape[0]
    decay_ref = param_ref.at[pl.ds(6, 1)]
    skip_ref = param_ref.at[pl.ds(7, 1)]

    turned = jnp.transpose(proj_ref[:, rank : rank + 2 * STATE])
    for t in range(rows):
        bc_wide[t] = jnp.broadcast_to(turned[:, t : t + 1], (2 * STATE, LANES))
    final_ref[...] = jnp.zeros_like(final_ref)
    power = (lax.broadcasted_iota(jnp.int32, (8, LANES), 0) + 1).astype(jnp.float32)

    def wide_step(t, i, step, push, fade8, state, rates):
        b_low, b_high = bc_wide[t, 0:8], bc_wide[t, 8:16]
        c_low, c_high = bc_wide[t, 16:24], bc_wide[t, 24:32]
        outs, new = [], []
        for j in range(tiles):
            s_row, p_row, f_row = (
                jnp.broadcast_to(part[j][i : i + 1], (8, LANES)) for part in (step, push, fade8)
            )
            d_low = jnp.exp(s_row * rates[j])
            d_high = d_low * f_row
            low = d_low * state[2 * j] + b_low * p_row
            high = d_high * state[2 * j + 1] + b_high * p_row
            new += [low, high]
            outs.append(jnp.sum(c_low * low + c_high * high, axis=0, keepdims=True))
        return outs, tuple(new)

    def one_block(g, carry):
        base = pl.multiple_of(g * width, LANES)
        tile_cols = [pl.ds(pl.multiple_of(base + j * LANES, LANES), LANES) for j in range(tiles)]
        rates = [-decay_ref[:, c] * power for c in tile_cols]
        decays = [decay_ref[:, c] for c in tile_cols]

        def load(row, count):
            step = [step_ref[pl.ds(row, count), c] for c in tile_cols]
            push = [s * mixed_ref[pl.ds(row, count), c] for s, c in zip(step, tile_cols)]
            fade8 = [jnp.exp(-8.0 * (s * d)) for s, d in zip(step, decays)]
            return step, push, fade8

        def eight(block, state, limits=None):
            row = pl.multiple_of(block * 8, 8)
            step, push, fade8 = load(row, 8)
            kept = [[] for _ in range(tiles)]
            for i in range(8):
                outs, new = wide_step(row + i, i, step, push, fade8, state, rates)
                if limits is not None:
                    active = (row + i >= limits[0]) & (row + i < limits[1])
                    new = tuple(jnp.where(active, a, b) for a, b in zip(new, state))
                state = new
                for j in range(tiles):
                    kept[j].append(outs[j])
            for j in range(tiles):
                y = jnp.concatenate(kept[j], axis=0)
                if limits is not None:
                    at = row + lax.broadcasted_iota(jnp.int32, (8, LANES), 0)
                    y = jnp.where(
                        (at >= limits[0]) & (at < limits[1]), y, y_ref[pl.ds(row, 8), tile_cols[j]]
                    )
                y_ref[pl.ds(row, 8), tile_cols[j]] = y
            return state

        for r in range(final_ref.shape[0]):
            _, begin, end, new, ends = segment(info, r, rows)

            @pl.when(end > begin)
            def _():
                state = []
                for c in tile_cols:
                    for half in (pl.ds(0, 8), pl.ds(8, 8)):
                        old = enter_ref[half, c]
                        seed = start_ref[r, half, c].astype(jnp.float32)
                        state.append(jnp.where(new, seed, old))
                state = tuple(state)
                part = functools.partial(eight, limits=(begin, end))
                low, low_up, high = begin // 8, (begin + 7) // 8, end // 8
                state = lax.fori_loop(low, low_up, part, state)
                state = lax.fori_loop(low_up, jnp.maximum(high, low_up), eight, state)
                tail = jnp.where((high >= low_up) & (end % 8 > 0), high + 1, high)
                state = lax.fori_loop(high, tail, part, state)

                @pl.when(ends)
                def _():
                    for j, c in enumerate(tile_cols):
                        final_ref[r, pl.ds(0, 8), c] = state[2 * j]
                        final_ref[r, pl.ds(8, 8), c] = state[2 * j + 1]

        y = y_ref[:, pl.ds(base, width)]
        y = y + skip_ref[:, pl.ds(base, width)] * mixed_ref[:, pl.ds(base, width)]
        ssm_b[:, pl.ds(base, width)] = y.astype(jnp.bfloat16)
        return carry

    lax.fori_loop(0, inner // width, one_block, 0)
    fetch.wait()
    fetch_hidden.wait()
    middle = jnp.transpose(hidden_ref[...].astype(jnp.float32))
    for first in range(0, inner, width):
        middle = middle + lax.dot_general(
            ssm_b[:, first : first + width],
            out_w[:, first : first + width],
            (((1,), (1,)), ((), ())),
            preferred_element_type=jnp.float32,
        )
    middle_ref[...] = middle
    scale = lax.rsqrt(jnp.mean(middle * middle, axis=1, keepdims=True) + NORM_EPS)
    normed_ref[...] = (middle * scale * param_ref[8:9, :model]).astype(jnp.bfloat16)


def scan_call(info, args, out_w, rows, inner, model, requests):
    f32 = jnp.float32
    return pl.pallas_call(
        scan_stage,
        out_shape=(
            jax.ShapeDtypeStruct((rows, model), f32),
            jax.ShapeDtypeStruct((rows, model), jnp.bfloat16),
            jax.ShapeDtypeStruct((requests, STATE, inner), f32),
        ),
        in_specs=[sspec()] + [vspec()] * (len(args) - 1) + [hspec()] * 2,
        out_specs=tuple([vspec()] * 3),
        scratch_shapes=[
            VMEM((rows, 2 * STATE, LANES), f32),
            VMEM((rows, inner), f32),
            VMEM((rows, inner), jnp.bfloat16),
            VMEM((model, inner), jnp.bfloat16),
            VMEM((model, rows), jnp.bfloat16),
            pltpu.SemaphoreType.DMA,
            pltpu.SemaphoreType.DMA,
        ],
        compiler_params=pltpu.CompilerParams(vmem_limit_bytes=61 << 20),
        cost_estimate=pl.CostEstimate(
            flops=1_400_000_000, bytes_accessed=18_000_000, transcendentals=4_000_000
        ),
        name="scan_stage",
    )(info, *args, out_w)


def mlp_stage(
    devices,
    info,
    normed_hbm,
    middle_hbm,
    final_hbm,
    last_edge_hbm,
    gate_hbm,
    up_hbm,
    down_hbm,
    out_ref,
    new_state_ref,
    new_edge_ref,
    normed_ref,
    middle_ref,
    final_ref,
    last_edge_ref,
    gate_w,
    up_w,
    down_w,
    fetch_sems,
    near1,
    near2,
    far,
    out1,
    out2,
    far_out,
    own_out,
    low_in,
    high_in,
    far_in,
    ring_sems,
    full,
    full_edge,
    *spread_refs,
):
    rows, model = normed_ref.shape
    half = rows // 2
    inner = final_ref.shape[2]
    requests = final_ref.shape[0]
    me, _, _, _, partner, z_peers, x_peers = near_devices(devices)
    ring = lax.axis_size("req")
    here = lax.axis_index("req")
    above, below = (here + 1) % ring, (here + ring - 1) % ring
    fetches = [
        pltpu.make_async_copy(src, dst, fetch_sems.at[i])
        for i, (src, dst) in enumerate(
            (
                (normed_hbm, normed_ref),
                (final_hbm, final_ref),
                (last_edge_hbm, last_edge_ref),
                (gate_hbm, gate_w),
                (up_hbm, up_w),
                (down_hbm, down_w),
                (middle_hbm, middle_ref),
            )
        )
    ]
    for copy in fetches:
        copy.start()
    greet(
        [("req", above), ("req", below)] + [("seq", p) for p in [partner] + z_peers + x_peers]
    )

    def hop(src, dst, index, peer):
        return pltpu.make_async_remote_copy(
            src_ref=src,
            dst_ref=dst,
            send_sem=ring_sems.at[0, index],
            recv_sem=ring_sems.at[1, index],
            device_id={"req": peer},
            device_id_type=MESH_ID,
        )

    first, second = pl.ds(0, half), pl.ds(half, half)
    up_a = hop(normed_ref.at[first], near1.at[first], 0, above)
    down_b = hop(normed_ref.at[second], near1.at[second], 1, below)
    up_a2 = hop(near1.at[first], far.at[first], 2, above)
    down_b2 = hop(near1.at[second], far.at[second], 3, below)
    up_b = hop(normed_ref.at[second], near2.at[first], 4, above)
    down_a = hop(normed_ref.at[first], near2.at[second], 5, below)
    far_up = hop(far_out.at[first], far_in.at[first], 6, above)
    far_down = hop(far_out.at[second], far_in.at[second], 7, below)
    back_down = hop(out1.at[first], high_in.at[first], 8, below)
    back_up = hop(out1.at[second], low_in.at[second], 9, above)
    last_down = hop(out2.at[first], high_in.at[second], 10, below)
    last_up = hop(out2.at[second], low_in.at[first], 11, above)
    fetches[0].wait()
    up_a.start()
    down_b.start()
    per = len(Spread.scratch(devices, inner, 1, False))
    finals = Spread(devices, inner, requests, True, spread_refs[:per])
    edges = Spread(devices, inner, 1, False, spread_refs[per:])
    fetches[1].wait()
    for r in range(requests):
        finals.mine[r] = final_ref[r].astype(jnp.bfloat16)
    finals.start_core()
    fetches[2].wait()
    edges.mine[0] = last_edge_ref[...].astype(jnp.bfloat16)
    edges.start_core()

    def hidden_units(value):
        gate = jnp.dot(value, gate_w[...], preferred_element_type=jnp.float32)
        up = jnp.dot(value, up_w[...], preferred_element_type=jnp.float32)
        hidden = (gate / (1.0 + jnp.exp(-gate)) * up).astype(jnp.bfloat16)
        return lax.dot_general(
            hidden, down_w[...], (((1,), (1,)), ((), ())), preferred_element_type=jnp.float32
        )

    finals.finish_core()
    finals.start_z()
    edges.finish_core()
    for copy in fetches[3:]:
        copy.wait()
    up_a.wait_recv()
    up_a2.start()
    down_b.wait_recv()
    down_b2.start()
    up_b.start()
    down_a.start()
    out1[...] = hidden_units(near1[...]).astype(jnp.bfloat16)
    finals.finish_z()
    finals.start_x()
    edges.start_z()
    up_a2.wait_recv()
    down_b2.wait_recv()
    far_out[...] = hidden_units(far[...]).astype(jnp.bfloat16)
    far_up.start()
    far_down.start()
    back_down.start()
    back_up.start()
    up_b.wait_recv()
    down_a.wait_recv()
    own_out[...] = hidden_units(near2[...])
    finals.finish_x()
    finals.start_z2()
    far_down.wait_recv()
    out2[first] = (own_out[first] + far_in[second].astype(jnp.float32)).astype(jnp.bfloat16)
    last_down.start()
    far_up.wait_recv()
    out2[second] = (own_out[second] + far_in[first].astype(jnp.float32)).astype(jnp.bfloat16)
    last_up.start()
    edges.finish_z()
    edges.start_x()
    own_out[...] = hidden_units(normed_ref[...]) + middle_ref[...]
    finals.finish_z2()
    finals.start_core2()
    edges.finish_x()
    edges.start_core2()
    finals.finish_core2(full)
    state = jnp.zeros((STATE, inner), jnp.float32)
    for r in range(requests):
        state = jnp.where(info[12 + r] == me, full[r].astype(jnp.float32), state)
    new_state_ref[...] = state
    edges.finish_core2(full_edge)
    gathered = full_edge[0].astype(jnp.float32)
    edge = jnp.zeros((EDGE, inner), jnp.float32)
    for r in range(requests):
        owned = info[12 + r] == me
        edge = jnp.where(owned, gathered[r * EDGE : (r + 1) * EDGE], edge)
    new_edge_ref[...] = edge.astype(jnp.bfloat16)
    back_down.wait_recv()
    back_up.wait_recv()
    last_up.wait_recv()
    last_down.wait_recv()
    total = own_out[...] + low_in[...].astype(jnp.float32) + high_in[...].astype(jnp.float32)
    out_ref[...] = jnp.transpose(total).astype(jnp.bfloat16)
    for copy in (
        up_a, down_b, up_a2, down_b2, up_b, down_a,
        far_up, far_down, back_down, back_up, last_up, last_down,
    ):
        copy.wait_send()


def mlp_call(devices, info, args, weights, rows, model, inner, requests):
    f32, bf16 = jnp.float32, jnp.bfloat16
    hidden = weights[0].shape[1]
    return pl.pallas_call(
        functools.partial(mlp_stage, devices),
        out_shape=(
            jax.ShapeDtypeStruct((model, rows), bf16),
            jax.ShapeDtypeStruct((STATE, inner), f32),
            jax.ShapeDtypeStruct((EDGE, inner), bf16),
        ),
        in_specs=[sspec()] + [hspec()] * (len(args) + len(weights)),
        out_specs=tuple([vspec()] * 3),
        scratch_shapes=[
            VMEM((rows, model), bf16),
            VMEM((rows, model), f32),
            VMEM((requests, STATE, inner), f32),
            VMEM((16, inner), f32),
            VMEM((model, hidden), bf16),
            VMEM((model, hidden), bf16),
            VMEM((model, hidden), bf16),
            pltpu.SemaphoreType.DMA((7,)),
            VMEM((rows, model), bf16),
            VMEM((rows, model), bf16),
            VMEM((rows, model), bf16),
            VMEM((rows, model), bf16),
            VMEM((rows, model), bf16),
            VMEM((rows, model), bf16),
            VMEM((rows, model), f32),
            VMEM((rows, model), bf16),
            VMEM((rows, model), bf16),
            VMEM((rows, model), bf16),
            pltpu.SemaphoreType.DMA((2, 12)),
            VMEM((requests, 16, inner), bf16),
            VMEM((1, 16, inner), bf16),
        ]
        + Spread.scratch(devices, inner, requests, True)
        + Spread.scratch(devices, inner, 1, False),
        compiler_params=pltpu.CompilerParams(
            vmem_limit_bytes=61 << 20, collective_id=1, has_side_effects=True
        ),
        cost_estimate=pl.CostEstimate(
            flops=7_000_000_000, bytes_accessed=16_000_000, transcendentals=1_000_000
        ),
        name="mlp_stage",
    )(info, *args, *weights)


def handing_stage(*refs):
    count = (len(refs) - 1) // 2
    sems = refs[-1]
    copies = [
        pltpu.make_async_copy(refs[i], refs[count + i], sems.at[i]) for i in range(count)
    ]
    for copy in copies:
        copy.start()
    for copy in copies:
        copy.wait()


def handed(*arrays):
    return pl.pallas_call(
        handing_stage,
        out_shape=tuple(jax.ShapeDtypeStruct(a.shape, a.dtype) for a in arrays),
        in_specs=[pl.BlockSpec(memory_space=pl.ANY)] * len(arrays),
        out_specs=tuple([hspec()] * len(arrays)),
        scratch_shapes=[pltpu.SemaphoreType.DMA((len(arrays),))],
        name="handing_stage",
    )(*arrays)


def shards(
    hidden_in,
    mamba_in,
    conv_weight,
    conv_bias,
    x_proj,
    dt_proj,
    dt_bias,
    decay_rate,
    skip_gain,
    out_proj,
    norm_gain,
    mlp_gate,
    mlp_up,
    mlp_down,
    cache_state,
    cache_edge,
    req_lengths,
    cont_flag,
    cache_source,
    owner_slot,
):
    rows, inner = mamba_in.shape[1:]
    model = hidden_in.shape[2]
    requests = req_lengths.shape[1]
    devices = lax.axis_size("seq")
    place = lax.axis_index("seq")
    info = jnp.concatenate(
        [
            req_lengths[0],
            cont_flag[0],
            cache_source[0],
            owner_slot[0],
            jnp.reshape(place * rows, (1,)).astype(jnp.int32),
        ]
    )
    mixed, step, proj, enter, last_edge, start_state, params = front_call(
        devices,
        info,
        (
            conv_weight,
            conv_bias,
            dt_bias,
            decay_rate,
            skip_gain,
            norm_gain,
            mamba_in[0],
            cache_state[0, 0],
            cache_edge[0, 0],
            x_proj.T,
            dt_proj,
        ),
        rows,
        inner,
        x_proj.shape[1],
        requests,
    )
    middle, normed, finals = scan_call(
        info,
        (mixed, step, proj, enter, start_state, params, hidden_in[0].T),
        out_proj.T,
        rows,
        inner,
        model,
        requests,
    )
    block_out, new_state, new_edge = handed(
        *mlp_call(
            devices,
            info,
            (normed, middle, finals, last_edge),
            (mlp_gate, mlp_up, mlp_down.T),
            rows,
            model,
            inner,
            requests,
        )
    )
    return block_out.T[None], new_state[None, None], new_edge[None, None]


def solution(mesh):
    grouped = P("req", "seq", None)
    slots = P("req", "seq", None, None)
    return jax.shard_map(
        shards,
        mesh=mesh,
        in_specs=(grouped, grouped)
        + (P(),) * 9
        + (P(None, "req"), P(None, "req"), P("req", None), slots, slots)
        + (P("req", None),) * 4,
        out_specs=(grouped, slots, slots),
        check_vma=False,
    )
```

```python
import functools

import jax
import jax.numpy as jnp
from jax import lax
from jax.experimental import pallas as pl
from jax.experimental.pallas import tpu as pltpu
from jax.sharding import PartitionSpec as P

STATE = 16
EDGE = 3
NORM_EPS = 1e-06
LANES = 128
FAR = 1e30
HIGHEST_PREC = lax.Precision.HIGHEST
VMEM = pltpu.VMEM
SMEM = pltpu.SMEM


def vspec():
    return pl.BlockSpec(memory_space=VMEM)


def hspec():
    return pl.BlockSpec(memory_space=pltpu.HBM)


def sspec():
    return pl.BlockSpec(memory_space=SMEM)


def col_block(width):
    return 640 if width % 640 == 0 else LANES


MESH_ID = pl.DeviceIdType.MESH


def layout_of(devices):
    depth = 4 if devices >= 32 else 2
    return devices // (2 * depth), depth


def half_width(inner):
    return -(-inner // (2 * LANES)) * LANES


def near_devices(devices):
    across, depth = layout_of(devices)
    me = lax.axis_index("seq")
    core, z, x = me % 2, (me // 2) % depth, me // (2 * depth)
    partner = me + 1 - 2 * core
    z_peers = [x * 2 * depth + ((z + d) % depth) * 2 + core for d in range(1, depth)]
    x_peers = [((x + d) % across) * 2 * depth + z * 2 + core for d in range(1, across)]
    return me, core, z, x, partner, z_peers, x_peers


def my_lanes(core, inner):
    half = half_width(inner)
    return pl.ds(pl.multiple_of(core * (inner - half), LANES), half)


def send(src, dst, sems, index, peer):
    return pltpu.make_async_remote_copy(
        src_ref=src,
        dst_ref=dst,
        send_sem=sems.at[0, index],
        recv_sem=sems.at[1, index],
        device_id={"seq": peer},
        device_id_type=MESH_ID,
    )


def greet(axis_peers):
    barrier = pltpu.get_barrier_semaphore()
    for axis, peer in axis_peers:
        pl.semaphore_signal(barrier, inc=1, device_id={axis: peer}, device_id_type=MESH_ID)
    pl.semaphore_wait(barrier, len(axis_peers))


class Spread:
    def __init__(self, devices, inner, count, split, refs):
        self.devices, self.inner, self.count, self.split = devices, inner, count, split
        self.across, self.depth = layout_of(devices)
        self.part = count // self.depth if split else count
        (
            self.mine,
            self.from_core,
            self.acc,
            self.from_z,
            self.from_x,
            self.from_z2,
            self.other,
            self.sems,
        ) = refs
        _, self.core, self.z, self.x, self.partner, self.z_peers, self.x_peers = near_devices(
            devices
        )
        self.lanes = my_lanes(self.core, inner)
        self.far_lanes = my_lanes(1 - self.core, inner)
        self.copies = []

    @staticmethod
    def scratch(devices, inner, count, split):
        across, depth = layout_of(devices)
        part = count // depth if split else count
        half = half_width(inner)
        b = jnp.bfloat16
        return [
            VMEM((count, 16, inner), b),
            VMEM((count, 16, half), b),
            VMEM((count, 16, half), b),
            VMEM((depth - 1, part, 16, half), b),
            VMEM((across - 1, part, 16, half), b),
            VMEM((depth - 1, part, 16, half), b),
            VMEM((count, 16, half), b),
            pltpu.SemaphoreType.DMA((2, 2 + 2 * (depth - 1) + (across - 1))),
        ]

    def own_part(self, shift=0):
        if not self.split:
            return pl.ds(0, self.part)
        return pl.ds(((self.z + shift) % self.depth) * self.part, self.part)

    def begin(self, copies):
        self.copies = copies
        for copy in copies:
            copy.start()

    def end(self):
        for copy in self.copies:
            copy.wait()

    def start_core(self):
        self.begin(
            [send(self.mine.at[:, :, self.far_lanes], self.from_core, self.sems, 0, self.partner)]
        )

    def finish_core(self):
        self.end()
        total = self.mine[:, :, self.lanes].astype(jnp.float32) + self.from_core[...].astype(
            jnp.float32
        )
        self.acc[...] = total.astype(jnp.bfloat16)

    def start_z(self):
        self.begin(
            [
                send(self.acc.at[self.own_part(d + 1)], self.from_z.at[d], self.sems, 1 + d, peer)
                for d, peer in enumerate(self.z_peers)
            ]
        )

    def finish_z(self):
        self.end()
        here = self.own_part()
        total = self.acc[here].astype(jnp.float32)
        for d in range(self.depth - 1):
            total = total + self.from_z[d].astype(jnp.float32)
        self.acc[here] = total.astype(jnp.bfloat16)

    def start_x(self):
        base = self.depth
        self.begin(
            [
                send(self.acc.at[self.own_part()], self.from_x.at[d], self.sems, base + d, peer)
                for d, peer in enumerate(self.x_peers)
            ]
        )

    def finish_x(self):
        self.end()
        here = self.own_part()
        total = self.acc[here].astype(jnp.float32)
        for d in range(self.across - 1):
            total = total + self.from_x[d].astype(jnp.float32)
        self.acc[here] = total.astype(jnp.bfloat16)

    def start_z2(self):
        if not self.split:
            return
        base = self.depth + self.across - 1
        self.begin(
            [
                send(self.acc.at[self.own_part()], self.from_z2.at[d], self.sems, base + d, peer)
                for d, peer in enumerate(self.z_peers)
            ]
        )

    def finish_z2(self):
        if not self.split:
            return
        self.end()
        for d in range(self.depth - 1):
            self.acc[self.own_part(-(d + 1))] = self.from_z2[d]

    def start_core2(self):
        last = 2 * (self.depth - 1) + self.across
        self.begin([send(self.acc, self.other, self.sems, last, self.partner)])

    def finish_core2(self, out_ref):
        self.end()
        out_ref[:, :, self.lanes] = self.acc[...]
        out_ref[:, :, self.far_lanes] = self.other[...]


def segment(info, r, rows):
    begin = jnp.int32(0)
    for q in range(r):
        begin = begin + info[q]
    end = begin + info[r]
    first = info[16]
    low = jnp.clip(begin - first, 0, rows)
    high = jnp.clip(end - first, 0, rows)
    fresh = begin >= first
    ends = (end > first) & (end <= first + rows)
    return begin, low, high, fresh, ends


def front_stage(
    devices,
    info,
    taps_ref,
    conv_b_flat,
    dt_bias_flat,
    decay_flat,
    skip_flat,
    gain_flat,
    x_hbm,
    cache_hbm,
    cache_edge_hbm,
    x_proj_hbm,
    dt_proj_hbm,
    mixed_hbm,
    step_hbm,
    proj_ref,
    enter_ref,
    last_edge_ref,
    start_ref,
    param_ref,
    mixed_ref,
    step_ref,
    keep_sems,
    since_ref,
    x_ref,
    cache_ref,
    cache_edge_ref,
    x_proj_ref,
    dt_proj_ref,
    fetch_sems,
    ext,
    mixed_b,
    suffix,
    b_wide,
    halo_ref,
    edge3_ref,
    end_ref,
    sum_ref,
    halo_sems,
    pair_h,
    pair_s,
    own_h,
    own_s,
    z_h,
    z_s,
    x_h,
    x_s,
    half_out,
    half_in,
    pre_sems,
    *spread_refs,
):
    fetches = [
        pltpu.make_async_copy(src, dst, fetch_sems.at[i])
        for i, (src, dst) in enumerate(
            (
                (x_hbm, x_ref),
                (cache_edge_hbm, cache_edge_ref),
                (cache_hbm, cache_ref),
                (x_proj_hbm, x_proj_ref),
                (dt_proj_hbm, dt_proj_ref),
            )
        )
    ]
    for copy in fetches:
        copy.start()
    param_ref[pl.ds(0, 4), :] = taps_ref[...]
    for i, flat in enumerate((conv_b_flat, dt_bias_flat, decay_flat, skip_flat, gain_flat)):
        size = flat.shape[0]
        param_ref[pl.ds(4 + i, 1), pl.ds(0, size)] = flat[...].reshape(1, size)
    conv_w_ref = param_ref.at[pl.ds(0, 4)]
    conv_b_ref = param_ref.at[pl.ds(4, 1)]
    dt_bias_ref = param_ref.at[pl.ds(5, 1)]
    decay_ref = param_ref.at[pl.ds(6, 1)]
    rows, inner = x_ref.shape
    requests = start_ref.shape[0]
    me, core, z, x, partner, z_peers, x_peers = near_devices(devices)
    after, before = (me + 1) % devices, (me + devices - 1) % devices
    greet([("seq", p) for p in [partner, after, before] + z_peers + x_peers])
    halo_copy = send(x_ref.at[pl.ds(rows - 16, 16)], halo_ref, halo_sems, 0, after)
    fetches[0].wait()
    halo_copy.start()
    fetches[1].wait()
    per = len(Spread.scratch(devices, inner, 1, False))
    edge_sum = Spread(devices, inner, 1, False, spread_refs[:per])
    state_sum = Spread(devices, inner, requests, True, spread_refs[per:])
    spot = lax.broadcasted_iota(jnp.int32, (16, inner), 0)
    edge_rows = cache_edge_ref[...].astype(jnp.float32)
    placed = jnp.zeros((16, inner), jnp.float32)
    for r in range(requests):
        take = (info[8 + r] == me) & (info[4 + r] > 0)
        for j in range(EDGE):
            placed = jnp.where((spot == r * EDGE + j) & take, edge_rows[j : j + 1], placed)
    edge_sum.mine[0] = placed.astype(jnp.bfloat16)
    edge_sum.start_core()
    fetches[2].wait()
    for r in range(requests):
        take = (info[8 + r] == me) & (info[4 + r] > 0)
        state_sum.mine[r] = jnp.where(take, cache_ref[...], 0.0).astype(jnp.bfloat16)
    state_sum.start_core()
    ext[pl.ds(16, rows), :] = x_ref[...].astype(jnp.float32)
    fetches[3].wait()
    fetches[4].wait()
    edge_sum.finish_core()
    edge_sum.start_z()
    state_sum.finish_core()
    edge_sum.finish_z()
    edge_sum.start_x()
    state_sum.start_z()
    edge_sum.finish_x()
    edge_sum.start_core2()
    edge_sum.finish_core2(edge3_ref)
    edge_ref = edge3_ref.at[0]
    halo_copy.wait()
    width = col_block(inner)
    rank = dt_proj_ref.shape[0]
    ext[pl.ds(0, 16), :] = halo_ref[...].astype(jnp.float32)
    first_pos = info[16]
    position = first_pos + lax.broadcasted_iota(jnp.int32, (rows, LANES), 0)
    marks = [segment(info, r, rows) for r in range(requests)]
    begin = jnp.zeros((rows, LANES), jnp.int32)
    request = jnp.zeros((rows, LANES), jnp.int32)
    last_begin, last_req = jnp.int32(0), jnp.int32(0)
    for r in range(1, requests):
        reached = position >= marks[r][0]
        begin = jnp.where(reached, marks[r][0], begin)
        request = jnp.where(reached, r, request)
        inside = first_pos + rows - 1 >= marks[r][0]
        last_begin = jnp.where(inside, marks[r][0], last_begin)
        last_req = jnp.where(inside, r, last_req)
    offset = position - begin
    in_last = (position >= last_begin).astype(jnp.float32)
    edge_id = lax.broadcasted_iota(jnp.int32, (rows, 16), 1)
    hots = []
    for lag in (1, 2, 3):
        want = request * EDGE + EDGE + offset - lag
        hit = (edge_id == want[:, :16]) & (offset[:, :16] < lag)
        hots.append(hit.astype(jnp.float32).astype(jnp.bfloat16))

    keep = {}
    for lag in (1, 2, 3):
        keep[lag] = jnp.concatenate([offset] * (width // LANES), axis=1) >= lag
    for first in range(0, inner, width):
        cols = pl.ds(first, width)
        edges = edge_ref[:, cols]
        total = conv_b_ref[:, cols] + conv_w_ref[pl.ds(3, 1), cols] * ext[pl.ds(16, rows), cols]
        for lag in (1, 2, 3):
            near = ext[pl.ds(16 - lag, rows), cols]
            far = jnp.dot(hots[lag - 1], edges, preferred_element_type=jnp.float32)
            row = jnp.where(keep[lag], near, far)
            total = total + conv_w_ref[pl.ds(3 - lag, 1), cols] * row
        mixed = (total / (1.0 + jnp.exp(-total))).astype(jnp.bfloat16)
        mixed_b[:, cols] = mixed
        mixed_ref[:, cols] = mixed.astype(jnp.float32)

    state_sum.finish_z()
    state_sum.start_x()
    keep_mixed = pltpu.make_async_copy(mixed_ref, mixed_hbm, keep_sems.at[0])
    keep_mixed.start()
    proj = lax.dot_general(
        mixed_b[...],
        x_proj_ref[...],
        (((1,), (1,)), ((), ())),
        preferred_element_type=jnp.float32,
    )
    proj_ref[...] = proj
    for s in range(STATE):
        b_wide[s] = jnp.broadcast_to(proj[:, rank + s : rank + s + 1], (rows, LANES))
    dt_low = proj[:, :rank].astype(jnp.bfloat16)
    row_id = lax.broadcasted_iota(jnp.int32, (rows, rows), 0)
    col_id = lax.broadcasted_iota(jnp.int32, (rows, rows), 1)
    later = (col_id > row_id).astype(jnp.bfloat16)
    for first in range(0, inner, width):
        cols = pl.ds(first, width)
        v = jnp.dot(dt_low, dt_proj_ref[:, cols], preferred_element_type=jnp.float32)
        v = v + dt_bias_ref[:, cols]
        step = jnp.maximum(v, 0.0) + jnp.log1p(jnp.exp(-jnp.abs(v)))
        step_ref[:, cols] = step
        high = step.astype(jnp.bfloat16)
        rest = step - high.astype(jnp.float32)
        mid = rest.astype(jnp.bfloat16)
        low = (rest - mid.astype(jnp.float32)).astype(jnp.bfloat16)
        after = (
            jnp.dot(later, high, preferred_element_type=jnp.float32)
            + jnp.dot(later, mid, preferred_element_type=jnp.float32)
            + jnp.dot(later, low, preferred_element_type=jnp.float32)
        )
        suffix[:, cols] = after

    keep_step = pltpu.make_async_copy(step_ref, step_hbm, keep_sems.at[1])
    keep_step.start()
    state_sum.finish_x()
    state_sum.start_z2()
    starts_here = (last_begin >= first_pos).astype(jnp.int32)
    flag = jnp.full((1, LANES), starts_here, jnp.int32).astype(jnp.float32)
    power = (lax.broadcasted_iota(jnp.int32, (STATE, LANES), 0) + 1).astype(jnp.float32)

    def one_tile(j, carry):
        cols = pl.ds(pl.multiple_of(j * LANES, LANES), LANES)
        rate = decay_ref[:, cols]
        acc = [jnp.zeros((8, LANES), jnp.float32) for _ in range(STATE)]
        since = jnp.zeros((8, LANES), jnp.float32)
        for tile in range(rows // 8):
            here = pl.ds(tile * 8, 8)
            fade = jnp.exp(-rate * suffix[here, cols])
            step = step_ref[here, cols] * in_last[tile * 8 : tile * 8 + 8]
            since = since + step
            push = step * mixed_ref[here, cols]
            for s in range(STATE):
                push = push * fade
                acc[s] = acc[s] + push * b_wide[s, here, :]
        ends = jnp.concatenate([jnp.sum(a, axis=0, keepdims=True) for a in acc], axis=0)
        end_ref[:, cols] = ends
        since = jnp.sum(since, axis=0, keepdims=True)
        since_ref[:, cols] = since
        sum_ref[:, cols] = jnp.where(flag > 0.5, FAR, since)
        return carry

    def one_seed(j, carry):
        cols = pl.ds(pl.multiple_of(j * LANES, LANES), LANES)
        rate = decay_ref[:, cols]
        since = since_ref[:, cols]
        seed = jnp.exp(-(rate * since) * power) * start_ref[last_req, :, cols].astype(jnp.float32)
        end_ref[:, cols] = end_ref[:, cols] + flag * seed
        return carry

    lax.fori_loop(0, inner // LANES, one_tile, 0)
    state_sum.finish_z2()
    state_sum.start_core2()
    state_sum.finish_core2(start_ref)
    lax.fori_loop(0, inner // LANES, one_seed, 0)
    power16 = (lax.broadcasted_iota(jnp.int32, (STATE, LANES), 0) + 1).astype(jnp.float32)
    half = half_width(inner)
    tiles = half // LANES
    base = core * (inner - half)
    own_h[...] = end_ref[...].astype(jnp.bfloat16)
    for j in range(inner // LANES):
        own_s[pl.ds(j, 1), :] = sum_ref[:, pl.ds(j * LANES, LANES)]
    pair = [
        send(own_h, pair_h, pre_sems, 0, partner),
        send(own_s, pair_s, pre_sems, 1, partner),
    ]
    for copy in pair:
        copy.start()
    across, depth = layout_of(devices)
    first_core = core == 0

    def lane(j):
        return pl.ds(pl.multiple_of(base + j * LANES, LANES), LANES)

    def f32(value):
        return value.astype(jnp.float32)

    for copy in pair:
        copy.wait()
    z_sum = []
    for j in range(tiles):
        rate = decay_ref[:, lane(j)] * power16
        mine, theirs = own_h[:, lane(j)], pair_h[:, lane(j)]
        shift = (inner - half) // LANES
        s_mine = jnp.where(first_core, own_s[j : j + 1], own_s[j + shift : j + shift + 1])
        s_pair = jnp.where(first_core, pair_s[j : j + 1], pair_s[j + shift : j + shift + 1])
        h0 = f32(jnp.where(first_core, f32(mine), f32(theirs)))
        h1 = f32(jnp.where(first_core, f32(theirs), f32(mine)))
        s1 = jnp.where(first_core, s_pair, s_mine)
        z_h[0, :, pl.ds(j * LANES, LANES)] = (jnp.exp(-rate * s1) * h0 + h1).astype(jnp.bfloat16)
        z_s[0, pl.ds(j, 1), :] = s_mine + s_pair
    copies = []
    for d, peer in enumerate(z_peers):
        copies.append(send(z_h.at[0], z_h.at[d + 1], pre_sems, 2 + 2 * d, peer))
        copies.append(send(z_s.at[0], z_s.at[d + 1], pre_sems, 3 + 2 * d, peer))
    for copy in copies:
        copy.start()
    for copy in copies:
        copy.wait()
    prefix = []
    for j in range(tiles):
        cols = pl.ds(j * LANES, LANES)
        rate = decay_ref[:, lane(j)] * power16
        total = jnp.zeros((STATE, LANES), jnp.float32)
        part = jnp.zeros((STATE, LANES), jnp.float32)
        total_s = jnp.zeros((1, LANES), jnp.float32)
        part_s = jnp.zeros((1, LANES), jnp.float32)
        for k in range(depth):
            slot = (z - k + depth) % depth
            s_k = z_s[slot, pl.ds(j, 1), :]
            h_k = f32(z_h[slot, :, cols])
            fade = jnp.exp(-rate * s_k)
            total = fade * total + h_k
            part = jnp.where(k < z, fade * part + h_k, part)
            total_s = total_s + s_k
            part_s = jnp.where(k < z, part_s + s_k, part_s)
        x_h[0, :, cols] = total.astype(jnp.bfloat16)
        x_s[0, pl.ds(j, 1), :] = total_s
        prefix.append((part, part_s))
    copies = []
    first = 2 + 2 * (depth - 1)
    for d, peer in enumerate(x_peers):
        copies.append(send(x_h.at[0], x_h.at[d + 1], pre_sems, first + 2 * d, peer))
        copies.append(send(x_s.at[0], x_s.at[d + 1], pre_sems, first + 1 + 2 * d, peer))
    for copy in copies:
        copy.start()
    for copy in copies:
        copy.wait()
    for j in range(tiles):
        cols = pl.ds(j * LANES, LANES)
        rate = decay_ref[:, lane(j)] * power16
        part = jnp.zeros((STATE, LANES), jnp.float32)
        for k in range(across):
            slot = (x - k + across) % across
            value = jnp.exp(-rate * x_s[slot, pl.ds(j, 1), :]) * part + f32(x_h[slot, :, cols])
            part = jnp.where(k < x, value, part)
        inner_part, inner_s = prefix[j]
        half_out[:, cols] = jnp.exp(-rate * inner_s) * part + inner_part
    last = first + 2 * (across - 1)
    swap = send(half_out, half_in, pre_sems, last, partner)
    swap.start()
    swap.wait()
    enter_ref[:, my_lanes(core, inner)] = half_out[...]
    enter_ref[:, my_lanes(1 - core, inner)] = half_in[...]
    for j in range(inner // LANES):
        cols = pl.ds(j * LANES, LANES)
        rate = decay_ref[:, cols] * power16
        chip = enter_ref[:, cols]
        second = jnp.exp(-rate * pair_s[j : j + 1]) * chip + f32(pair_h[:, cols])
        enter_ref[:, cols] = jnp.where(first_core, chip, second)

    row_of = lax.broadcasted_iota(jnp.int32, (16, LANES), 0)
    from_of = lax.broadcasted_iota(jnp.int32, (16, LANES), 1)
    near_at = jnp.full((16, LANES), -1, jnp.int32)
    far_at = jnp.full((16, LANES), -1, jnp.int32)
    for r in range(requests):
        _, _, high, _, ends = marks[r]
        size = info[r]
        for j in range(EDGE):
            lag = EDGE - 1 - j
            near = jnp.where(ends & (size > lag), high + 15 - lag, -1)
            far = jnp.where(ends & (size <= lag), r * EDGE + EDGE + size - 1 - lag, -1)
            near_at = jnp.where(row_of == r * EDGE + j, near, near_at)
            far_at = jnp.where(row_of == r * EDGE + j, far, far_at)

    def hot_rows(at, count):
        return (from_of[:, :count] == at[:, :count]).astype(jnp.float32).astype(jnp.bfloat16)

    for first in range(0, inner, width):
        cols = pl.ds(first, width)
        last_edge_ref[:, cols] = (
            jnp.dot(hot_rows(near_at - 16, rows), x_ref[:, cols], preferred_element_type=jnp.float32)
            + jnp.dot(hot_rows(near_at, 16), halo_ref[:, cols], preferred_element_type=jnp.float32)
            + jnp.dot(hot_rows(far_at, 16), edge_ref[:, cols], preferred_element_type=jnp.float32)
        )
    keep_mixed.wait()
    keep_step.wait()


def front_call(devices, info, args, rows, inner, proj_width, requests):
    f32, bf16 = jnp.float32, jnp.bfloat16
    across, depth = layout_of(devices)
    half = half_width(inner)
    s_rows = -(-(inner // LANES) // 8) * 8
    return pl.pallas_call(
        functools.partial(front_stage, devices),
        out_shape=(
            jax.ShapeDtypeStruct((rows, inner), f32),
            jax.ShapeDtypeStruct((rows, inner), f32),
            jax.ShapeDtypeStruct((rows, proj_width), f32),
            jax.ShapeDtypeStruct((STATE, inner), f32),
            jax.ShapeDtypeStruct((16, inner), f32),
            jax.ShapeDtypeStruct((requests, STATE, inner), bf16),
            jax.ShapeDtypeStruct((16, inner), f32),
        ),
        in_specs=[sspec()] + [vspec()] * 6 + [hspec()] * (len(args) - 6),
        out_specs=tuple([hspec()] * 2 + [vspec()] * 5),
        scratch_shapes=[
            VMEM((rows, inner), f32),
            VMEM((rows, inner), f32),
            pltpu.SemaphoreType.DMA((2,)),
            VMEM((1, inner), f32),
            VMEM((rows, inner), bf16),
            VMEM((STATE, inner), f32),
            VMEM((EDGE, inner), bf16),
            VMEM((proj_width, inner), bf16),
            VMEM((proj_width - 2 * STATE, inner), bf16),
            pltpu.SemaphoreType.DMA((5,)),
            VMEM((rows + 16, inner), f32),
            VMEM((rows, inner), bf16),
            VMEM((rows, inner), f32),
            VMEM((STATE, rows, LANES), f32),
            VMEM((16, inner), bf16),
            VMEM((1, 16, inner), bf16),
            VMEM((STATE, inner), f32),
            VMEM((1, inner), f32),
            pltpu.SemaphoreType.DMA((2, 1)),
            VMEM((STATE, inner), bf16),
            VMEM((s_rows, LANES), f32),
            VMEM((STATE, inner), bf16),
            VMEM((s_rows, LANES), f32),
            VMEM((depth, STATE, half), bf16),
            VMEM((depth, 16, LANES), f32),
            VMEM((across, STATE, half), bf16),
            VMEM((across, 16, LANES), f32),
            VMEM((STATE, half), f32),
            VMEM((STATE, half), f32),
            pltpu.SemaphoreType.DMA((2, 3 + 2 * (depth + across - 2))),
        ]
        + Spread.scratch(devices, inner, 1, False)
        + Spread.scratch(devices, inner, requests, True),
        compiler_params=pltpu.CompilerParams(
            vmem_limit_bytes=61 << 20, collective_id=0, has_side_effects=True
        ),
        cost_estimate=pl.CostEstimate(
            flops=400_000_000, bytes_accessed=8_000_000, transcendentals=2_000_000
        ),
        name="front_stage",
    )(info, *args)


def scan_stage(
    info,
    mixed_hbm,
    step_hbm,
    proj_ref,
    enter_ref,
    start_ref,
    param_ref,
    hidden_hbm,
    out_w_hbm,
    middle_ref,
    normed_ref,
    final_hbm,
    mixed_ref,
    step_ref,
    final_ref,
    block_sems,
    final_sem,
    bc_wide,
    y_ref,
    ssm_b,
    out_w,
    hidden_ref,
    w_sem,
    hidden_sem,
):
    rows, inner = mixed_ref.shape
    width = col_block(inner)
    tiles = width // LANES
    rank = proj_ref.shape[1] - 2 * STATE
    width = col_block(step_ref.shape[1])

    def block_copies(g):
        cols = pl.ds(pl.multiple_of(g * width, LANES), width)
        return (
            pltpu.make_async_copy(
                mixed_hbm.at[:, cols], mixed_ref.at[:, cols], block_sems.at[0, g]
            ),
            pltpu.make_async_copy(step_hbm.at[:, cols], step_ref.at[:, cols], block_sems.at[1, g]),
        )

    for g in range(step_ref.shape[1] // width):
        for copy in block_copies(g):
            copy.start()
    fetch = pltpu.make_async_copy(out_w_hbm, out_w, w_sem)
    fetch.start()
    fetch_hidden = pltpu.make_async_copy(hidden_hbm, hidden_ref, hidden_sem)
    fetch_hidden.start()
    model = hidden_ref.shape[0]
    decay_ref = param_ref.at[pl.ds(6, 1)]
    skip_ref = param_ref.at[pl.ds(7, 1)]

    turned = jnp.transpose(proj_ref[:, rank : rank + 2 * STATE])
    for t in range(rows):
        bc_wide[t] = jnp.broadcast_to(turned[:, t : t + 1], (2 * STATE, LANES))
    final_ref[...] = jnp.zeros_like(final_ref)
    power = (lax.broadcasted_iota(jnp.int32, (8, LANES), 0) + 1).astype(jnp.float32)

    def wide_step(t, i, step, push, fade8, state, rates):
        b_low, b_high = bc_wide[t, 0:8], bc_wide[t, 8:16]
        c_low, c_high = bc_wide[t, 16:24], bc_wide[t, 24:32]
        outs, new = [], []
        for j in range(tiles):
            s_row, p_row, f_row = (
                jnp.broadcast_to(part[j][i : i + 1], (8, LANES)) for part in (step, push, fade8)
            )
            d_low = jnp.exp(s_row * rates[j])
            d_high = d_low * f_row
            low = d_low * state[2 * j] + b_low * p_row
            high = d_high * state[2 * j + 1] + b_high * p_row
            new += [low, high]
            outs.append(jnp.sum(c_low * low + c_high * high, axis=0, keepdims=True))
        return outs, tuple(new)

    def one_block(g, carry):
        for copy in block_copies(g):
            copy.wait()
        base = pl.multiple_of(g * width, LANES)
        tile_cols = [pl.ds(pl.multiple_of(base + j * LANES, LANES), LANES) for j in range(tiles)]
        rates = [-decay_ref[:, c] * power for c in tile_cols]
        decays = [decay_ref[:, c] for c in tile_cols]

        def load(row, count):
            step = [step_ref[pl.ds(row, count), c] for c in tile_cols]
            push = [s * mixed_ref[pl.ds(row, count), c] for s, c in zip(step, tile_cols)]
            fade8 = [jnp.exp(-8.0 * (s * d)) for s, d in zip(step, decays)]
            return step, push, fade8

        def eight(block, state, limits=None):
            row = pl.multiple_of(block * 8, 8)
            step, push, fade8 = load(row, 8)
            kept = [[] for _ in range(tiles)]
            for i in range(8):
                outs, new = wide_step(row + i, i, step, push, fade8, state, rates)
                if limits is not None:
                    active = (row + i >= limits[0]) & (row + i < limits[1])
                    new = tuple(jnp.where(active, a, b) for a, b in zip(new, state))
                state = new
                for j in range(tiles):
                    kept[j].append(outs[j])
            for j in range(tiles):
                y = jnp.concatenate(kept[j], axis=0)
                if limits is not None:
                    at = row + lax.broadcasted_iota(jnp.int32, (8, LANES), 0)
                    y = jnp.where(
                        (at >= limits[0]) & (at < limits[1]), y, y_ref[pl.ds(row, 8), tile_cols[j]]
                    )
                y_ref[pl.ds(row, 8), tile_cols[j]] = y
            return state

        for r in range(final_ref.shape[0]):
            _, begin, end, new, ends = segment(info, r, rows)

            @pl.when(end > begin)
            def _():
                state = []
                for c in tile_cols:
                    for half in (pl.ds(0, 8), pl.ds(8, 8)):
                        old = enter_ref[half, c]
                        seed = start_ref[r, half, c].astype(jnp.float32)
                        state.append(jnp.where(new, seed, old))
                state = tuple(state)
                part = functools.partial(eight, limits=(begin, end))
                low, low_up, high = begin // 8, (begin + 7) // 8, end // 8
                state = lax.fori_loop(low, low_up, part, state)
                state = lax.fori_loop(low_up, jnp.maximum(high, low_up), eight, state)
                tail = jnp.where((high >= low_up) & (end % 8 > 0), high + 1, high)
                state = lax.fori_loop(high, tail, part, state)

                @pl.when(ends)
                def _():
                    for j, c in enumerate(tile_cols):
                        final_ref[r, pl.ds(0, 8), c] = state[2 * j]
                        final_ref[r, pl.ds(8, 8), c] = state[2 * j + 1]

        y = y_ref[:, pl.ds(base, width)]
        y = y + skip_ref[:, pl.ds(base, width)] * mixed_ref[:, pl.ds(base, width)]
        ssm_b[:, pl.ds(base, width)] = y.astype(jnp.bfloat16)
        return carry

    lax.fori_loop(0, inner // width, one_block, 0)
    keep_final = pltpu.make_async_copy(final_ref, final_hbm, final_sem)
    keep_final.start()
    fetch.wait()
    fetch_hidden.wait()
    middle = jnp.transpose(hidden_ref[...].astype(jnp.float32))
    for first in range(0, inner, width):
        middle = middle + lax.dot_general(
            ssm_b[:, first : first + width],
            out_w[:, first : first + width],
            (((1,), (1,)), ((), ())),
            preferred_element_type=jnp.float32,
        )
    middle_ref[...] = middle
    scale = lax.rsqrt(jnp.mean(middle * middle, axis=1, keepdims=True) + NORM_EPS)
    normed_ref[...] = (middle * scale * param_ref[8:9, :model]).astype(jnp.bfloat16)
    keep_final.wait()


def scan_call(info, args, out_w, rows, inner, model, requests):
    f32 = jnp.float32
    return pl.pallas_call(
        scan_stage,
        out_shape=(
            jax.ShapeDtypeStruct((rows, model), f32),
            jax.ShapeDtypeStruct((rows, model), jnp.bfloat16),
            jax.ShapeDtypeStruct((requests, STATE, inner), f32),
        ),
        in_specs=[sspec()] + [hspec()] * 2 + [vspec()] * (len(args) - 3) + [hspec()] * 2,
        out_specs=tuple([vspec()] * 2 + [hspec()]),
        scratch_shapes=[
            VMEM((rows, inner), f32),
            VMEM((rows, inner), f32),
            VMEM((requests, STATE, inner), f32),
            pltpu.SemaphoreType.DMA((2, inner // col_block(inner))),
            pltpu.SemaphoreType.DMA,
            VMEM((rows, 2 * STATE, LANES), f32),
            VMEM((rows, inner), f32),
            VMEM((rows, inner), jnp.bfloat16),
            VMEM((model, inner), jnp.bfloat16),
            VMEM((model, rows), jnp.bfloat16),
            pltpu.SemaphoreType.DMA,
            pltpu.SemaphoreType.DMA,
        ],
        compiler_params=pltpu.CompilerParams(vmem_limit_bytes=61 << 20),
        cost_estimate=pl.CostEstimate(
            flops=1_400_000_000, bytes_accessed=18_000_000, transcendentals=4_000_000
        ),
        name="scan_stage",
    )(info, *args, out_w)


def mlp_stage(
    devices,
    info,
    normed_hbm,
    middle_hbm,
    final_hbm,
    last_edge_hbm,
    gate_hbm,
    up_hbm,
    down_hbm,
    out_ref,
    new_state_ref,
    new_edge_ref,
    normed_ref,
    middle_ref,
    final_ref,
    last_edge_ref,
    gate_w,
    up_w,
    down_w,
    fetch_sems,
    near1,
    near2,
    far,
    out1,
    out2,
    far_out,
    own_out,
    low_in,
    high_in,
    far_in,
    ring_sems,
    full,
    full_edge,
    *spread_refs,
):
    rows, model = normed_ref.shape
    half = rows // 2
    inner = final_ref.shape[2]
    requests = final_ref.shape[0]
    me, _, _, _, partner, z_peers, x_peers = near_devices(devices)
    ring = lax.axis_size("req")
    here = lax.axis_index("req")
    above, below = (here + 1) % ring, (here + ring - 1) % ring
    fetches = [
        pltpu.make_async_copy(src, dst, fetch_sems.at[i])
        for i, (src, dst) in enumerate(
            (
                (normed_hbm, normed_ref),
                (final_hbm, final_ref),
                (last_edge_hbm, last_edge_ref),
                (gate_hbm, gate_w),
                (up_hbm, up_w),
                (down_hbm, down_w),
                (middle_hbm, middle_ref),
            )
        )
    ]
    for copy in fetches:
        copy.start()
    greet(
        [("req", above), ("req", below)] + [("seq", p) for p in [partner] + z_peers + x_peers]
    )

    def hop(src, dst, index, peer):
        return pltpu.make_async_remote_copy(
            src_ref=src,
            dst_ref=dst,
            send_sem=ring_sems.at[0, index],
            recv_sem=ring_sems.at[1, index],
            device_id={"req": peer},
            device_id_type=MESH_ID,
        )

    first, second = pl.ds(0, half), pl.ds(half, half)
    up_a = hop(normed_ref.at[first], near1.at[first], 0, above)
    down_b = hop(normed_ref.at[second], near1.at[second], 1, below)
    up_a2 = hop(near1.at[first], far.at[first], 2, above)
    down_b2 = hop(near1.at[second], far.at[second], 3, below)
    up_b = hop(normed_ref.at[second], near2.at[first], 4, above)
    down_a = hop(normed_ref.at[first], near2.at[second], 5, below)
    far_up = hop(far_out.at[first], far_in.at[first], 6, above)
    far_down = hop(far_out.at[second], far_in.at[second], 7, below)
    back_down = hop(out1.at[first], high_in.at[first], 8, below)
    back_up = hop(out1.at[second], low_in.at[second], 9, above)
    last_down = hop(out2.at[first], high_in.at[second], 10, below)
    last_up = hop(out2.at[second], low_in.at[first], 11, above)
    fetches[0].wait()
    up_a.start()
    down_b.start()
    per = len(Spread.scratch(devices, inner, 1, False))
    finals = Spread(devices, inner, requests, True, spread_refs[:per])
    edges = Spread(devices, inner, 1, False, spread_refs[per:])
    fetches[1].wait()
    for r in range(requests):
        finals.mine[r] = final_ref[r].astype(jnp.bfloat16)
    finals.start_core()
    fetches[2].wait()
    edges.mine[0] = last_edge_ref[...].astype(jnp.bfloat16)
    edges.start_core()

    def hidden_units(value):
        gate = jnp.dot(value, gate_w[...], preferred_element_type=jnp.float32)
        up = jnp.dot(value, up_w[...], preferred_element_type=jnp.float32)
        hidden = (gate / (1.0 + jnp.exp(-gate)) * up).astype(jnp.bfloat16)
        return lax.dot_general(
            hidden, down_w[...], (((1,), (1,)), ((), ())), preferred_element_type=jnp.float32
        )

    finals.finish_core()
    finals.start_z()
    edges.finish_core()
    up_a.wait_recv()
    up_a2.start()
    down_b.wait_recv()
    down_b2.start()
    for copy in fetches[3:]:
        copy.wait()
    out1[...] = hidden_units(near1[...]).astype(jnp.bfloat16)
    up_b.start()
    down_a.start()
    up_a2.wait_recv()
    down_b2.wait_recv()
    far_out[...] = hidden_units(far[...]).astype(jnp.bfloat16)
    far_up.start()
    far_down.start()
    finals.finish_z()
    finals.start_x()
    edges.start_z()
    up_b.wait_recv()
    down_a.wait_recv()
    own_out[...] = hidden_units(near2[...])
    back_down.start()
    back_up.start()
    far_down.wait_recv()
    out2[first] = (own_out[first] + far_in[second].astype(jnp.float32)).astype(jnp.bfloat16)
    last_down.start()
    far_up.wait_recv()
    out2[second] = (own_out[second] + far_in[first].astype(jnp.float32)).astype(jnp.bfloat16)
    last_up.start()
    finals.finish_x()
    finals.start_z2()
    edges.finish_z()
    edges.start_x()
    own_out[...] = hidden_units(normed_ref[...]) + middle_ref[...]
    finals.finish_z2()
    finals.start_core2()
    edges.finish_x()
    edges.start_core2()
    finals.finish_core2(full)
    state = jnp.zeros((STATE, inner), jnp.float32)
    for r in range(requests):
        state = jnp.where(info[12 + r] == me, full[r].astype(jnp.float32), state)
    new_state_ref[...] = state
    edges.finish_core2(full_edge)
    gathered = full_edge[0].astype(jnp.float32)
    edge = jnp.zeros((EDGE, inner), jnp.float32)
    for r in range(requests):
        owned = info[12 + r] == me
        edge = jnp.where(owned, gathered[r * EDGE : (r + 1) * EDGE], edge)
    new_edge_ref[...] = edge.astype(jnp.bfloat16)
    back_down.wait_recv()
    back_up.wait_recv()
    last_up.wait_recv()
    last_down.wait_recv()
    total = own_out[...] + low_in[...].astype(jnp.float32) + high_in[...].astype(jnp.float32)
    out_ref[...] = jnp.transpose(total).astype(jnp.bfloat16)
    for copy in (
        up_a, down_b, up_a2, down_b2, up_b, down_a,
        far_up, far_down, back_down, back_up, last_up, last_down,
    ):
        copy.wait_send()


def mlp_call(devices, info, args, weights, rows, model, inner, requests):
    f32, bf16 = jnp.float32, jnp.bfloat16
    hidden = weights[0].shape[1]
    return pl.pallas_call(
        functools.partial(mlp_stage, devices),
        out_shape=(
            jax.ShapeDtypeStruct((model, rows), bf16),
            jax.ShapeDtypeStruct((STATE, inner), f32),
            jax.ShapeDtypeStruct((EDGE, inner), bf16),
        ),
        in_specs=[sspec()] + [hspec()] * (len(args) + len(weights)),
        out_specs=tuple([vspec()] * 3),
        scratch_shapes=[
            VMEM((rows, model), bf16),
            VMEM((rows, model), f32),
            VMEM((requests, STATE, inner), f32),
            VMEM((16, inner), f32),
            VMEM((model, hidden), bf16),
            VMEM((model, hidden), bf16),
            VMEM((model, hidden), bf16),
            pltpu.SemaphoreType.DMA((7,)),
            VMEM((rows, model), bf16),
            VMEM((rows, model), bf16),
            VMEM((rows, model), bf16),
            VMEM((rows, model), bf16),
            VMEM((rows, model), bf16),
            VMEM((rows, model), bf16),
            VMEM((rows, model), f32),
            VMEM((rows, model), bf16),
            VMEM((rows, model), bf16),
            VMEM((rows, model), bf16),
            pltpu.SemaphoreType.DMA((2, 12)),
            VMEM((requests, 16, inner), bf16),
            VMEM((1, 16, inner), bf16),
        ]
        + Spread.scratch(devices, inner, requests, True)
        + Spread.scratch(devices, inner, 1, False),
        compiler_params=pltpu.CompilerParams(
            vmem_limit_bytes=61 << 20, collective_id=1, has_side_effects=True
        ),
        cost_estimate=pl.CostEstimate(
            flops=7_000_000_000, bytes_accessed=16_000_000, transcendentals=1_000_000
        ),
        name="mlp_stage",
    )(info, *args, *weights)


def handing_stage(*refs):
    count = len(refs) // 2
    for i in range(count):
        refs[count + i][...] = refs[i][...]


def handed(*arrays):
    return pl.pallas_call(
        handing_stage,
        out_shape=tuple(jax.ShapeDtypeStruct(a.shape, a.dtype) for a in arrays),
        in_specs=[vspec()] * len(arrays),
        out_specs=tuple([vspec()] * len(arrays)),
        name="handing_stage",
    )(*arrays)


def shards(
    hidden_in,
    mamba_in,
    conv_weight,
    conv_bias,
    x_proj,
    dt_proj,
    dt_bias,
    decay_rate,
    skip_gain,
    out_proj,
    norm_gain,
    mlp_gate,
    mlp_up,
    mlp_down,
    cache_state,
    cache_edge,
    req_lengths,
    cont_flag,
    cache_source,
    owner_slot,
):
    rows, inner = mamba_in.shape[1:]
    model = hidden_in.shape[2]
    requests = req_lengths.shape[1]
    devices = lax.axis_size("seq")
    place = lax.axis_index("seq")
    info = jnp.concatenate(
        [
            req_lengths[0],
            cont_flag[0],
            cache_source[0],
            owner_slot[0],
            jnp.reshape(place * rows, (1,)).astype(jnp.int32),
        ]
    )
    mixed, step, proj, enter, last_edge, start_state, params = front_call(
        devices,
        info,
        (
            conv_weight,
            conv_bias,
            dt_bias,
            decay_rate,
            skip_gain,
            norm_gain,
            mamba_in[0],
            cache_state[0, 0],
            cache_edge[0, 0],
            x_proj.T,
            dt_proj,
        ),
        rows,
        inner,
        x_proj.shape[1],
        requests,
    )
    middle, normed, finals = scan_call(
        info,
        (mixed, step, proj, enter, start_state, params, hidden_in[0].T),
        out_proj.T,
        rows,
        inner,
        model,
        requests,
    )
    block_out, new_state, new_edge = handed(
        *mlp_call(
            devices,
            info,
            (normed, middle, finals, last_edge),
            (mlp_gate, mlp_up, mlp_down.T),
            rows,
            model,
            inner,
            requests,
        )
    )
    return block_out.T[None], new_state[None, None], new_edge[None, None]


def solution(mesh):
    grouped = P("req", "seq", None)
    slots = P("req", "seq", None, None)
    return jax.shard_map(
        shards,
        mesh=mesh,
        in_specs=(grouped, grouped)
        + (P(),) * 9
        + (P(None, "req"), P(None, "req"), P("req", None), slots, slots)
        + (P("req", None),) * 4,
        out_specs=(grouped, slots, slots),
        check_vma=False,
    )
```

```python
import functools

import jax
import jax.numpy as jnp
from jax import lax
from jax.experimental import pallas as pl
from jax.experimental.pallas import tpu as pltpu
from jax.sharding import PartitionSpec as P

STATE = 16
EDGE = 3
NORM_EPS = 1e-06
LANES = 128
FAR = 1e30
HIGHEST_PREC = lax.Precision.HIGHEST
VMEM = pltpu.VMEM
SMEM = pltpu.SMEM


def vspec():
    return pl.BlockSpec(memory_space=VMEM)


def hspec():
    return pl.BlockSpec(memory_space=pltpu.HBM)


def sspec():
    return pl.BlockSpec(memory_space=SMEM)


def col_block(width):
    return 640 if width % 640 == 0 else LANES


MESH_ID = pl.DeviceIdType.MESH


def layout_of(devices):
    depth = 4 if devices >= 32 else 2
    return devices // (2 * depth), depth


def padded(width):
    return -(-width // LANES) * LANES


def half_width(inner):
    return -(-inner // (2 * LANES)) * LANES


def near_devices(devices):
    across, depth = layout_of(devices)
    me = lax.axis_index("seq")
    core, z, x = me % 2, (me // 2) % depth, me // (2 * depth)
    partner = me + 1 - 2 * core
    z_peers = [x * 2 * depth + ((z + d) % depth) * 2 + core for d in range(1, depth)]
    x_peers = [((x + d) % across) * 2 * depth + z * 2 + core for d in range(1, across)]
    return me, core, z, x, partner, z_peers, x_peers


def my_lanes(core, inner):
    half = half_width(inner)
    return pl.ds(pl.multiple_of(core * (inner - half), LANES), half)


def send(src, dst, sems, index, peer):
    return pltpu.make_async_remote_copy(
        src_ref=src,
        dst_ref=dst,
        send_sem=sems.at[0, index],
        recv_sem=sems.at[1, index],
        device_id={"seq": peer},
        device_id_type=MESH_ID,
    )


def greet(axis_peers):
    barrier = pltpu.get_barrier_semaphore()
    for axis, peer in axis_peers:
        pl.semaphore_signal(barrier, inc=1, device_id={axis: peer}, device_id_type=MESH_ID)
    pl.semaphore_wait(barrier, len(axis_peers))


class Spread:
    def __init__(self, devices, inner, count, split, refs):
        self.devices, self.inner, self.count, self.split = devices, inner, count, split
        self.across, self.depth = layout_of(devices)
        self.part = count // self.depth if split else count
        (
            self.mine,
            self.from_core,
            self.acc,
            self.from_z,
            self.from_x,
            self.from_z2,
            self.other,
            self.sems,
        ) = refs
        _, self.core, self.z, self.x, self.partner, self.z_peers, self.x_peers = near_devices(
            devices
        )
        self.lanes = my_lanes(self.core, inner)
        self.far_lanes = my_lanes(1 - self.core, inner)
        self.copies = []

    @staticmethod
    def scratch(devices, inner, count, split):
        across, depth = layout_of(devices)
        part = count // depth if split else count
        half = half_width(inner)
        b = jnp.bfloat16
        return [
            VMEM((count, 16, inner), b),
            VMEM((count, 16, half), b),
            VMEM((count, 16, half), b),
            VMEM((depth - 1, part, 16, half), b),
            VMEM((across - 1, part, 16, half), b),
            VMEM((depth - 1, part, 16, half), b),
            VMEM((count, 16, half), b),
            pltpu.SemaphoreType.DMA((2, 2 + 2 * (depth - 1) + (across - 1))),
        ]

    def own_part(self, shift=0):
        if not self.split:
            return pl.ds(0, self.part)
        return pl.ds(((self.z + shift) % self.depth) * self.part, self.part)

    def begin(self, copies):
        self.copies = copies
        for copy in copies:
            copy.start()

    def end(self):
        for copy in self.copies:
            copy.wait()

    def start_core(self):
        self.begin(
            [send(self.mine.at[:, :, self.far_lanes], self.from_core, self.sems, 0, self.partner)]
        )

    def finish_core(self):
        self.end()
        total = self.mine[:, :, self.lanes].astype(jnp.float32) + self.from_core[...].astype(
            jnp.float32
        )
        self.acc[...] = total.astype(jnp.bfloat16)

    def start_z(self):
        self.begin(
            [
                send(self.acc.at[self.own_part(d + 1)], self.from_z.at[d], self.sems, 1 + d, peer)
                for d, peer in enumerate(self.z_peers)
            ]
        )

    def finish_z(self):
        self.end()
        here = self.own_part()
        total = self.acc[here].astype(jnp.float32)
        for d in range(self.depth - 1):
            total = total + self.from_z[d].astype(jnp.float32)
        self.acc[here] = total.astype(jnp.bfloat16)

    def start_x(self):
        base = self.depth
        self.begin(
            [
                send(self.acc.at[self.own_part()], self.from_x.at[d], self.sems, base + d, peer)
                for d, peer in enumerate(self.x_peers)
            ]
        )

    def finish_x(self):
        self.end()
        here = self.own_part()
        total = self.acc[here].astype(jnp.float32)
        for d in range(self.across - 1):
            total = total + self.from_x[d].astype(jnp.float32)
        self.acc[here] = total.astype(jnp.bfloat16)

    def start_z2(self):
        if not self.split:
            return
        base = self.depth + self.across - 1
        self.begin(
            [
                send(self.acc.at[self.own_part()], self.from_z2.at[d], self.sems, base + d, peer)
                for d, peer in enumerate(self.z_peers)
            ]
        )

    def finish_z2(self):
        if not self.split:
            return
        self.end()
        for d in range(self.depth - 1):
            self.acc[self.own_part(-(d + 1))] = self.from_z2[d]

    def start_core2(self):
        last = 2 * (self.depth - 1) + self.across
        self.begin([send(self.acc, self.other, self.sems, last, self.partner)])

    def finish_core2(self, out_ref):
        self.end()
        out_ref[:, :, self.lanes] = self.acc[...]
        out_ref[:, :, self.far_lanes] = self.other[...]


def segment(info, r, rows):
    begin = jnp.int32(0)
    for q in range(r):
        begin = begin + info[q]
    end = begin + info[r]
    first = info[16]
    low = jnp.clip(begin - first, 0, rows)
    high = jnp.clip(end - first, 0, rows)
    fresh = begin >= first
    ends = (end > first) & (end <= first + rows)
    return begin, low, high, fresh, ends


def summed(ones, step):
    high = step.astype(jnp.bfloat16)
    rest = step - high.astype(jnp.float32)
    mid = rest.astype(jnp.bfloat16)
    low = (rest - mid.astype(jnp.float32)).astype(jnp.bfloat16)
    return (
        jnp.dot(ones, high, preferred_element_type=jnp.float32)
        + jnp.dot(ones, mid, preferred_element_type=jnp.float32)
        + jnp.dot(ones, low, preferred_element_type=jnp.float32)
    )


def local_scan(g, width, rows, mixed_ref, step_ref, decay_ref, reset_ref, bc_wide, y_ref):
    tiles = width // LANES
    power = (lax.broadcasted_iota(jnp.int32, (8, LANES), 0) + 1).astype(jnp.float32)
    tile_cols = [
        pl.ds(pl.multiple_of(g * width + j * LANES, LANES), LANES) for j in range(tiles)
    ]
    decays = [decay_ref[:, c] for c in tile_cols]
    rates = [-d * power for d in decays]

    def eight(block, state):
        row = pl.multiple_of(block * 8, 8)
        here = pl.ds(row, 8)
        reset = reset_ref[here, :]
        step = [step_ref[here, c] for c in tile_cols]
        push = [s * mixed_ref[here, c] for s, c in zip(step, tile_cols)]
        step = [s + reset for s in step]
        fade8 = [jnp.exp(-8.0 * (s * d)) for s, d in zip(step, decays)]
        kept = [[] for _ in range(tiles)]
        for i in range(8):
            b_low, b_high = bc_wide[row + i, 0:8], bc_wide[row + i, 8:16]
            c_low, c_high = bc_wide[row + i, 16:24], bc_wide[row + i, 24:32]
            new = []
            for j in range(tiles):
                s_row, p_row, f_row = (
                    jnp.broadcast_to(part[j][i : i + 1], (8, LANES))
                    for part in (step, push, fade8)
                )
                d_low = jnp.exp(s_row * rates[j])
                low = d_low * state[2 * j] + b_low * p_row
                high = d_low * f_row * state[2 * j + 1] + b_high * p_row
                new += [low, high]
                kept[j].append(jnp.sum(c_low * low + c_high * high, axis=0, keepdims=True))
            state = tuple(new)
        for j in range(tiles):
            y_ref[here, tile_cols[j]] = jnp.concatenate(kept[j], axis=0)
        return state

    zero = jnp.zeros((8, LANES), jnp.float32)
    lax.fori_loop(0, rows // 8, eight, (zero,) * (2 * tiles))


def front_stage(
    devices,
    info,
    taps_ref,
    conv_b_flat,
    dt_bias_flat,
    decay_flat,
    skip_flat,
    gain_flat,
    x_hbm,
    cache_hbm,
    cache_edge_hbm,
    x_proj_hbm,
    dt_proj_hbm,
    mixed_hbm,
    step_hbm,
    y_hbm,
    pre_hbm,
    proj_ref,
    enter_ref,
    last_edge_ref,
    start_ref,
    param_ref,
    mixed_ref,
    step_ref,
    keep_sems,
    since_ref,
    y_ref,
    pre_ref,
    bc_wide,
    reset_ref,
    block_sems,
    x_ref,
    cache_ref,
    cache_edge_ref,
    x_proj_ref,
    dt_proj_ref,
    fetch_sems,
    ext,
    mixed_b,
    suffix,
    b_wide,
    halo_ref,
    edge3_ref,
    end_ref,
    sum_ref,
    halo_sems,
    pair_h,
    pair_s,
    own_h,
    own_s,
    z_h,
    z_s,
    x_h,
    x_s,
    half_out,
    half_in,
    pre_sems,
    *spread_refs,
):
    fetches = [
        pltpu.make_async_copy(src, dst, fetch_sems.at[i])
        for i, (src, dst) in enumerate(
            (
                (x_hbm, x_ref),
                (cache_edge_hbm, cache_edge_ref),
                (cache_hbm, cache_ref),
                (x_proj_hbm, x_proj_ref),
                (dt_proj_hbm, dt_proj_ref),
            )
        )
    ]
    for copy in fetches:
        copy.start()
    param_ref[pl.ds(0, 4), :] = taps_ref[...]
    for i, flat in enumerate((conv_b_flat, dt_bias_flat, decay_flat, skip_flat, gain_flat)):
        size = flat.shape[0]
        param_ref[pl.ds(4 + i, 1), pl.ds(0, size)] = flat[...].reshape(1, size)
    conv_w_ref = param_ref.at[pl.ds(0, 4)]
    conv_b_ref = param_ref.at[pl.ds(4, 1)]
    dt_bias_ref = param_ref.at[pl.ds(5, 1)]
    decay_ref = param_ref.at[pl.ds(6, 1)]
    rows, inner = x_ref.shape
    requests = start_ref.shape[0]
    me, core, z, x, partner, z_peers, x_peers = near_devices(devices)
    after, before = (me + 1) % devices, (me + devices - 1) % devices
    greet([("seq", p) for p in [partner, after, before] + z_peers + x_peers])
    halo_copy = send(x_ref.at[pl.ds(rows - 16, 16)], halo_ref, halo_sems, 0, after)
    fetches[0].wait()
    halo_copy.start()
    fetches[1].wait()
    per = len(Spread.scratch(devices, inner, 1, False))
    edge_sum = Spread(devices, inner, 1, False, spread_refs[:per])
    state_sum = Spread(devices, inner, requests, True, spread_refs[per:])
    spot = lax.broadcasted_iota(jnp.int32, (16, inner), 0)
    edge_rows = cache_edge_ref[...].astype(jnp.float32)
    placed = jnp.zeros((16, inner), jnp.float32)
    for r in range(requests):
        take = (info[8 + r] == me) & (info[4 + r] > 0)
        for j in range(EDGE):
            placed = jnp.where((spot == r * EDGE + j) & take, edge_rows[j : j + 1], placed)
    edge_sum.mine[0] = placed.astype(jnp.bfloat16)
    edge_sum.start_core()
    fetches[2].wait()
    for r in range(requests):
        take = (info[8 + r] == me) & (info[4 + r] > 0)
        state_sum.mine[r] = jnp.where(take, cache_ref[...], 0.0).astype(jnp.bfloat16)
    state_sum.start_core()
    ext[pl.ds(16, rows), :] = x_ref[...].astype(jnp.float32)
    fetches[3].wait()
    fetches[4].wait()
    edge_sum.finish_core()
    edge_sum.start_z()
    state_sum.finish_core()
    edge_sum.finish_z()
    edge_sum.start_x()
    state_sum.start_z()
    edge_sum.finish_x()
    edge_sum.start_core2()
    edge_sum.finish_core2(edge3_ref)
    edge_ref = edge3_ref.at[0]
    halo_copy.wait()
    width = col_block(inner)
    rank = dt_proj_ref.shape[0]
    ext[pl.ds(0, 16), :] = halo_ref[...].astype(jnp.float32)
    first_pos = info[16]
    position = first_pos + lax.broadcasted_iota(jnp.int32, (rows, LANES), 0)
    marks = [segment(info, r, rows) for r in range(requests)]
    begin = jnp.zeros((rows, LANES), jnp.int32)
    request = jnp.zeros((rows, LANES), jnp.int32)
    last_begin, last_req = jnp.int32(0), jnp.int32(0)
    for r in range(1, requests):
        reached = position >= marks[r][0]
        begin = jnp.where(reached, marks[r][0], begin)
        request = jnp.where(reached, r, request)
        inside = first_pos + rows - 1 >= marks[r][0]
        last_begin = jnp.where(inside, marks[r][0], last_begin)
        last_req = jnp.where(inside, r, last_req)
    offset = position - begin
    in_last = (position >= last_begin).astype(jnp.float32)
    edge_id = lax.broadcasted_iota(jnp.int32, (rows, 16), 1)
    hots = []
    for lag in (1, 2, 3):
        want = request * EDGE + EDGE + offset - lag
        hit = (edge_id == want[:, :16]) & (offset[:, :16] < lag)
        hots.append(hit.astype(jnp.float32).astype(jnp.bfloat16))

    keep = {}
    for lag in (1, 2, 3):
        keep[lag] = jnp.concatenate([offset] * (width // LANES), axis=1) >= lag
    for first in range(0, inner, width):
        cols = pl.ds(first, width)
        edges = edge_ref[:, cols]
        total = conv_b_ref[:, cols] + conv_w_ref[pl.ds(3, 1), cols] * ext[pl.ds(16, rows), cols]
        for lag in (1, 2, 3):
            near = ext[pl.ds(16 - lag, rows), cols]
            far = jnp.dot(hots[lag - 1], edges, preferred_element_type=jnp.float32)
            row = jnp.where(keep[lag], near, far)
            total = total + conv_w_ref[pl.ds(3 - lag, 1), cols] * row
        mixed = (total / (1.0 + jnp.exp(-total))).astype(jnp.bfloat16)
        mixed_b[:, cols] = mixed
        mixed_ref[:, cols] = mixed.astype(jnp.float32)

    state_sum.finish_z()
    state_sum.start_x()
    keep_mixed = pltpu.make_async_copy(mixed_ref, mixed_hbm, keep_sems.at[0])
    keep_mixed.start()
    proj = lax.dot_general(
        mixed_b[...],
        x_proj_ref[...],
        (((1,), (1,)), ((), ())),
        preferred_element_type=jnp.float32,
    )
    proj_ref[...] = proj
    for s in range(STATE):
        b_wide[s] = jnp.broadcast_to(proj[:, rank + s : rank + s + 1], (rows, LANES))
    dt_low = proj[:, :rank].astype(jnp.bfloat16)
    row_id = lax.broadcasted_iota(jnp.int32, (rows, rows), 0)
    col_id = lax.broadcasted_iota(jnp.int32, (rows, rows), 1)
    later = (col_id > row_id).astype(jnp.bfloat16)
    for first in range(0, inner, width):
        cols = pl.ds(first, width)
        v = jnp.dot(dt_low, dt_proj_ref[:, cols], preferred_element_type=jnp.float32)
        v = v + dt_bias_ref[:, cols]
        step = jnp.maximum(v, 0.0) + jnp.log1p(jnp.exp(-jnp.abs(v)))
        step_ref[:, cols] = step
        suffix[:, cols] = summed(later, step)

    keep_step = pltpu.make_async_copy(step_ref, step_hbm, keep_sems.at[1])
    keep_step.start()
    state_sum.finish_x()
    state_sum.start_z2()
    starts_here = (last_begin >= first_pos).astype(jnp.int32)
    flag = jnp.full((1, LANES), starts_here, jnp.int32).astype(jnp.float32)
    power = (lax.broadcasted_iota(jnp.int32, (STATE, LANES), 0) + 1).astype(jnp.float32)

    def one_tile(j, carry):
        cols = pl.ds(pl.multiple_of(j * LANES, LANES), LANES)
        rate = decay_ref[:, cols]
        acc = [jnp.zeros((8, LANES), jnp.float32) for _ in range(STATE)]
        since = jnp.zeros((8, LANES), jnp.float32)
        for tile in range(rows // 8):
            here = pl.ds(tile * 8, 8)
            fade = jnp.exp(-rate * suffix[here, cols])
            step = step_ref[here, cols] * in_last[tile * 8 : tile * 8 + 8]
            since = since + step
            push = step * mixed_ref[here, cols]
            for s in range(STATE):
                push = push * fade
                acc[s] = acc[s] + push * b_wide[s, here, :]
        ends = jnp.concatenate([jnp.sum(a, axis=0, keepdims=True) for a in acc], axis=0)
        end_ref[:, cols] = ends
        since = jnp.sum(since, axis=0, keepdims=True)
        since_ref[:, cols] = since
        sum_ref[:, cols] = jnp.where(flag > 0.5, FAR, since)
        return carry

    def one_seed(j, carry):
        cols = pl.ds(pl.multiple_of(j * LANES, LANES), LANES)
        rate = decay_ref[:, cols]
        since = since_ref[:, cols]
        seed = jnp.exp(-(rate * since) * power) * start_ref[last_req, :, cols].astype(jnp.float32)
        end_ref[:, cols] = end_ref[:, cols] + flag * seed
        return carry

    lax.fori_loop(0, inner // LANES, one_tile, 0)
    state_sum.finish_z2()
    state_sum.start_core2()
    state_sum.finish_core2(start_ref)
    lax.fori_loop(0, inner // LANES, one_seed, 0)
    power16 = (lax.broadcasted_iota(jnp.int32, (STATE, LANES), 0) + 1).astype(jnp.float32)
    half = half_width(inner)
    tiles = half // LANES
    base = core * (inner - half)
    own_h[...] = end_ref[...].astype(jnp.bfloat16)
    for j in range(inner // LANES):
        own_s[pl.ds(j, 1), :] = sum_ref[:, pl.ds(j * LANES, LANES)]
    pair = [
        send(own_h, pair_h, pre_sems, 0, partner),
        send(own_s, pair_s, pre_sems, 1, partner),
    ]
    for copy in pair:
        copy.start()
    reset_ref[...] = jnp.where(offset == 0, FAR, 0.0)
    turned = jnp.transpose(proj_ref[:, rank : rank + 2 * STATE])
    for t in range(rows):
        bc_wide[t] = jnp.broadcast_to(turned[:, t : t + 1], (2 * STATE, LANES))
    at_row = first_pos + row_id
    at_col = first_pos + col_id
    begin_row = jnp.zeros((rows, rows), jnp.int32)
    begin_col = jnp.zeros((rows, rows), jnp.int32)
    for r in range(1, requests):
        begin_row = jnp.where(at_row >= marks[r][0], marks[r][0], begin_row)
        begin_col = jnp.where(at_col >= marks[r][0], marks[r][0], begin_col)
    upto = ((col_id <= row_id) & (begin_row == begin_col)).astype(jnp.float32)
    upto = upto.astype(jnp.bfloat16)
    blocks = inner // width
    cuts = [0, -(-blocks // 5), -(-3 * blocks // 5), blocks]

    def block_keeps(g):
        cols = pl.ds(pl.multiple_of(g * width, LANES), width)
        return (
            pltpu.make_async_copy(y_ref.at[:, cols], y_hbm.at[:, cols], block_sems.at[0, g]),
            pltpu.make_async_copy(pre_ref.at[:, cols], pre_hbm.at[:, cols], block_sems.at[1, g]),
        )

    def scan_block(g, carry):
        cols = pl.ds(pl.multiple_of(g * width, LANES), width)
        local_scan(
            g, width, rows, mixed_ref, step_ref, decay_ref, reset_ref, bc_wide, y_ref
        )
        y_ref[:, cols] = y_ref[:, cols] + param_ref[7:8, cols] * mixed_ref[:, cols]
        pre_ref[:, cols] = summed(upto, step_ref[:, cols])
        for copy in block_keeps(g):
            copy.start()
        return carry

    lax.fori_loop(cuts[0], cuts[1], scan_block, 0)
    across, depth = layout_of(devices)
    first_core = core == 0

    def lane(j):
        return pl.ds(pl.multiple_of(base + j * LANES, LANES), LANES)

    def f32(value):
        return value.astype(jnp.float32)

    for copy in pair:
        copy.wait()
    z_sum = []
    for j in range(tiles):
        rate = decay_ref[:, lane(j)] * power16
        mine, theirs = own_h[:, lane(j)], pair_h[:, lane(j)]
        shift = (inner - half) // LANES
        s_mine = jnp.where(first_core, own_s[j : j + 1], own_s[j + shift : j + shift + 1])
        s_pair = jnp.where(first_core, pair_s[j : j + 1], pair_s[j + shift : j + shift + 1])
        h0 = f32(jnp.where(first_core, f32(mine), f32(theirs)))
        h1 = f32(jnp.where(first_core, f32(theirs), f32(mine)))
        s1 = jnp.where(first_core, s_pair, s_mine)
        z_h[0, :, pl.ds(j * LANES, LANES)] = (jnp.exp(-rate * s1) * h0 + h1).astype(jnp.bfloat16)
        z_s[0, pl.ds(j, 1), :] = s_mine + s_pair
    copies = []
    for d, peer in enumerate(z_peers):
        copies.append(send(z_h.at[0], z_h.at[d + 1], pre_sems, 2 + 2 * d, peer))
        copies.append(send(z_s.at[0], z_s.at[d + 1], pre_sems, 3 + 2 * d, peer))
    for copy in copies:
        copy.start()
    lax.fori_loop(cuts[1], cuts[2], scan_block, 0)
    for copy in copies:
        copy.wait()
    prefix = []
    for j in range(tiles):
        cols = pl.ds(j * LANES, LANES)
        rate = decay_ref[:, lane(j)] * power16
        total = jnp.zeros((STATE, LANES), jnp.float32)
        part = jnp.zeros((STATE, LANES), jnp.float32)
        total_s = jnp.zeros((1, LANES), jnp.float32)
        part_s = jnp.zeros((1, LANES), jnp.float32)
        for k in range(depth):
            slot = (z - k + depth) % depth
            s_k = z_s[slot, pl.ds(j, 1), :]
            h_k = f32(z_h[slot, :, cols])
            fade = jnp.exp(-rate * s_k)
            total = fade * total + h_k
            part = jnp.where(k < z, fade * part + h_k, part)
            total_s = total_s + s_k
            part_s = jnp.where(k < z, part_s + s_k, part_s)
        x_h[0, :, cols] = total.astype(jnp.bfloat16)
        x_s[0, pl.ds(j, 1), :] = total_s
        prefix.append((part, part_s))
    copies = []
    first = 2 + 2 * (depth - 1)
    for d, peer in enumerate(x_peers):
        copies.append(send(x_h.at[0], x_h.at[d + 1], pre_sems, first + 2 * d, peer))
        copies.append(send(x_s.at[0], x_s.at[d + 1], pre_sems, first + 1 + 2 * d, peer))
    for copy in copies:
        copy.start()
    lax.fori_loop(cuts[2], cuts[3], scan_block, 0)
    for copy in copies:
        copy.wait()
    for j in range(tiles):
        cols = pl.ds(j * LANES, LANES)
        rate = decay_ref[:, lane(j)] * power16
        part = jnp.zeros((STATE, LANES), jnp.float32)
        for k in range(across):
            slot = (x - k + across) % across
            value = jnp.exp(-rate * x_s[slot, pl.ds(j, 1), :]) * part + f32(x_h[slot, :, cols])
            part = jnp.where(k < x, value, part)
        inner_part, inner_s = prefix[j]
        half_out[:, cols] = jnp.exp(-rate * inner_s) * part + inner_part
    last = first + 2 * (across - 1)
    swap = send(half_out, half_in, pre_sems, last, partner)
    swap.start()
    swap.wait()
    enter_ref[:, my_lanes(core, inner)] = half_out[...]
    enter_ref[:, my_lanes(1 - core, inner)] = half_in[...]
    for j in range(inner // LANES):
        cols = pl.ds(j * LANES, LANES)
        rate = decay_ref[:, cols] * power16
        chip = enter_ref[:, cols]
        second = jnp.exp(-rate * pair_s[j : j + 1]) * chip + f32(pair_h[:, cols])
        enter_ref[:, cols] = jnp.where(first_core, chip, second)

    row_of = lax.broadcasted_iota(jnp.int32, (16, LANES), 0)
    from_of = lax.broadcasted_iota(jnp.int32, (16, LANES), 1)
    near_at = jnp.full((16, LANES), -1, jnp.int32)
    far_at = jnp.full((16, LANES), -1, jnp.int32)
    for r in range(requests):
        _, _, high, _, ends = marks[r]
        size = info[r]
        for j in range(EDGE):
            lag = EDGE - 1 - j
            near = jnp.where(ends & (size > lag), high + 15 - lag, -1)
            far = jnp.where(ends & (size <= lag), r * EDGE + EDGE + size - 1 - lag, -1)
            near_at = jnp.where(row_of == r * EDGE + j, near, near_at)
            far_at = jnp.where(row_of == r * EDGE + j, far, far_at)

    def hot_rows(at, count):
        return (from_of[:, :count] == at[:, :count]).astype(jnp.float32).astype(jnp.bfloat16)

    for first in range(0, inner, width):
        cols = pl.ds(first, width)
        last_edge_ref[:, cols] = (
            jnp.dot(hot_rows(near_at - 16, rows), x_ref[:, cols], preferred_element_type=jnp.float32)
            + jnp.dot(hot_rows(near_at, 16), halo_ref[:, cols], preferred_element_type=jnp.float32)
            + jnp.dot(hot_rows(far_at, 16), edge_ref[:, cols], preferred_element_type=jnp.float32)
        )
    keep_mixed.wait()
    keep_step.wait()
    for g in range(blocks):
        for copy in block_keeps(g):
            copy.wait()


def front_call(devices, info, args, rows, inner, proj_width, requests):
    f32, bf16 = jnp.float32, jnp.bfloat16
    across, depth = layout_of(devices)
    half = half_width(inner)
    s_rows = -(-(inner // LANES) // 8) * 8
    return pl.pallas_call(
        functools.partial(front_stage, devices),
        out_shape=(
            jax.ShapeDtypeStruct((rows, inner), f32),
            jax.ShapeDtypeStruct((rows, inner), f32),
            jax.ShapeDtypeStruct((rows, inner), f32),
            jax.ShapeDtypeStruct((rows, inner), f32),
            jax.ShapeDtypeStruct((rows, proj_width), f32),
            jax.ShapeDtypeStruct((STATE, inner), f32),
            jax.ShapeDtypeStruct((16, inner), f32),
            jax.ShapeDtypeStruct((requests, STATE, inner), bf16),
            jax.ShapeDtypeStruct((16, inner), f32),
        ),
        in_specs=[sspec()] + [vspec()] * 6 + [hspec()] * (len(args) - 6),
        out_specs=tuple([hspec()] * 4 + [vspec()] * 5),
        scratch_shapes=[
            VMEM((rows, inner), f32),
            VMEM((rows, inner), f32),
            pltpu.SemaphoreType.DMA((2,)),
            VMEM((1, inner), f32),
            VMEM((rows, inner), f32),
            VMEM((rows, inner), f32),
            VMEM((rows, 2 * STATE, LANES), f32),
            VMEM((rows, LANES), f32),
            pltpu.SemaphoreType.DMA((2, inner // col_block(inner))),
            VMEM((rows, inner), bf16),
            VMEM((STATE, inner), f32),
            VMEM((EDGE, inner), bf16),
            VMEM((proj_width, inner), bf16),
            VMEM((proj_width - 2 * STATE, inner), bf16),
            pltpu.SemaphoreType.DMA((5,)),
            VMEM((rows + 16, inner), f32),
            VMEM((rows, inner), bf16),
            VMEM((rows, inner), f32),
            VMEM((STATE, rows, LANES), f32),
            VMEM((16, inner), bf16),
            VMEM((1, 16, inner), bf16),
            VMEM((STATE, inner), f32),
            VMEM((1, inner), f32),
            pltpu.SemaphoreType.DMA((2, 1)),
            VMEM((STATE, inner), bf16),
            VMEM((s_rows, LANES), f32),
            VMEM((STATE, inner), bf16),
            VMEM((s_rows, LANES), f32),
            VMEM((depth, STATE, half), bf16),
            VMEM((depth, 16, LANES), f32),
            VMEM((across, STATE, half), bf16),
            VMEM((across, 16, LANES), f32),
            VMEM((STATE, half), f32),
            VMEM((STATE, half), f32),
            pltpu.SemaphoreType.DMA((2, 3 + 2 * (depth + across - 2))),
        ]
        + Spread.scratch(devices, inner, 1, False)
        + Spread.scratch(devices, inner, requests, True),
        compiler_params=pltpu.CompilerParams(
            vmem_limit_bytes=61 << 20, collective_id=0, has_side_effects=True
        ),
        cost_estimate=pl.CostEstimate(
            flops=400_000_000, bytes_accessed=8_000_000, transcendentals=2_000_000
        ),
        name="front_stage",
    )(info, *args)


def join_stage(
    info,
    y_hbm,
    pre_hbm,
    step_hbm,
    mixed_hbm,
    proj_ref,
    enter_ref,
    start_ref,
    param_ref,
    hidden_hbm,
    out_w_hbm,
    middle_ref,
    normed_ref,
    final_hbm,
    y_ref,
    pre_ref,
    step_ref,
    mixed_ref,
    final_ref,
    block_sems,
    extra_sems,
    final_sem,
    b_wide,
    c_wide,
    ssm_b,
    out_w,
    hidden_ref,
    w_sem,
    hidden_sem,
):
    rows, inner = y_ref.shape
    width = col_block(inner)
    tiles = width // LANES
    requests = final_ref.shape[0]
    rank = proj_ref.shape[1] - 2 * STATE
    model = hidden_ref.shape[0]
    decay_ref = param_ref.at[pl.ds(6, 1)]
    span = min(64, rows)
    marks = [segment(info, r, rows) for r in range(requests)]
    any_end = marks[0][4]
    for r in range(1, requests):
        any_end = any_end | marks[r][4]

    def block_copies(g):
        cols = pl.ds(pl.multiple_of(g * width, LANES), width)
        return (
            pltpu.make_async_copy(pre_hbm.at[:, cols], pre_ref.at[:, cols], block_sems.at[0, g]),
            pltpu.make_async_copy(y_hbm.at[:, cols], y_ref.at[:, cols], block_sems.at[1, g]),
        )

    extra = (
        pltpu.make_async_copy(step_hbm, step_ref, extra_sems.at[0]),
        pltpu.make_async_copy(mixed_hbm, mixed_ref, extra_sems.at[1]),
    )
    for g in range(inner // width):
        for copy in block_copies(g):
            copy.start()

    @pl.when(any_end)
    def _():
        for copy in extra:
            copy.start()

    fetch = pltpu.make_async_copy(out_w_hbm, out_w, w_sem)
    fetch.start()
    fetch_hidden = pltpu.make_async_copy(hidden_hbm, hidden_ref, hidden_sem)
    fetch_hidden.start()
    proj = proj_ref[...]
    for s in range(STATE):
        at = rank + STATE + s
        c_wide[s] = jnp.broadcast_to(proj[:, at : at + 1], (rows, LANES))
    final_ref[...] = jnp.zeros_like(final_ref)

    @pl.when(any_end)
    def _():
        for s in range(STATE):
            b_wide[s] = jnp.broadcast_to(proj[:, rank + s : rank + s + 1], (rows, LANES))
        for copy in extra:
            copy.wait()

    power = (lax.broadcasted_iota(jnp.int32, (STATE, LANES), 0) + 1).astype(jnp.float32)
    tile_row = lax.broadcasted_iota(jnp.int32, (8, LANES), 0)

    def one_block(g, carry):
        for copy in block_copies(g):
            copy.wait()
        for r in range(requests):
            _, low, high, new, ends = marks[r]
            spans = (low // span, (high + span - 1) // span)

            @pl.when(high > low)
            def _():
                def one_tile(j, inside):
                    cols = pl.ds(pl.multiple_of(g * width + j * LANES, LANES), LANES)
                    decay = decay_ref[:, cols]
                    seed = start_ref[r, :, cols].astype(jnp.float32)
                    origin = jnp.where(new, seed, enter_ref[:, cols])
                    wide = [jnp.broadcast_to(origin[s : s + 1], (8, LANES)) for s in range(STATE)]

                    def parts(q):
                        found = []
                        for k in range(span // 8):
                            row = pl.multiple_of(q * span + k * 8, 8)
                            at = row + tile_row
                            found.append((pl.ds(row, 8), (at >= low) & (at < high)))
                        return found

                    def add(q, done):
                        for here, inside in parts(q):
                            fade = jnp.exp(-decay * pre_ref[here, cols])
                            total = c_wide[STATE - 1, here, :] * wide[STATE - 1]
                            for s in range(STATE - 2, -1, -1):
                                total = total * fade + c_wide[s, here, :] * wide[s]
                            y = y_ref[here, cols]
                            y_ref[here, cols] = jnp.where(inside, y + total * fade, y)
                        return done

                    lax.fori_loop(spans[0], spans[1], add, 0)

                    @pl.when(ends)
                    def _():
                        def count(q, whole):
                            for here, inside in parts(q):
                                whole = whole + jnp.where(inside, step_ref[here, cols], 0.0)
                            return whole

                        whole = lax.fori_loop(
                            spans[0], spans[1], count, jnp.zeros((8, LANES), jnp.float32)
                        )
                        whole = jnp.sum(whole, axis=0, keepdims=True)

                        def gather(q, acc):
                            acc = list(acc)
                            for here, inside in parts(q):
                                left = jnp.where(inside, whole - pre_ref[here, cols], 0.0)
                                fade = jnp.exp(-decay * left)
                                push = step_ref[here, cols] * mixed_ref[here, cols]
                                push = jnp.where(inside, push, 0.0)
                                for s in range(STATE):
                                    push = push * fade
                                    acc[s] = acc[s] + push * b_wide[s, here, :]
                            return tuple(acc)

                        zero = jnp.zeros((8, LANES), jnp.float32)
                        acc = lax.fori_loop(spans[0], spans[1], gather, (zero,) * STATE)
                        own = [jnp.sum(a, axis=0, keepdims=True) for a in acc]
                        own = jnp.concatenate(own, axis=0)
                        final_ref[r, :, cols] = own + jnp.exp(-(decay * whole) * power) * origin

                    return inside

                lax.fori_loop(0, tiles, one_tile, 0)

        cols = pl.ds(pl.multiple_of(g * width, LANES), width)
        ssm_b[:, cols] = y_ref[:, cols].astype(jnp.bfloat16)
        return carry

    lax.fori_loop(0, inner // width, one_block, 0)
    keep_final = pltpu.make_async_copy(final_ref, final_hbm, final_sem)
    keep_final.start()
    fetch.wait()
    fetch_hidden.wait()
    middle = jnp.transpose(hidden_ref[...].astype(jnp.float32))
    for first in range(0, inner, width):
        middle = middle + lax.dot_general(
            ssm_b[:, first : first + width],
            out_w[:, first : first + width],
            (((1,), (1,)), ((), ())),
            preferred_element_type=jnp.float32,
        )
    middle_ref[...] = middle
    scale = lax.rsqrt(jnp.mean(middle * middle, axis=1, keepdims=True) + NORM_EPS)
    normed = (middle * scale * param_ref[8:9, :model]).astype(jnp.bfloat16)
    if normed_ref.shape[1] > model:
        normed_ref[...] = jnp.zeros_like(normed_ref)
    normed_ref[:, :model] = normed
    keep_final.wait()


def join_call(info, args, out_w, rows, inner, model, requests):
    f32 = jnp.float32
    return pl.pallas_call(
        join_stage,
        out_shape=(
            jax.ShapeDtypeStruct((rows, model), f32),
            jax.ShapeDtypeStruct((rows, padded(model)), jnp.bfloat16),
            jax.ShapeDtypeStruct((requests, STATE, inner), f32),
        ),
        in_specs=[sspec()] + [hspec()] * 4 + [vspec()] * (len(args) - 5) + [hspec()] * 2,
        out_specs=tuple([vspec()] * 2 + [hspec()]),
        scratch_shapes=[
            VMEM((rows, inner), f32),
            VMEM((rows, inner), f32),
            VMEM((rows, inner), f32),
            VMEM((rows, inner), f32),
            VMEM((requests, STATE, inner), f32),
            pltpu.SemaphoreType.DMA((2, inner // col_block(inner))),
            pltpu.SemaphoreType.DMA((2,)),
            pltpu.SemaphoreType.DMA,
            VMEM((STATE, rows, LANES), f32),
            VMEM((STATE, rows, LANES), f32),
            VMEM((rows, inner), jnp.bfloat16),
            VMEM((model, inner), jnp.bfloat16),
            VMEM((model, rows), jnp.bfloat16),
            pltpu.SemaphoreType.DMA,
            pltpu.SemaphoreType.DMA,
        ],
        compiler_params=pltpu.CompilerParams(vmem_limit_bytes=61 << 20),
        cost_estimate=pl.CostEstimate(
            flops=1_400_000_000, bytes_accessed=18_000_000, transcendentals=4_000_000
        ),
        name="join_stage",
    )(info, *args, out_w)


def mlp_stage(
    devices,
    info,
    normed_hbm,
    middle_hbm,
    final_hbm,
    last_edge_hbm,
    gate_hbm,
    up_hbm,
    down_hbm,
    out_ref,
    new_state_ref,
    new_edge_ref,
    normed_ref,
    middle_ref,
    final_ref,
    last_edge_ref,
    gate_w,
    up_w,
    down_w,
    fetch_sems,
    near1,
    near2,
    far,
    out1,
    out2,
    far_out,
    own_out,
    low_in,
    high_in,
    far_in,
    ring_sems,
    full,
    full_edge,
    *spread_refs,
):
    rows, model = middle_ref.shape
    half = rows // 2
    inner = final_ref.shape[2]
    requests = final_ref.shape[0]
    me, _, _, _, partner, z_peers, x_peers = near_devices(devices)
    ring = lax.axis_size("req")
    here = lax.axis_index("req")
    above, below = (here + 1) % ring, (here + ring - 1) % ring
    fetches = [
        pltpu.make_async_copy(src, dst, fetch_sems.at[i])
        for i, (src, dst) in enumerate(
            (
                (normed_hbm, normed_ref),
                (final_hbm, final_ref),
                (last_edge_hbm, last_edge_ref),
                (gate_hbm, gate_w),
                (up_hbm, up_w),
                (down_hbm, down_w),
                (middle_hbm, middle_ref),
            )
        )
    ]
    for copy in fetches:
        copy.start()
    greet(
        [("req", above), ("req", below)] + [("seq", p) for p in [partner] + z_peers + x_peers]
    )

    def hop(src, dst, index, peer):
        return pltpu.make_async_remote_copy(
            src_ref=src,
            dst_ref=dst,
            send_sem=ring_sems.at[0, index],
            recv_sem=ring_sems.at[1, index],
            device_id={"req": peer},
            device_id_type=MESH_ID,
        )

    piece = [pl.ds(i * (half // 2), half // 2) for i in range(4)]
    first, second = pl.ds(0, half), pl.ds(half, half)
    toward = [above, above, below, below]
    out_hops = [hop(normed_ref.at[piece[i]], near1.at[piece[i]], i, toward[i]) for i in range(4)]
    on_hops = [hop(near1.at[piece[i]], far.at[piece[i]], 4 + i, toward[i]) for i in range(4)]
    up_b = hop(normed_ref.at[second], near2.at[first], 8, above)
    down_a = hop(normed_ref.at[first], near2.at[second], 9, below)
    far_hops = [hop(far_out.at[piece[i]], far_in.at[piece[i]], 10 + i, toward[i]) for i in range(4)]
    back_down = hop(out1.at[first], high_in.at[first], 14, below)
    back_up = hop(out1.at[second], low_in.at[second], 15, above)
    swap = [2, 3, 0, 1]
    last_hops = [
        hop(
            out2.at[piece[swap[i]]],
            (low_in if i < 2 else high_in).at[piece[i]],
            16 + i,
            toward[i],
        )
        for i in range(4)
    ]
    order = (0, 2, 1, 3)
    fetches[0].wait()
    for i in order:
        out_hops[i].start()
    per = len(Spread.scratch(devices, inner, 1, False))
    finals = Spread(devices, inner, requests, True, spread_refs[:per])
    edges = Spread(devices, inner, 1, False, spread_refs[per:])
    fetches[1].wait()
    for r in range(requests):
        finals.mine[r] = final_ref[r].astype(jnp.bfloat16)
    finals.start_core()
    fetches[2].wait()
    edges.mine[0] = last_edge_ref[...].astype(jnp.bfloat16)
    edges.start_core()

    def hidden_units(value):
        gate = jnp.dot(value, gate_w[...], preferred_element_type=jnp.float32)
        up = jnp.dot(value, up_w[...], preferred_element_type=jnp.float32)
        hidden = (gate / (1.0 + jnp.exp(-gate)) * up).astype(jnp.bfloat16)
        return lax.dot_general(
            hidden, down_w[...], (((1,), (1,)), ((), ())), preferred_element_type=jnp.float32
        )

    finals.finish_core()
    finals.start_z()
    edges.finish_core()
    for i in order:
        out_hops[i].wait_recv()
        on_hops[i].start()
    up_b.start()
    down_a.start()
    for copy in fetches[3:]:
        copy.wait()
    out1[:, :model] = hidden_units(near1[:, :model]).astype(jnp.bfloat16)
    for i in order:
        on_hops[i].wait_recv()
    far_out[:, :model] = hidden_units(far[:, :model]).astype(jnp.bfloat16)
    for i in order:
        far_hops[i].start()
    finals.finish_z()
    finals.start_x()
    edges.start_z()
    up_b.wait_recv()
    down_a.wait_recv()
    own_out[...] = hidden_units(near2[:, :model])
    for i in order:
        far_hops[i].wait_recv()
        rows_at = piece[swap[i]]
        joined = own_out[rows_at] + far_in[piece[i], :model].astype(jnp.float32)
        out2[rows_at, :model] = joined.astype(jnp.bfloat16)
        last_hops[i].start()
    back_down.start()
    back_up.start()
    finals.finish_x()
    finals.start_z2()
    edges.finish_z()
    edges.start_x()
    own_out[...] = hidden_units(normed_ref[:, :model]) + middle_ref[...]
    finals.finish_z2()
    finals.start_core2()
    edges.finish_x()
    edges.start_core2()
    finals.finish_core2(full)
    state = jnp.zeros((STATE, inner), jnp.float32)
    for r in range(requests):
        state = jnp.where(info[12 + r] == me, full[r].astype(jnp.float32), state)
    new_state_ref[...] = state
    edges.finish_core2(full_edge)
    gathered = full_edge[0].astype(jnp.float32)
    edge = jnp.zeros((EDGE, inner), jnp.float32)
    for r in range(requests):
        owned = info[12 + r] == me
        edge = jnp.where(owned, gathered[r * EDGE : (r + 1) * EDGE], edge)
    new_edge_ref[...] = edge.astype(jnp.bfloat16)
    for i in order:
        last_hops[i].wait_recv()
    back_down.wait_recv()
    back_up.wait_recv()
    total = own_out[...] + low_in[:, :model].astype(jnp.float32)
    total = total + high_in[:, :model].astype(jnp.float32)
    out_ref[...] = jnp.transpose(total).astype(jnp.bfloat16)
    for copy in out_hops + on_hops + far_hops + last_hops + [up_b, down_a, back_down, back_up]:
        copy.wait_send()


def mlp_call(devices, info, args, weights, rows, model, inner, requests):
    f32, bf16 = jnp.float32, jnp.bfloat16
    hidden = weights[0].shape[1]
    wide = padded(model)
    return pl.pallas_call(
        functools.partial(mlp_stage, devices),
        out_shape=(
            jax.ShapeDtypeStruct((model, rows), bf16),
            jax.ShapeDtypeStruct((STATE, inner), f32),
            jax.ShapeDtypeStruct((EDGE, inner), bf16),
        ),
        in_specs=[sspec()] + [hspec()] * (len(args) + len(weights)),
        out_specs=tuple([vspec()] * 3),
        scratch_shapes=[
            VMEM((rows, wide), bf16),
            VMEM((rows, model), f32),
            VMEM((requests, STATE, inner), f32),
            VMEM((16, inner), f32),
            VMEM((model, hidden), bf16),
            VMEM((model, hidden), bf16),
            VMEM((model, hidden), bf16),
            pltpu.SemaphoreType.DMA((7,)),
            VMEM((rows, wide), bf16),
            VMEM((rows, wide), bf16),
            VMEM((rows, wide), bf16),
            VMEM((rows, wide), bf16),
            VMEM((rows, wide), bf16),
            VMEM((rows, wide), bf16),
            VMEM((rows, model), f32),
            VMEM((rows, wide), bf16),
            VMEM((rows, wide), bf16),
            VMEM((rows, wide), bf16),
            pltpu.SemaphoreType.DMA((2, 20)),
            VMEM((requests, 16, inner), bf16),
            VMEM((1, 16, inner), bf16),
        ]
        + Spread.scratch(devices, inner, requests, True)
        + Spread.scratch(devices, inner, 1, False),
        compiler_params=pltpu.CompilerParams(
            vmem_limit_bytes=61 << 20, collective_id=1, has_side_effects=True
        ),
        cost_estimate=pl.CostEstimate(
            flops=7_000_000_000, bytes_accessed=16_000_000, transcendentals=1_000_000
        ),
        name="mlp_stage",
    )(info, *args, *weights)


def handing_stage(*refs):
    count = len(refs) // 2
    for i in range(count):
        refs[count + i][...] = refs[i][...]


def handed(*arrays):
    return pl.pallas_call(
        handing_stage,
        out_shape=tuple(jax.ShapeDtypeStruct(a.shape, a.dtype) for a in arrays),
        in_specs=[vspec()] * len(arrays),
        out_specs=tuple([vspec()] * len(arrays)),
        name="handing_stage",
    )(*arrays)


def shards(
    hidden_in,
    mamba_in,
    conv_weight,
    conv_bias,
    x_proj,
    dt_proj,
    dt_bias,
    decay_rate,
    skip_gain,
    out_proj,
    norm_gain,
    mlp_gate,
    mlp_up,
    mlp_down,
    cache_state,
    cache_edge,
    req_lengths,
    cont_flag,
    cache_source,
    owner_slot,
):
    rows, inner = mamba_in.shape[1:]
    model = hidden_in.shape[2]
    requests = req_lengths.shape[1]
    devices = lax.axis_size("seq")
    place = lax.axis_index("seq")
    info = jnp.concatenate(
        [
            req_lengths[0],
            cont_flag[0],
            cache_source[0],
            owner_slot[0],
            jnp.reshape(place * rows, (1,)).astype(jnp.int32),
        ]
    )
    mixed, step, y, pre, proj, enter, last_edge, start_state, params = front_call(
        devices,
        info,
        (
            conv_weight,
            conv_bias,
            dt_bias,
            decay_rate,
            skip_gain,
            norm_gain,
            mamba_in[0],
            cache_state[0, 0],
            cache_edge[0, 0],
            x_proj.T,
            dt_proj,
        ),
        rows,
        inner,
        x_proj.shape[1],
        requests,
    )
    middle, normed, finals = join_call(
        info,
        (y, pre, step, mixed, proj, enter, start_state, params, hidden_in[0].T),
        out_proj.T,
        rows,
        inner,
        model,
        requests,
    )
    block_out, new_state, new_edge = handed(
        *mlp_call(
            devices,
            info,
            (normed, middle, finals, last_edge),
            (mlp_gate, mlp_up, mlp_down.T),
            rows,
            model,
            inner,
            requests,
        )
    )
    return block_out.T[None], new_state[None, None], new_edge[None, None]


def solution(mesh):
    grouped = P("req", "seq", None)
    slots = P("req", "seq", None, None)
    return jax.shard_map(
        shards,
        mesh=mesh,
        in_specs=(grouped, grouped)
        + (P(),) * 9
        + (P(None, "req"), P(None, "req"), P("req", None), slots, slots)
        + (P("req", None),) * 4,
        out_specs=(grouped, slots, slots),
        check_vma=False,
    )
```

```python
import functools

import jax
import jax.numpy as jnp
from jax import lax
from jax.experimental import pallas as pl
from jax.experimental.pallas import tpu as pltpu
from jax.sharding import PartitionSpec as P

STATE = 16
EDGE = 3
NORM_EPS = 1e-06
LANES = 128
FAR = 1e30
HIGHEST_PREC = lax.Precision.HIGHEST
VMEM = pltpu.VMEM
SMEM = pltpu.SMEM


def vspec():
    return pl.BlockSpec(memory_space=VMEM)


def hspec():
    return pl.BlockSpec(memory_space=pltpu.HBM)


def sspec():
    return pl.BlockSpec(memory_space=SMEM)


def col_block(width):
    return 640 if width % 640 == 0 else LANES


MESH_ID = pl.DeviceIdType.MESH


def layout_of(devices):
    depth = 4 if devices >= 32 else 2
    return devices // (2 * depth), depth


def padded(width):
    return -(-width // LANES) * LANES


def half_width(inner):
    return -(-inner // (2 * LANES)) * LANES


def near_devices(devices):
    across, depth = layout_of(devices)
    me = lax.axis_index("seq")
    core, z, x = me % 2, (me // 2) % depth, me // (2 * depth)
    partner = me + 1 - 2 * core
    z_peers = [x * 2 * depth + ((z + d) % depth) * 2 + core for d in range(1, depth)]
    x_peers = [((x + d) % across) * 2 * depth + z * 2 + core for d in range(1, across)]
    return me, core, z, x, partner, z_peers, x_peers


def my_lanes(core, inner):
    half = half_width(inner)
    return pl.ds(pl.multiple_of(core * (inner - half), LANES), half)


def send(src, dst, sems, index, peer):
    return pltpu.make_async_remote_copy(
        src_ref=src,
        dst_ref=dst,
        send_sem=sems.at[0, index],
        recv_sem=sems.at[1, index],
        device_id={"seq": peer},
        device_id_type=MESH_ID,
    )


def greet(axis_peers):
    barrier = pltpu.get_barrier_semaphore()
    for axis, peer in axis_peers:
        pl.semaphore_signal(barrier, inc=1, device_id={axis: peer}, device_id_type=MESH_ID)
    pl.semaphore_wait(barrier, len(axis_peers))


class Spread:
    def __init__(self, devices, inner, count, split, refs):
        self.devices, self.inner, self.count, self.split = devices, inner, count, split
        self.across, self.depth = layout_of(devices)
        self.part = count // self.depth if split else count
        (
            self.mine,
            self.from_core,
            self.acc,
            self.from_z,
            self.from_x,
            self.from_z2,
            self.other,
            self.sems,
        ) = refs
        _, self.core, self.z, self.x, self.partner, self.z_peers, self.x_peers = near_devices(
            devices
        )
        self.lanes = my_lanes(self.core, inner)
        self.far_lanes = my_lanes(1 - self.core, inner)
        self.copies = []

    @staticmethod
    def scratch(devices, inner, count, split):
        across, depth = layout_of(devices)
        part = count // depth if split else count
        half = half_width(inner)
        b = jnp.bfloat16
        return [
            VMEM((count, 16, inner), b),
            VMEM((count, 16, half), b),
            VMEM((count, 16, half), b),
            VMEM((depth - 1, part, 16, half), b),
            VMEM((across - 1, part, 16, half), b),
            VMEM((depth - 1, part, 16, half), b),
            VMEM((count, 16, half), b),
            pltpu.SemaphoreType.DMA((2, 2 + 2 * (depth - 1) + (across - 1))),
        ]

    def own_part(self, shift=0):
        if not self.split:
            return pl.ds(0, self.part)
        return pl.ds(((self.z + shift) % self.depth) * self.part, self.part)

    def begin(self, copies):
        self.copies = copies
        for copy in copies:
            copy.start()

    def end(self):
        for copy in self.copies:
            copy.wait()

    def start_core(self):
        self.begin(
            [send(self.mine.at[:, :, self.far_lanes], self.from_core, self.sems, 0, self.partner)]
        )

    def finish_core(self):
        self.end()
        total = self.mine[:, :, self.lanes].astype(jnp.float32) + self.from_core[...].astype(
            jnp.float32
        )
        self.acc[...] = total.astype(jnp.bfloat16)

    def start_z(self):
        self.begin(
            [
                send(self.acc.at[self.own_part(d + 1)], self.from_z.at[d], self.sems, 1 + d, peer)
                for d, peer in enumerate(self.z_peers)
            ]
        )

    def finish_z(self):
        self.end()
        here = self.own_part()
        total = self.acc[here].astype(jnp.float32)
        for d in range(self.depth - 1):
            total = total + self.from_z[d].astype(jnp.float32)
        self.acc[here] = total.astype(jnp.bfloat16)

    def start_x(self):
        base = self.depth
        self.begin(
            [
                send(self.acc.at[self.own_part()], self.from_x.at[d], self.sems, base + d, peer)
                for d, peer in enumerate(self.x_peers)
            ]
        )

    def finish_x(self):
        self.end()
        here = self.own_part()
        total = self.acc[here].astype(jnp.float32)
        for d in range(self.across - 1):
            total = total + self.from_x[d].astype(jnp.float32)
        self.acc[here] = total.astype(jnp.bfloat16)

    def start_z2(self):
        if not self.split:
            return
        base = self.depth + self.across - 1
        self.begin(
            [
                send(self.acc.at[self.own_part()], self.from_z2.at[d], self.sems, base + d, peer)
                for d, peer in enumerate(self.z_peers)
            ]
        )

    def finish_z2(self):
        if not self.split:
            return
        self.end()
        for d in range(self.depth - 1):
            self.acc[self.own_part(-(d + 1))] = self.from_z2[d]

    def start_core2(self):
        last = 2 * (self.depth - 1) + self.across
        self.begin([send(self.acc, self.other, self.sems, last, self.partner)])

    def finish_core2(self, out_ref):
        self.end()
        out_ref[:, :, self.lanes] = self.acc[...]
        out_ref[:, :, self.far_lanes] = self.other[...]


def segment(info, r, rows):
    begin = jnp.int32(0)
    for q in range(r):
        begin = begin + info[q]
    end = begin + info[r]
    first = info[16]
    low = jnp.clip(begin - first, 0, rows)
    high = jnp.clip(end - first, 0, rows)
    fresh = begin >= first
    ends = (end > first) & (end <= first + rows)
    return begin, low, high, fresh, ends


def front_stage(
    devices,
    info,
    taps_ref,
    conv_b_flat,
    dt_bias_flat,
    decay_flat,
    skip_flat,
    gain_flat,
    x_hbm,
    cache_hbm,
    cache_edge_hbm,
    x_proj_hbm,
    dt_proj_hbm,
    mixed_hbm,
    step_hbm,
    proj_ref,
    enter_ref,
    last_edge_ref,
    start_ref,
    param_ref,
    mixed_ref,
    step_ref,
    keep_sems,
    since_ref,
    x_ref,
    cache_ref,
    cache_edge_ref,
    x_proj_ref,
    dt_proj_ref,
    fetch_sems,
    ext,
    mixed_b,
    suffix,
    b_wide,
    halo_ref,
    edge3_ref,
    end_ref,
    sum_ref,
    halo_sems,
    pair_h,
    pair_s,
    own_h,
    own_s,
    z_h,
    z_s,
    x_h,
    x_s,
    half_out,
    half_in,
    pre_sems,
    *spread_refs,
):
    fetches = [
        pltpu.make_async_copy(src, dst, fetch_sems.at[i])
        for i, (src, dst) in enumerate(
            (
                (x_hbm, x_ref),
                (cache_edge_hbm, cache_edge_ref),
                (cache_hbm, cache_ref),
                (x_proj_hbm, x_proj_ref),
                (dt_proj_hbm, dt_proj_ref),
            )
        )
    ]
    for copy in fetches:
        copy.start()
    param_ref[pl.ds(0, 4), :] = taps_ref[...]
    for i, flat in enumerate((conv_b_flat, dt_bias_flat, decay_flat, skip_flat, gain_flat)):
        size = flat.shape[0]
        param_ref[pl.ds(4 + i, 1), pl.ds(0, size)] = flat[...].reshape(1, size)
    conv_w_ref = param_ref.at[pl.ds(0, 4)]
    conv_b_ref = param_ref.at[pl.ds(4, 1)]
    dt_bias_ref = param_ref.at[pl.ds(5, 1)]
    decay_ref = param_ref.at[pl.ds(6, 1)]
    rows, inner = x_ref.shape
    requests = start_ref.shape[0]
    me, core, z, x, partner, z_peers, x_peers = near_devices(devices)
    after, before = (me + 1) % devices, (me + devices - 1) % devices
    greet([("seq", p) for p in [partner, after, before] + z_peers + x_peers])
    halo_copy = send(x_ref.at[pl.ds(rows - 16, 16)], halo_ref, halo_sems, 0, after)
    fetches[0].wait()
    halo_copy.start()
    fetches[1].wait()
    per = len(Spread.scratch(devices, inner, 1, False))
    edge_sum = Spread(devices, inner, 1, False, spread_refs[:per])
    state_sum = Spread(devices, inner, requests, True, spread_refs[per:])
    spot = lax.broadcasted_iota(jnp.int32, (16, inner), 0)
    edge_rows = cache_edge_ref[...].astype(jnp.float32)
    placed = jnp.zeros((16, inner), jnp.float32)
    for r in range(requests):
        take = (info[8 + r] == me) & (info[4 + r] > 0)
        for j in range(EDGE):
            placed = jnp.where((spot == r * EDGE + j) & take, edge_rows[j : j + 1], placed)
    edge_sum.mine[0] = placed.astype(jnp.bfloat16)
    edge_sum.start_core()
    fetches[2].wait()
    for r in range(requests):
        take = (info[8 + r] == me) & (info[4 + r] > 0)
        state_sum.mine[r] = jnp.where(take, cache_ref[...], 0.0).astype(jnp.bfloat16)
    state_sum.start_core()
    ext[pl.ds(16, rows), :] = x_ref[...].astype(jnp.float32)
    fetches[3].wait()
    fetches[4].wait()
    edge_sum.finish_core()
    edge_sum.start_z()
    state_sum.finish_core()
    edge_sum.finish_z()
    edge_sum.start_x()
    state_sum.start_z()
    halo_copy.wait()
    ext[pl.ds(0, 16), :] = halo_ref[...].astype(jnp.float32)
    width = col_block(inner)
    rank = dt_proj_ref.shape[0]
    first_pos = info[16]
    position = first_pos + lax.broadcasted_iota(jnp.int32, (rows, LANES), 0)
    marks = [segment(info, r, rows) for r in range(requests)]
    begin = jnp.zeros((rows, LANES), jnp.int32)
    request = jnp.zeros((rows, LANES), jnp.int32)
    last_begin, last_req = jnp.int32(0), jnp.int32(0)
    for r in range(1, requests):
        reached = position >= marks[r][0]
        begin = jnp.where(reached, marks[r][0], begin)
        request = jnp.where(reached, r, request)
        inside = first_pos + rows - 1 >= marks[r][0]
        last_begin = jnp.where(inside, marks[r][0], last_begin)
        last_req = jnp.where(inside, r, last_req)
    offset = position - begin
    in_last = (position >= last_begin).astype(jnp.float32)
    edge_id = lax.broadcasted_iota(jnp.int32, (rows, 16), 1)
    hots = []
    for lag in (1, 2, 3):
        want = request * EDGE + EDGE + offset - lag
        hit = (edge_id == want[:, :16]) & (offset[:, :16] < lag)
        hots.append(hit.astype(jnp.float32).astype(jnp.bfloat16))

    keep = {}
    for lag in (1, 2, 3):
        keep[lag] = jnp.concatenate([offset] * (width // LANES), axis=1) >= lag
    for first in range(0, inner, width):
        cols = pl.ds(first, width)
        total = conv_b_ref[:, cols] + conv_w_ref[pl.ds(3, 1), cols] * ext[pl.ds(16, rows), cols]
        for lag in (1, 2, 3):
            near = ext[pl.ds(16 - lag, rows), cols]
            row = jnp.where(keep[lag], near, 0.0)
            total = total + conv_w_ref[pl.ds(3 - lag, 1), cols] * row
        suffix[:, cols] = total
    edge_sum.finish_x()
    edge_sum.start_core2()
    edge_sum.finish_core2(edge3_ref)
    edge_ref = edge3_ref.at[0]
    hot = jnp.concatenate(hots * 3, axis=1)
    for first in range(0, inner, width):
        cols = pl.ds(first, width)
        edges = edge_ref[:, cols].astype(jnp.float32)
        far = jnp.concatenate(
            [conv_w_ref[pl.ds(3 - lag, 1), cols] * edges for lag in (1, 2, 3)], axis=0
        )
        high = far.astype(jnp.bfloat16)
        rest = far - high.astype(jnp.float32)
        mid = rest.astype(jnp.bfloat16)
        low = (rest - mid.astype(jnp.float32)).astype(jnp.bfloat16)
        far = jnp.concatenate([high, mid, low], axis=0)
        total = suffix[:, cols] + jnp.dot(hot, far, preferred_element_type=jnp.float32)
        mixed = (total / (1.0 + jnp.exp(-total))).astype(jnp.bfloat16)
        mixed_b[:, cols] = mixed
        mixed_ref[:, cols] = mixed.astype(jnp.float32)

    state_sum.finish_z()
    state_sum.start_x()
    keep_mixed = pltpu.make_async_copy(mixed_ref, mixed_hbm, keep_sems.at[0])
    keep_mixed.start()
    proj = lax.dot_general(
        mixed_b[...],
        x_proj_ref[...],
        (((1,), (1,)), ((), ())),
        preferred_element_type=jnp.float32,
    )
    proj_ref[...] = proj
    for s in range(STATE):
        b_wide[s] = jnp.broadcast_to(proj[:, rank + s : rank + s + 1], (rows, LANES))
    dt_low = proj[:, :rank].astype(jnp.bfloat16)
    row_id = lax.broadcasted_iota(jnp.int32, (rows, rows), 0)
    col_id = lax.broadcasted_iota(jnp.int32, (rows, rows), 1)
    later = (col_id > row_id).astype(jnp.bfloat16)
    for first in range(0, inner, width):
        cols = pl.ds(first, width)
        v = jnp.dot(dt_low, dt_proj_ref[:, cols], preferred_element_type=jnp.float32)
        v = v + dt_bias_ref[:, cols]
        step = jnp.maximum(v, 0.0) + jnp.log1p(jnp.exp(-jnp.abs(v)))
        step_ref[:, cols] = step
        high = step.astype(jnp.bfloat16)
        rest = step - high.astype(jnp.float32)
        mid = rest.astype(jnp.bfloat16)
        low = (rest - mid.astype(jnp.float32)).astype(jnp.bfloat16)
        after = (
            jnp.dot(later, high, preferred_element_type=jnp.float32)
            + jnp.dot(later, mid, preferred_element_type=jnp.float32)
            + jnp.dot(later, low, preferred_element_type=jnp.float32)
        )
        suffix[:, cols] = after

    keep_step = pltpu.make_async_copy(step_ref, step_hbm, keep_sems.at[1])
    keep_step.start()
    state_sum.finish_x()
    state_sum.start_z2()
    starts_here = (last_begin >= first_pos).astype(jnp.int32)
    flag = jnp.full((1, LANES), starts_here, jnp.int32).astype(jnp.float32)
    power = (lax.broadcasted_iota(jnp.int32, (STATE, LANES), 0) + 1).astype(jnp.float32)

    def one_tile(j, carry):
        cols = pl.ds(pl.multiple_of(j * LANES, LANES), LANES)
        rate = decay_ref[:, cols]
        acc = [jnp.zeros((8, LANES), jnp.float32) for _ in range(STATE)]
        since = jnp.zeros((8, LANES), jnp.float32)
        for tile in range(rows // 8):
            here = pl.ds(tile * 8, 8)
            fade = jnp.exp(-rate * suffix[here, cols])
            step = step_ref[here, cols] * in_last[tile * 8 : tile * 8 + 8]
            since = since + step
            push = step * mixed_ref[here, cols]
            for s in range(STATE):
                push = push * fade
                acc[s] = acc[s] + push * b_wide[s, here, :]
        ends = jnp.concatenate([jnp.sum(a, axis=0, keepdims=True) for a in acc], axis=0)
        end_ref[:, cols] = ends
        since = jnp.sum(since, axis=0, keepdims=True)
        since_ref[:, cols] = since
        sum_ref[:, cols] = jnp.where(flag > 0.5, FAR, since)
        return carry

    def one_seed(j, carry):
        cols = pl.ds(pl.multiple_of(j * LANES, LANES), LANES)
        rate = decay_ref[:, cols]
        since = since_ref[:, cols]
        seed = jnp.exp(-(rate * since) * power) * start_ref[last_req, :, cols].astype(jnp.float32)
        end_ref[:, cols] = end_ref[:, cols] + flag * seed
        return carry

    lax.fori_loop(0, inner // LANES, one_tile, 0)
    state_sum.finish_z2()
    state_sum.start_core2()
    state_sum.finish_core2(start_ref)
    lax.fori_loop(0, inner // LANES, one_seed, 0)
    power16 = (lax.broadcasted_iota(jnp.int32, (STATE, LANES), 0) + 1).astype(jnp.float32)
    half = half_width(inner)
    tiles = half // LANES
    base = core * (inner - half)
    own_h[...] = end_ref[...].astype(jnp.bfloat16)
    for j in range(inner // LANES):
        own_s[pl.ds(j, 1), :] = sum_ref[:, pl.ds(j * LANES, LANES)]
    pair = [
        send(own_h, pair_h, pre_sems, 0, partner),
        send(own_s, pair_s, pre_sems, 1, partner),
    ]
    for copy in pair:
        copy.start()
    across, depth = layout_of(devices)
    first_core = core == 0

    def lane(j):
        return pl.ds(pl.multiple_of(base + j * LANES, LANES), LANES)

    def f32(value):
        return value.astype(jnp.float32)

    for copy in pair:
        copy.wait()
    z_sum = []
    for j in range(tiles):
        rate = decay_ref[:, lane(j)] * power16
        mine, theirs = own_h[:, lane(j)], pair_h[:, lane(j)]
        shift = (inner - half) // LANES
        s_mine = jnp.where(first_core, own_s[j : j + 1], own_s[j + shift : j + shift + 1])
        s_pair = jnp.where(first_core, pair_s[j : j + 1], pair_s[j + shift : j + shift + 1])
        h0 = f32(jnp.where(first_core, f32(mine), f32(theirs)))
        h1 = f32(jnp.where(first_core, f32(theirs), f32(mine)))
        s1 = jnp.where(first_core, s_pair, s_mine)
        z_h[0, :, pl.ds(j * LANES, LANES)] = (jnp.exp(-rate * s1) * h0 + h1).astype(jnp.bfloat16)
        z_s[0, pl.ds(j, 1), :] = s_mine + s_pair
    copies = []
    for d, peer in enumerate(z_peers):
        copies.append(send(z_h.at[0], z_h.at[d + 1], pre_sems, 2 + 2 * d, peer))
        copies.append(send(z_s.at[0], z_s.at[d + 1], pre_sems, 3 + 2 * d, peer))
    for copy in copies:
        copy.start()
    for copy in copies:
        copy.wait()
    prefix = []
    for j in range(tiles):
        cols = pl.ds(j * LANES, LANES)
        rate = decay_ref[:, lane(j)] * power16
        total = jnp.zeros((STATE, LANES), jnp.float32)
        part = jnp.zeros((STATE, LANES), jnp.float32)
        total_s = jnp.zeros((1, LANES), jnp.float32)
        part_s = jnp.zeros((1, LANES), jnp.float32)
        for k in range(depth):
            slot = (z - k + depth) % depth
            s_k = z_s[slot, pl.ds(j, 1), :]
            h_k = f32(z_h[slot, :, cols])
            fade = jnp.exp(-rate * s_k)
            total = fade * total + h_k
            part = jnp.where(k < z, fade * part + h_k, part)
            total_s = total_s + s_k
            part_s = jnp.where(k < z, part_s + s_k, part_s)
        x_h[0, :, cols] = total.astype(jnp.bfloat16)
        x_s[0, pl.ds(j, 1), :] = total_s
        prefix.append((part, part_s))
    copies = []
    first = 2 + 2 * (depth - 1)
    for d, peer in enumerate(x_peers):
        copies.append(send(x_h.at[0], x_h.at[d + 1], pre_sems, first + 2 * d, peer))
        copies.append(send(x_s.at[0], x_s.at[d + 1], pre_sems, first + 1 + 2 * d, peer))
    for copy in copies:
        copy.start()
    for copy in copies:
        copy.wait()
    for j in range(tiles):
        cols = pl.ds(j * LANES, LANES)
        rate = decay_ref[:, lane(j)] * power16
        part = jnp.zeros((STATE, LANES), jnp.float32)
        for k in range(across):
            slot = (x - k + across) % across
            value = jnp.exp(-rate * x_s[slot, pl.ds(j, 1), :]) * part + f32(x_h[slot, :, cols])
            part = jnp.where(k < x, value, part)
        inner_part, inner_s = prefix[j]
        half_out[:, cols] = jnp.exp(-rate * inner_s) * part + inner_part
    last = first + 2 * (across - 1)
    swap = send(half_out, half_in, pre_sems, last, partner)
    swap.start()
    swap.wait()
    enter_ref[:, my_lanes(core, inner)] = half_out[...]
    enter_ref[:, my_lanes(1 - core, inner)] = half_in[...]
    for j in range(inner // LANES):
        cols = pl.ds(j * LANES, LANES)
        rate = decay_ref[:, cols] * power16
        chip = enter_ref[:, cols]
        second = jnp.exp(-rate * pair_s[j : j + 1]) * chip + f32(pair_h[:, cols])
        enter_ref[:, cols] = jnp.where(first_core, chip, second)

    row_of = lax.broadcasted_iota(jnp.int32, (16, LANES), 0)
    from_of = lax.broadcasted_iota(jnp.int32, (16, LANES), 1)
    near_at = jnp.full((16, LANES), -1, jnp.int32)
    far_at = jnp.full((16, LANES), -1, jnp.int32)
    for r in range(requests):
        _, _, high, _, ends = marks[r]
        size = info[r]
        for j in range(EDGE):
            lag = EDGE - 1 - j
            near = jnp.where(ends & (size > lag), high + 15 - lag, -1)
            far = jnp.where(ends & (size <= lag), r * EDGE + EDGE + size - 1 - lag, -1)
            near_at = jnp.where(row_of == r * EDGE + j, near, near_at)
            far_at = jnp.where(row_of == r * EDGE + j, far, far_at)

    def hot_rows(at, count):
        return (from_of[:, :count] == at[:, :count]).astype(jnp.float32).astype(jnp.bfloat16)

    for first in range(0, inner, width):
        cols = pl.ds(first, width)
        last_edge_ref[:, cols] = (
            jnp.dot(hot_rows(near_at - 16, rows), x_ref[:, cols], preferred_element_type=jnp.float32)
            + jnp.dot(hot_rows(near_at, 16), halo_ref[:, cols], preferred_element_type=jnp.float32)
            + jnp.dot(hot_rows(far_at, 16), edge_ref[:, cols], preferred_element_type=jnp.float32)
        )
    keep_mixed.wait()
    keep_step.wait()


def front_call(devices, info, args, rows, inner, proj_width, requests):
    f32, bf16 = jnp.float32, jnp.bfloat16
    across, depth = layout_of(devices)
    half = half_width(inner)
    s_rows = -(-(inner // LANES) // 8) * 8
    return pl.pallas_call(
        functools.partial(front_stage, devices),
        out_shape=(
            jax.ShapeDtypeStruct((rows, inner), f32),
            jax.ShapeDtypeStruct((rows, inner), f32),
            jax.ShapeDtypeStruct((rows, proj_width), f32),
            jax.ShapeDtypeStruct((STATE, inner), f32),
            jax.ShapeDtypeStruct((16, inner), f32),
            jax.ShapeDtypeStruct((requests, STATE, inner), bf16),
            jax.ShapeDtypeStruct((16, inner), f32),
        ),
        in_specs=[sspec()] + [vspec()] * 6 + [hspec()] * (len(args) - 6),
        out_specs=tuple([hspec()] * 2 + [vspec()] * 5),
        scratch_shapes=[
            VMEM((rows, inner), f32),
            VMEM((rows, inner), f32),
            pltpu.SemaphoreType.DMA((2,)),
            VMEM((1, inner), f32),
            VMEM((rows, inner), bf16),
            VMEM((STATE, inner), f32),
            VMEM((EDGE, inner), bf16),
            VMEM((proj_width, inner), bf16),
            VMEM((proj_width - 2 * STATE, inner), bf16),
            pltpu.SemaphoreType.DMA((5,)),
            VMEM((rows + 16, inner), f32),
            VMEM((rows, inner), bf16),
            VMEM((rows, inner), f32),
            VMEM((STATE, rows, LANES), f32),
            VMEM((16, inner), bf16),
            VMEM((1, 16, inner), bf16),
            VMEM((STATE, inner), f32),
            VMEM((1, inner), f32),
            pltpu.SemaphoreType.DMA((2, 1)),
            VMEM((STATE, inner), bf16),
            VMEM((s_rows, LANES), f32),
            VMEM((STATE, inner), bf16),
            VMEM((s_rows, LANES), f32),
            VMEM((depth, STATE, half), bf16),
            VMEM((depth, 16, LANES), f32),
            VMEM((across, STATE, half), bf16),
            VMEM((across, 16, LANES), f32),
            VMEM((STATE, half), f32),
            VMEM((STATE, half), f32),
            pltpu.SemaphoreType.DMA((2, 3 + 2 * (depth + across - 2))),
        ]
        + Spread.scratch(devices, inner, 1, False)
        + Spread.scratch(devices, inner, requests, True),
        compiler_params=pltpu.CompilerParams(
            vmem_limit_bytes=61 << 20, collective_id=0, has_side_effects=True
        ),
        cost_estimate=pl.CostEstimate(
            flops=400_000_000, bytes_accessed=8_000_000, transcendentals=2_000_000
        ),
        name="front_stage",
    )(info, *args)


def row_sums(parts):
    row = lax.broadcasted_iota(jnp.int32, parts[0].shape, 0)
    for step in (4, 2, 1):
        odd = (row // step) % 2 == 1
        joined = []
        for i in range(step):
            a, b = parts[i], parts[i + step]
            keep, move = jnp.where(odd, b, a), jnp.where(odd, a, b)
            moved = pltpu.roll(move, step, 0)
            if step < 4:
                moved = jnp.where(odd, moved, pltpu.roll(move, 8 - step, 0))
            joined.append(keep + moved)
        parts = joined
    return parts[0]


def scan_stage(
    info,
    mixed_hbm,
    step_hbm,
    proj_ref,
    enter_ref,
    start_ref,
    param_ref,
    hidden_hbm,
    out_w_hbm,
    middle_ref,
    normed_ref,
    final_hbm,
    mixed_ref,
    step_ref,
    final_ref,
    block_sems,
    final_sem,
    bc_wide,
    y_ref,
    ssm_b,
    out_w,
    hidden_ref,
    w_sem,
    hidden_sem,
):
    rows, inner = mixed_ref.shape
    width = col_block(inner)
    tiles = width // LANES
    rank = proj_ref.shape[1] - 2 * STATE
    width = col_block(step_ref.shape[1])

    def block_copies(g):
        cols = pl.ds(pl.multiple_of(g * width, LANES), width)
        return (
            pltpu.make_async_copy(
                mixed_hbm.at[:, cols], mixed_ref.at[:, cols], block_sems.at[0, g]
            ),
            pltpu.make_async_copy(step_hbm.at[:, cols], step_ref.at[:, cols], block_sems.at[1, g]),
        )

    for g in range(step_ref.shape[1] // width):
        for copy in block_copies(g):
            copy.start()
    fetch = pltpu.make_async_copy(out_w_hbm, out_w, w_sem)
    fetch.start()
    fetch_hidden = pltpu.make_async_copy(hidden_hbm, hidden_ref, hidden_sem)
    fetch_hidden.start()
    model = hidden_ref.shape[0]
    decay_ref = param_ref.at[pl.ds(6, 1)]
    skip_ref = param_ref.at[pl.ds(7, 1)]

    turned = jnp.transpose(proj_ref[:, rank : rank + 2 * STATE])
    for t in range(rows):
        bc_wide[t] = jnp.broadcast_to(turned[:, t : t + 1], (2 * STATE, LANES))
    final_ref[...] = jnp.zeros_like(final_ref)
    power = (lax.broadcasted_iota(jnp.int32, (8, LANES), 0) + 1).astype(jnp.float32)

    def wide_step(t, i, step, push, fade8, state, rates):
        b_low, b_high = bc_wide[t, 0:8], bc_wide[t, 8:16]
        c_low, c_high = bc_wide[t, 16:24], bc_wide[t, 24:32]
        outs, new = [], []
        for j in range(tiles):
            s_row, p_row, f_row = (
                jnp.broadcast_to(part[j][i : i + 1], (8, LANES)) for part in (step, push, fade8)
            )
            d_low = jnp.exp(s_row * rates[j])
            d_high = d_low * f_row
            low = d_low * state[2 * j] + b_low * p_row
            high = d_high * state[2 * j + 1] + b_high * p_row
            new += [low, high]
            outs.append(c_low * low + c_high * high)
        return outs, tuple(new)

    def one_block(g, carry):
        for copy in block_copies(g):
            copy.wait()
        base = pl.multiple_of(g * width, LANES)
        tile_cols = [pl.ds(pl.multiple_of(base + j * LANES, LANES), LANES) for j in range(tiles)]
        rates = [-decay_ref[:, c] * power for c in tile_cols]
        decays = [decay_ref[:, c] for c in tile_cols]

        def load(row, count):
            step = [step_ref[pl.ds(row, count), c] for c in tile_cols]
            push = [s * mixed_ref[pl.ds(row, count), c] for s, c in zip(step, tile_cols)]
            fade8 = [jnp.exp(-8.0 * (s * d)) for s, d in zip(step, decays)]
            return step, push, fade8

        def eight(block, state, limits=None):
            row = pl.multiple_of(block * 8, 8)
            step, push, fade8 = load(row, 8)
            kept = [[] for _ in range(tiles)]
            for i in range(8):
                outs, new = wide_step(row + i, i, step, push, fade8, state, rates)
                if limits is not None:
                    active = (row + i >= limits[0]) & (row + i < limits[1])
                    new = tuple(jnp.where(active, a, b) for a, b in zip(new, state))
                state = new
                for j in range(tiles):
                    kept[j].append(outs[j])
            for j in range(tiles):
                y = row_sums(kept[j])
                if limits is not None:
                    at = row + lax.broadcasted_iota(jnp.int32, (8, LANES), 0)
                    y = jnp.where(
                        (at >= limits[0]) & (at < limits[1]), y, y_ref[pl.ds(row, 8), tile_cols[j]]
                    )
                y_ref[pl.ds(row, 8), tile_cols[j]] = y
            return state

        for r in range(final_ref.shape[0]):
            _, begin, end, new, ends = segment(info, r, rows)

            @pl.when(end > begin)
            def _():
                state = []
                for c in tile_cols:
                    for half in (pl.ds(0, 8), pl.ds(8, 8)):
                        old = enter_ref[half, c]
                        seed = start_ref[r, half, c].astype(jnp.float32)
                        state.append(jnp.where(new, seed, old))
                state = tuple(state)
                part = functools.partial(eight, limits=(begin, end))
                low, low_up, high = begin // 8, (begin + 7) // 8, end // 8
                state = lax.fori_loop(low, low_up, part, state)
                state = lax.fori_loop(low_up, jnp.maximum(high, low_up), eight, state)
                tail = jnp.where((high >= low_up) & (end % 8 > 0), high + 1, high)
                state = lax.fori_loop(high, tail, part, state)

                @pl.when(ends)
                def _():
                    for j, c in enumerate(tile_cols):
                        final_ref[r, pl.ds(0, 8), c] = state[2 * j]
                        final_ref[r, pl.ds(8, 8), c] = state[2 * j + 1]

        y = y_ref[:, pl.ds(base, width)]
        y = y + skip_ref[:, pl.ds(base, width)] * mixed_ref[:, pl.ds(base, width)]
        ssm_b[:, pl.ds(base, width)] = y.astype(jnp.bfloat16)
        return carry

    lax.fori_loop(0, inner // width, one_block, 0)
    keep_final = pltpu.make_async_copy(final_ref, final_hbm, final_sem)
    keep_final.start()
    fetch.wait()
    fetch_hidden.wait()
    middle = jnp.transpose(hidden_ref[...].astype(jnp.float32))
    for first in range(0, inner, width):
        middle = middle + lax.dot_general(
            ssm_b[:, first : first + width],
            out_w[:, first : first + width],
            (((1,), (1,)), ((), ())),
            preferred_element_type=jnp.float32,
        )
    middle_ref[...] = middle
    scale = lax.rsqrt(jnp.mean(middle * middle, axis=1, keepdims=True) + NORM_EPS)
    normed = (middle * scale * param_ref[8:9, :model]).astype(jnp.bfloat16)
    if normed_ref.shape[1] > model:
        normed_ref[...] = jnp.zeros_like(normed_ref)
    normed_ref[:, :model] = normed
    keep_final.wait()


def scan_call(info, args, out_w, rows, inner, model, requests):
    f32 = jnp.float32
    return pl.pallas_call(
        scan_stage,
        out_shape=(
            jax.ShapeDtypeStruct((rows, model), f32),
            jax.ShapeDtypeStruct((rows, padded(model)), jnp.bfloat16),
            jax.ShapeDtypeStruct((requests, STATE, inner), f32),
        ),
        in_specs=[sspec()] + [hspec()] * 2 + [vspec()] * (len(args) - 3) + [hspec()] * 2,
        out_specs=tuple([vspec()] * 2 + [hspec()]),
        scratch_shapes=[
            VMEM((rows, inner), f32),
            VMEM((rows, inner), f32),
            VMEM((requests, STATE, inner), f32),
            pltpu.SemaphoreType.DMA((2, inner // col_block(inner))),
            pltpu.SemaphoreType.DMA,
            VMEM((rows, 2 * STATE, LANES), f32),
            VMEM((rows, inner), f32),
            VMEM((rows, inner), jnp.bfloat16),
            VMEM((model, inner), jnp.bfloat16),
            VMEM((model, rows), jnp.bfloat16),
            pltpu.SemaphoreType.DMA,
            pltpu.SemaphoreType.DMA,
        ],
        compiler_params=pltpu.CompilerParams(vmem_limit_bytes=61 << 20),
        cost_estimate=pl.CostEstimate(
            flops=1_400_000_000, bytes_accessed=18_000_000, transcendentals=4_000_000
        ),
        name="scan_stage",
    )(info, *args, out_w)


def mlp_stage(
    devices,
    info,
    normed_hbm,
    middle_hbm,
    final_hbm,
    last_edge_hbm,
    gate_hbm,
    up_hbm,
    down_hbm,
    out_ref,
    new_state_ref,
    new_edge_ref,
    normed_ref,
    middle_ref,
    final_ref,
    last_edge_ref,
    gate_w,
    up_w,
    down_w,
    fetch_sems,
    near1,
    near2,
    far,
    out1,
    out2,
    far_out,
    own_out,
    low_in,
    high_in,
    far_in,
    ring_sems,
    full,
    full_edge,
    *spread_refs,
):
    rows, model = middle_ref.shape
    half = rows // 2
    inner = final_ref.shape[2]
    requests = final_ref.shape[0]
    me, _, _, _, partner, z_peers, x_peers = near_devices(devices)
    ring = lax.axis_size("req")
    here = lax.axis_index("req")
    above, below = (here + 1) % ring, (here + ring - 1) % ring
    fetches = [
        pltpu.make_async_copy(src, dst, fetch_sems.at[i])
        for i, (src, dst) in enumerate(
            (
                (normed_hbm, normed_ref),
                (final_hbm, final_ref),
                (last_edge_hbm, last_edge_ref),
                (gate_hbm, gate_w),
                (up_hbm, up_w),
                (down_hbm, down_w),
                (middle_hbm, middle_ref),
            )
        )
    ]
    for copy in fetches:
        copy.start()
    greet(
        [("req", above), ("req", below)] + [("seq", p) for p in [partner] + z_peers + x_peers]
    )

    def hop(src, dst, index, peer):
        return pltpu.make_async_remote_copy(
            src_ref=src,
            dst_ref=dst,
            send_sem=ring_sems.at[0, index],
            recv_sem=ring_sems.at[1, index],
            device_id={"req": peer},
            device_id_type=MESH_ID,
        )

    piece = [pl.ds(i * (half // 2), half // 2) for i in range(4)]
    first, second = pl.ds(0, half), pl.ds(half, half)
    toward = [above, above, below, below]
    out_hops = [hop(normed_ref.at[piece[i]], near1.at[piece[i]], i, toward[i]) for i in range(4)]
    on_hops = [hop(near1.at[piece[i]], far.at[piece[i]], 4 + i, toward[i]) for i in range(4)]
    up_b = hop(normed_ref.at[second], near2.at[first], 8, above)
    down_a = hop(normed_ref.at[first], near2.at[second], 9, below)
    far_hops = [hop(far_out.at[piece[i]], far_in.at[piece[i]], 10 + i, toward[i]) for i in range(4)]
    back_down = hop(out1.at[first], high_in.at[first], 14, below)
    back_up = hop(out1.at[second], low_in.at[second], 15, above)
    swap = [2, 3, 0, 1]
    last_hops = [
        hop(
            out2.at[piece[swap[i]]],
            (low_in if i < 2 else high_in).at[piece[i]],
            16 + i,
            toward[i],
        )
        for i in range(4)
    ]
    order = (0, 2, 1, 3)
    fetches[0].wait()
    for i in order:
        out_hops[i].start()
    per = len(Spread.scratch(devices, inner, 1, False))
    finals = Spread(devices, inner, requests, True, spread_refs[:per])
    edges = Spread(devices, inner, 1, False, spread_refs[per:])
    fetches[1].wait()
    for r in range(requests):
        finals.mine[r] = final_ref[r].astype(jnp.bfloat16)
    finals.start_core()
    fetches[2].wait()
    edges.mine[0] = last_edge_ref[...].astype(jnp.bfloat16)
    edges.start_core()

    def hidden_units(value):
        gate = jnp.dot(value, gate_w[...], preferred_element_type=jnp.float32)
        up = jnp.dot(value, up_w[...], preferred_element_type=jnp.float32)
        hidden = (gate / (1.0 + jnp.exp(-gate)) * up).astype(jnp.bfloat16)
        return lax.dot_general(
            hidden, down_w[...], (((1,), (1,)), ((), ())), preferred_element_type=jnp.float32
        )

    finals.finish_core()
    finals.start_z()
    edges.finish_core()
    for i in order:
        out_hops[i].wait_recv()
        on_hops[i].start()
    up_b.start()
    down_a.start()
    for copy in fetches[3:]:
        copy.wait()
    out1[:, :model] = hidden_units(near1[:, :model]).astype(jnp.bfloat16)
    for i in order:
        on_hops[i].wait_recv()
    far_out[:, :model] = hidden_units(far[:, :model]).astype(jnp.bfloat16)
    for i in order:
        far_hops[i].start()
    finals.finish_z()
    finals.start_x()
    edges.start_z()
    up_b.wait_recv()
    down_a.wait_recv()
    own_out[...] = hidden_units(near2[:, :model])
    for i in order:
        far_hops[i].wait_recv()
        rows_at = piece[swap[i]]
        joined = own_out[rows_at] + far_in[piece[i], :model].astype(jnp.float32)
        out2[rows_at, :model] = joined.astype(jnp.bfloat16)
        last_hops[i].start()
    back_down.start()
    back_up.start()
    finals.finish_x()
    finals.start_z2()
    edges.finish_z()
    edges.start_x()
    own_out[...] = hidden_units(normed_ref[:, :model]) + middle_ref[...]
    finals.finish_z2()
    finals.start_core2()
    edges.finish_x()
    edges.start_core2()
    finals.finish_core2(full)
    state = jnp.zeros((STATE, inner), jnp.float32)
    for r in range(requests):
        state = jnp.where(info[12 + r] == me, full[r].astype(jnp.float32), state)
    new_state_ref[...] = state
    edges.finish_core2(full_edge)
    gathered = full_edge[0].astype(jnp.float32)
    edge = jnp.zeros((EDGE, inner), jnp.float32)
    for r in range(requests):
        owned = info[12 + r] == me
        edge = jnp.where(owned, gathered[r * EDGE : (r + 1) * EDGE], edge)
    new_edge_ref[...] = edge.astype(jnp.bfloat16)
    for i in order:
        last_hops[i].wait_recv()
    back_down.wait_recv()
    back_up.wait_recv()
    total = own_out[...] + low_in[:, :model].astype(jnp.float32)
    total = total + high_in[:, :model].astype(jnp.float32)
    out_ref[...] = jnp.transpose(total).astype(jnp.bfloat16)
    for copy in out_hops + on_hops + far_hops + last_hops + [up_b, down_a, back_down, back_up]:
        copy.wait_send()


def mlp_call(devices, info, args, weights, rows, model, inner, requests):
    f32, bf16 = jnp.float32, jnp.bfloat16
    hidden = weights[0].shape[1]
    wide = padded(model)
    return pl.pallas_call(
        functools.partial(mlp_stage, devices),
        out_shape=(
            jax.ShapeDtypeStruct((model, rows), bf16),
            jax.ShapeDtypeStruct((STATE, inner), f32),
            jax.ShapeDtypeStruct((EDGE, inner), bf16),
        ),
        in_specs=[sspec()] + [hspec()] * (len(args) + len(weights)),
        out_specs=tuple([vspec()] * 3),
        scratch_shapes=[
            VMEM((rows, wide), bf16),
            VMEM((rows, model), f32),
            VMEM((requests, STATE, inner), f32),
            VMEM((16, inner), f32),
            VMEM((model, hidden), bf16),
            VMEM((model, hidden), bf16),
            VMEM((model, hidden), bf16),
            pltpu.SemaphoreType.DMA((7,)),
            VMEM((rows, wide), bf16),
            VMEM((rows, wide), bf16),
            VMEM((rows, wide), bf16),
            VMEM((rows, wide), bf16),
            VMEM((rows, wide), bf16),
            VMEM((rows, wide), bf16),
            VMEM((rows, model), f32),
            VMEM((rows, wide), bf16),
            VMEM((rows, wide), bf16),
            VMEM((rows, wide), bf16),
            pltpu.SemaphoreType.DMA((2, 20)),
            VMEM((requests, 16, inner), bf16),
            VMEM((1, 16, inner), bf16),
        ]
        + Spread.scratch(devices, inner, requests, True)
        + Spread.scratch(devices, inner, 1, False),
        compiler_params=pltpu.CompilerParams(
            vmem_limit_bytes=61 << 20, collective_id=1, has_side_effects=True
        ),
        cost_estimate=pl.CostEstimate(
            flops=7_000_000_000, bytes_accessed=16_000_000, transcendentals=1_000_000
        ),
        name="mlp_stage",
    )(info, *args, *weights)


def handing_stage(*refs):
    count = len(refs) // 2
    for i in range(count):
        refs[count + i][...] = refs[i][...]


def handed(*arrays):
    return pl.pallas_call(
        handing_stage,
        out_shape=tuple(jax.ShapeDtypeStruct(a.shape, a.dtype) for a in arrays),
        in_specs=[vspec()] * len(arrays),
        out_specs=tuple([vspec()] * len(arrays)),
        name="handing_stage",
    )(*arrays)


def shards(
    hidden_in,
    mamba_in,
    conv_weight,
    conv_bias,
    x_proj,
    dt_proj,
    dt_bias,
    decay_rate,
    skip_gain,
    out_proj,
    norm_gain,
    mlp_gate,
    mlp_up,
    mlp_down,
    cache_state,
    cache_edge,
    req_lengths,
    cont_flag,
    cache_source,
    owner_slot,
):
    rows, inner = mamba_in.shape[1:]
    model = hidden_in.shape[2]
    requests = req_lengths.shape[1]
    devices = lax.axis_size("seq")
    place = lax.axis_index("seq")
    info = jnp.concatenate(
        [
            req_lengths[0],
            cont_flag[0],
            cache_source[0],
            owner_slot[0],
            jnp.reshape(place * rows, (1,)).astype(jnp.int32),
        ]
    )
    mixed, step, proj, enter, last_edge, start_state, params = front_call(
        devices,
        info,
        (
            conv_weight,
            conv_bias,
            dt_bias,
            decay_rate,
            skip_gain,
            norm_gain,
            mamba_in[0],
            cache_state[0, 0],
            cache_edge[0, 0],
            x_proj.T,
            dt_proj,
        ),
        rows,
        inner,
        x_proj.shape[1],
        requests,
    )
    middle, normed, finals = scan_call(
        info,
        (mixed, step, proj, enter, start_state, params, hidden_in[0].T),
        out_proj.T,
        rows,
        inner,
        model,
        requests,
    )
    block_out, new_state, new_edge = handed(
        *mlp_call(
            devices,
            info,
            (normed, middle, finals, last_edge),
            (mlp_gate, mlp_up, mlp_down.T),
            rows,
            model,
            inner,
            requests,
        )
    )
    return block_out.T[None], new_state[None, None], new_edge[None, None]


def solution(mesh):
    grouped = P("req", "seq", None)
    slots = P("req", "seq", None, None)
    return jax.shard_map(
        shards,
        mesh=mesh,
        in_specs=(grouped, grouped)
        + (P(),) * 9
        + (P(None, "req"), P(None, "req"), P("req", None), slots, slots)
        + (P("req", None),) * 4,
        out_specs=(grouped, slots, slots),
        check_vma=False,
    )
```

```python
import functools

import jax
import jax.numpy as jnp
from jax import lax
from jax.experimental import pallas as pl
from jax.experimental.pallas import tpu as pltpu
from jax.sharding import PartitionSpec as P

STATE = 16
EDGE = 3
NORM_EPS = 1e-06
LANES = 128
FAR = 1e30
HIGHEST_PREC = lax.Precision.HIGHEST
VMEM = pltpu.VMEM
SMEM = pltpu.SMEM


def vspec():
    return pl.BlockSpec(memory_space=VMEM)


def hspec():
    return pl.BlockSpec(memory_space=pltpu.HBM)


def sspec():
    return pl.BlockSpec(memory_space=SMEM)


def col_block(width):
    return 640 if width % 640 == 0 else LANES


MESH_ID = pl.DeviceIdType.MESH


def layout_of(devices):
    depth = 4 if devices >= 32 else 2
    return devices // (2 * depth), depth


def padded(width):
    return -(-width // LANES) * LANES


def half_width(inner):
    return -(-inner // (2 * LANES)) * LANES


def near_devices(devices):
    across, depth = layout_of(devices)
    me = lax.axis_index("seq")
    core, z, x = me % 2, (me // 2) % depth, me // (2 * depth)
    partner = me + 1 - 2 * core
    z_peers = [x * 2 * depth + ((z + d) % depth) * 2 + core for d in range(1, depth)]
    x_peers = [((x + d) % across) * 2 * depth + z * 2 + core for d in range(1, across)]
    return me, core, z, x, partner, z_peers, x_peers


def my_lanes(core, inner):
    half = half_width(inner)
    return pl.ds(pl.multiple_of(core * (inner - half), LANES), half)


def send(src, dst, sems, index, peer):
    return pltpu.make_async_remote_copy(
        src_ref=src,
        dst_ref=dst,
        send_sem=sems.at[0, index],
        recv_sem=sems.at[1, index],
        device_id={"seq": peer},
        device_id_type=MESH_ID,
    )


def greet(axis_peers):
    barrier = pltpu.get_barrier_semaphore()
    for axis, peer in axis_peers:
        pl.semaphore_signal(barrier, inc=1, device_id={axis: peer}, device_id_type=MESH_ID)
    pl.semaphore_wait(barrier, len(axis_peers))


class Spread:
    def __init__(self, devices, inner, count, split, refs):
        self.devices, self.inner, self.count, self.split = devices, inner, count, split
        self.across, self.depth = layout_of(devices)
        self.part = count // self.depth if split else count
        (
            self.mine,
            self.from_core,
            self.acc,
            self.from_z,
            self.from_x,
            self.from_z2,
            self.other,
            self.sems,
        ) = refs
        _, self.core, self.z, self.x, self.partner, self.z_peers, self.x_peers = near_devices(
            devices
        )
        self.lanes = my_lanes(self.core, inner)
        self.far_lanes = my_lanes(1 - self.core, inner)
        self.copies = []

    @staticmethod
    def scratch(devices, inner, count, split):
        across, depth = layout_of(devices)
        part = count // depth if split else count
        half = half_width(inner)
        b = jnp.bfloat16
        return [
            VMEM((count, 16, inner), b),
            VMEM((count, 16, half), b),
            VMEM((count, 16, half), b),
            VMEM((depth - 1, part, 16, half), b),
            VMEM((across - 1, part, 16, half), b),
            VMEM((depth - 1, part, 16, half), b),
            VMEM((count, 16, half), b),
            pltpu.SemaphoreType.DMA((2, 2 + 2 * (depth - 1) + (across - 1))),
        ]

    def own_part(self, shift=0):
        if not self.split:
            return pl.ds(0, self.part)
        return pl.ds(((self.z + shift) % self.depth) * self.part, self.part)

    def begin(self, copies):
        self.copies = copies
        for copy in copies:
            copy.start()

    def end(self):
        for copy in self.copies:
            copy.wait()

    def start_core(self):
        self.begin(
            [send(self.mine.at[:, :, self.far_lanes], self.from_core, self.sems, 0, self.partner)]
        )

    def finish_core(self):
        self.end()
        total = self.mine[:, :, self.lanes].astype(jnp.float32) + self.from_core[...].astype(
            jnp.float32
        )
        self.acc[...] = total.astype(jnp.bfloat16)

    def start_z(self):
        self.begin(
            [
                send(self.acc.at[self.own_part(d + 1)], self.from_z.at[d], self.sems, 1 + d, peer)
                for d, peer in enumerate(self.z_peers)
            ]
        )

    def finish_z(self):
        self.end()
        here = self.own_part()
        total = self.acc[here].astype(jnp.float32)
        for d in range(self.depth - 1):
            total = total + self.from_z[d].astype(jnp.float32)
        self.acc[here] = total.astype(jnp.bfloat16)

    def start_x(self):
        base = self.depth
        self.begin(
            [
                send(self.acc.at[self.own_part()], self.from_x.at[d], self.sems, base + d, peer)
                for d, peer in enumerate(self.x_peers)
            ]
        )

    def finish_x(self):
        self.end()
        here = self.own_part()
        total = self.acc[here].astype(jnp.float32)
        for d in range(self.across - 1):
            total = total + self.from_x[d].astype(jnp.float32)
        self.acc[here] = total.astype(jnp.bfloat16)

    def start_z2(self):
        if not self.split:
            return
        base = self.depth + self.across - 1
        self.begin(
            [
                send(self.acc.at[self.own_part()], self.from_z2.at[d], self.sems, base + d, peer)
                for d, peer in enumerate(self.z_peers)
            ]
        )

    def finish_z2(self):
        if not self.split:
            return
        self.end()
        for d in range(self.depth - 1):
            self.acc[self.own_part(-(d + 1))] = self.from_z2[d]

    def start_core2(self):
        last = 2 * (self.depth - 1) + self.across
        self.begin([send(self.acc, self.other, self.sems, last, self.partner)])

    def finish_core2(self, out_ref):
        self.end()
        out_ref[:, :, self.lanes] = self.acc[...]
        out_ref[:, :, self.far_lanes] = self.other[...]


def segment(info, r, rows):
    begin = jnp.int32(0)
    for q in range(r):
        begin = begin + info[q]
    end = begin + info[r]
    first = info[16]
    low = jnp.clip(begin - first, 0, rows)
    high = jnp.clip(end - first, 0, rows)
    fresh = begin >= first
    ends = (end > first) & (end <= first + rows)
    return begin, low, high, fresh, ends


def front_stage(
    devices,
    info,
    taps_ref,
    conv_b_flat,
    dt_bias_flat,
    decay_flat,
    skip_flat,
    gain_flat,
    x_hbm,
    cache_hbm,
    cache_edge_hbm,
    x_proj_hbm,
    dt_proj_hbm,
    mixed_hbm,
    step_hbm,
    proj_ref,
    enter_ref,
    last_edge_ref,
    start_ref,
    param_ref,
    mixed_ref,
    step_ref,
    keep_sems,
    since_ref,
    x_ref,
    cache_ref,
    cache_edge_ref,
    x_proj_ref,
    dt_proj_ref,
    fetch_sems,
    ext,
    mixed_b,
    suffix,
    b_wide,
    halo_ref,
    edge3_ref,
    end_ref,
    sum_ref,
    halo_sems,
    pair_h,
    pair_s,
    own_h,
    own_s,
    z_h,
    z_s,
    x_h,
    x_s,
    half_out,
    half_in,
    pre_sems,
    *spread_refs,
):
    fetches = [
        pltpu.make_async_copy(src, dst, fetch_sems.at[i])
        for i, (src, dst) in enumerate(
            (
                (x_hbm, x_ref),
                (cache_edge_hbm, cache_edge_ref),
                (cache_hbm, cache_ref),
                (x_proj_hbm, x_proj_ref),
                (dt_proj_hbm, dt_proj_ref),
            )
        )
    ]
    for copy in fetches:
        copy.start()
    param_ref[pl.ds(0, 4), :] = taps_ref[...]
    for i, flat in enumerate((conv_b_flat, dt_bias_flat, decay_flat, skip_flat, gain_flat)):
        size = flat.shape[0]
        param_ref[pl.ds(4 + i, 1), pl.ds(0, size)] = flat[...].reshape(1, size)
    conv_w_ref = param_ref.at[pl.ds(0, 4)]
    conv_b_ref = param_ref.at[pl.ds(4, 1)]
    dt_bias_ref = param_ref.at[pl.ds(5, 1)]
    decay_ref = param_ref.at[pl.ds(6, 1)]
    rows, inner = x_ref.shape
    requests = start_ref.shape[0]
    me, core, z, x, partner, z_peers, x_peers = near_devices(devices)
    after, before = (me + 1) % devices, (me + devices - 1) % devices
    greet([("seq", p) for p in [partner, after, before] + z_peers + x_peers])
    halo_copy = send(x_ref.at[pl.ds(rows - 16, 16)], halo_ref, halo_sems, 0, after)
    fetches[0].wait()
    halo_copy.start()
    fetches[1].wait()
    per = len(Spread.scratch(devices, inner, 1, False))
    edge_sum = Spread(devices, inner, 1, False, spread_refs[:per])
    state_sum = Spread(devices, inner, requests, True, spread_refs[per:])
    spot = lax.broadcasted_iota(jnp.int32, (16, inner), 0)
    edge_rows = cache_edge_ref[...].astype(jnp.float32)
    placed = jnp.zeros((16, inner), jnp.float32)
    for r in range(requests):
        take = (info[8 + r] == me) & (info[4 + r] > 0)
        for j in range(EDGE):
            placed = jnp.where((spot == r * EDGE + j) & take, edge_rows[j : j + 1], placed)
    edge_sum.mine[0] = placed.astype(jnp.bfloat16)
    edge_sum.start_core()
    fetches[2].wait()
    for r in range(requests):
        take = (info[8 + r] == me) & (info[4 + r] > 0)
        state_sum.mine[r] = jnp.where(take, cache_ref[...], 0.0).astype(jnp.bfloat16)
    state_sum.start_core()
    ext[pl.ds(16, rows), :] = x_ref[...].astype(jnp.float32)
    fetches[3].wait()
    fetches[4].wait()
    edge_sum.finish_core()
    edge_sum.start_z()
    state_sum.finish_core()
    edge_sum.finish_z()
    edge_sum.start_x()
    state_sum.start_z()
    halo_copy.wait()
    ext[pl.ds(0, 16), :] = halo_ref[...].astype(jnp.float32)
    width = col_block(inner)
    rank = dt_proj_ref.shape[0]
    first_pos = info[16]
    position = first_pos + lax.broadcasted_iota(jnp.int32, (rows, LANES), 0)
    marks = [segment(info, r, rows) for r in range(requests)]
    begin = jnp.zeros((rows, LANES), jnp.int32)
    request = jnp.zeros((rows, LANES), jnp.int32)
    last_begin, last_req = jnp.int32(0), jnp.int32(0)
    for r in range(1, requests):
        reached = position >= marks[r][0]
        begin = jnp.where(reached, marks[r][0], begin)
        request = jnp.where(reached, r, request)
        inside = first_pos + rows - 1 >= marks[r][0]
        last_begin = jnp.where(inside, marks[r][0], last_begin)
        last_req = jnp.where(inside, r, last_req)
    offset = position - begin
    in_last = (position >= last_begin).astype(jnp.float32)
    edge_id = lax.broadcasted_iota(jnp.int32, (rows, 16), 1)
    hots = []
    for lag in (1, 2, 3):
        want = request * EDGE + EDGE + offset - lag
        hit = (edge_id == want[:, :16]) & (offset[:, :16] < lag)
        hots.append(hit.astype(jnp.float32).astype(jnp.bfloat16))

    keep = {}
    for lag in (1, 2, 3):
        keep[lag] = jnp.concatenate([offset] * (width // LANES), axis=1) >= lag
    for first in range(0, inner, width):
        cols = pl.ds(first, width)
        total = conv_b_ref[:, cols] + conv_w_ref[pl.ds(3, 1), cols] * ext[pl.ds(16, rows), cols]
        for lag in (1, 2, 3):
            near = ext[pl.ds(16 - lag, rows), cols]
            row = jnp.where(keep[lag], near, 0.0)
            total = total + conv_w_ref[pl.ds(3 - lag, 1), cols] * row
        suffix[:, cols] = total
    edge_sum.finish_x()
    edge_sum.start_core2()
    state_sum.finish_z()
    state_sum.start_x()
    edge_sum.finish_core2(edge3_ref)
    edge_ref = edge3_ref.at[0]
    hot = jnp.concatenate(hots * 3, axis=1)
    for first in range(0, inner, width):
        cols = pl.ds(first, width)
        edges = edge_ref[:, cols].astype(jnp.float32)
        far = jnp.concatenate(
            [conv_w_ref[pl.ds(3 - lag, 1), cols] * edges for lag in (1, 2, 3)], axis=0
        )
        high = far.astype(jnp.bfloat16)
        rest = far - high.astype(jnp.float32)
        mid = rest.astype(jnp.bfloat16)
        low = (rest - mid.astype(jnp.float32)).astype(jnp.bfloat16)
        far = jnp.concatenate([high, mid, low], axis=0)
        total = suffix[:, cols] + jnp.dot(hot, far, preferred_element_type=jnp.float32)
        mixed = (total / (1.0 + jnp.exp(-total))).astype(jnp.bfloat16)
        mixed_b[:, cols] = mixed
        mixed_ref[:, cols] = mixed.astype(jnp.float32)

    keep_mixed = pltpu.make_async_copy(mixed_ref, mixed_hbm, keep_sems.at[0])
    keep_mixed.start()
    proj = lax.dot_general(
        mixed_b[...],
        x_proj_ref[...],
        (((1,), (1,)), ((), ())),
        preferred_element_type=jnp.float32,
    )
    proj_ref[...] = proj
    for s in range(STATE):
        b_wide[s] = jnp.broadcast_to(proj[:, rank + s : rank + s + 1], (rows, LANES))
    dt_low = proj[:, :rank].astype(jnp.bfloat16)
    row_id = lax.broadcasted_iota(jnp.int32, (rows, rows), 0)
    col_id = lax.broadcasted_iota(jnp.int32, (rows, rows), 1)
    later = (col_id > row_id).astype(jnp.bfloat16)
    for first in range(0, inner, width):
        cols = pl.ds(first, width)
        v = jnp.dot(dt_low, dt_proj_ref[:, cols], preferred_element_type=jnp.float32)
        v = v + dt_bias_ref[:, cols]
        step = jnp.maximum(v, 0.0) + jnp.log1p(jnp.exp(-jnp.abs(v)))
        step_ref[:, cols] = step
        high = step.astype(jnp.bfloat16)
        rest = step - high.astype(jnp.float32)
        mid = rest.astype(jnp.bfloat16)
        low = (rest - mid.astype(jnp.float32)).astype(jnp.bfloat16)
        after = (
            jnp.dot(later, high, preferred_element_type=jnp.float32)
            + jnp.dot(later, mid, preferred_element_type=jnp.float32)
            + jnp.dot(later, low, preferred_element_type=jnp.float32)
        )
        suffix[:, cols] = after

    keep_step = pltpu.make_async_copy(step_ref, step_hbm, keep_sems.at[1])
    keep_step.start()
    state_sum.finish_x()
    state_sum.start_z2()
    starts_here = (last_begin >= first_pos).astype(jnp.int32)
    flag = jnp.full((1, LANES), starts_here, jnp.int32).astype(jnp.float32)
    power = (lax.broadcasted_iota(jnp.int32, (STATE, LANES), 0) + 1).astype(jnp.float32)

    def one_tile(j, carry):
        cols = pl.ds(pl.multiple_of(j * LANES, LANES), LANES)
        rate = decay_ref[:, cols]
        acc = [jnp.zeros((8, LANES), jnp.float32) for _ in range(STATE)]
        since = jnp.zeros((8, LANES), jnp.float32)
        for tile in range(rows // 8):
            here = pl.ds(tile * 8, 8)
            fade = jnp.exp(-rate * suffix[here, cols])
            step = step_ref[here, cols] * in_last[tile * 8 : tile * 8 + 8]
            since = since + step
            push = step * mixed_ref[here, cols]
            for s in range(STATE):
                push = push * fade
                acc[s] = acc[s] + push * b_wide[s, here, :]
        ends = jnp.concatenate([jnp.sum(a, axis=0, keepdims=True) for a in acc], axis=0)
        end_ref[:, cols] = ends
        since = jnp.sum(since, axis=0, keepdims=True)
        since_ref[:, cols] = since
        sum_ref[:, cols] = jnp.where(flag > 0.5, FAR, since)
        return carry

    def one_seed(j, carry):
        cols = pl.ds(pl.multiple_of(j * LANES, LANES), LANES)
        rate = decay_ref[:, cols]
        since = since_ref[:, cols]
        seed = jnp.exp(-(rate * since) * power) * start_ref[last_req, :, cols].astype(jnp.float32)
        end_ref[:, cols] = end_ref[:, cols] + flag * seed
        return carry

    lax.fori_loop(0, inner // LANES, one_tile, 0)
    state_sum.finish_z2()
    state_sum.start_core2()
    state_sum.finish_core2(start_ref)
    lax.fori_loop(0, inner // LANES, one_seed, 0)
    power16 = (lax.broadcasted_iota(jnp.int32, (STATE, LANES), 0) + 1).astype(jnp.float32)
    half = half_width(inner)
    tiles = half // LANES
    base = core * (inner - half)
    own_h[...] = end_ref[...].astype(jnp.bfloat16)
    for j in range(inner // LANES):
        own_s[pl.ds(j, 1), :] = sum_ref[:, pl.ds(j * LANES, LANES)]
    pair = [
        send(own_h, pair_h, pre_sems, 0, partner),
        send(own_s, pair_s, pre_sems, 1, partner),
    ]
    for copy in pair:
        copy.start()
    across, depth = layout_of(devices)
    first_core = core == 0

    def lane(j):
        return pl.ds(pl.multiple_of(base + j * LANES, LANES), LANES)

    def f32(value):
        return value.astype(jnp.float32)

    for copy in pair:
        copy.wait()
    z_sum = []
    for j in range(tiles):
        rate = decay_ref[:, lane(j)] * power16
        mine, theirs = own_h[:, lane(j)], pair_h[:, lane(j)]
        shift = (inner - half) // LANES
        s_mine = jnp.where(first_core, own_s[j : j + 1], own_s[j + shift : j + shift + 1])
        s_pair = jnp.where(first_core, pair_s[j : j + 1], pair_s[j + shift : j + shift + 1])
        h0 = f32(jnp.where(first_core, f32(mine), f32(theirs)))
        h1 = f32(jnp.where(first_core, f32(theirs), f32(mine)))
        s1 = jnp.where(first_core, s_pair, s_mine)
        z_h[0, :, pl.ds(j * LANES, LANES)] = (jnp.exp(-rate * s1) * h0 + h1).astype(jnp.bfloat16)
        z_s[0, pl.ds(j, 1), :] = s_mine + s_pair
    copies = []
    for d, peer in enumerate(z_peers):
        copies.append(send(z_h.at[0], z_h.at[d + 1], pre_sems, 2 + 2 * d, peer))
        copies.append(send(z_s.at[0], z_s.at[d + 1], pre_sems, 3 + 2 * d, peer))
    for copy in copies:
        copy.start()
    for copy in copies:
        copy.wait()
    prefix = []
    for j in range(tiles):
        cols = pl.ds(j * LANES, LANES)
        rate = decay_ref[:, lane(j)] * power16
        total = jnp.zeros((STATE, LANES), jnp.float32)
        part = jnp.zeros((STATE, LANES), jnp.float32)
        total_s = jnp.zeros((1, LANES), jnp.float32)
        part_s = jnp.zeros((1, LANES), jnp.float32)
        for k in range(depth):
            slot = (z - k + depth) % depth
            s_k = z_s[slot, pl.ds(j, 1), :]
            h_k = f32(z_h[slot, :, cols])
            fade = jnp.exp(-rate * s_k)
            total = fade * total + h_k
            part = jnp.where(k < z, fade * part + h_k, part)
            total_s = total_s + s_k
            part_s = jnp.where(k < z, part_s + s_k, part_s)
        x_h[0, :, cols] = total.astype(jnp.bfloat16)
        x_s[0, pl.ds(j, 1), :] = total_s
        prefix.append((part, part_s))
    copies = []
    first = 2 + 2 * (depth - 1)
    for d, peer in enumerate(x_peers):
        copies.append(send(x_h.at[0], x_h.at[d + 1], pre_sems, first + 2 * d, peer))
        copies.append(send(x_s.at[0], x_s.at[d + 1], pre_sems, first + 1 + 2 * d, peer))
    for copy in copies:
        copy.start()
    for copy in copies:
        copy.wait()
    for j in range(tiles):
        cols = pl.ds(j * LANES, LANES)
        rate = decay_ref[:, lane(j)] * power16
        part = jnp.zeros((STATE, LANES), jnp.float32)
        for k in range(across):
            slot = (x - k + across) % across
            value = jnp.exp(-rate * x_s[slot, pl.ds(j, 1), :]) * part + f32(x_h[slot, :, cols])
            part = jnp.where(k < x, value, part)
        inner_part, inner_s = prefix[j]
        half_out[:, cols] = jnp.exp(-rate * inner_s) * part + inner_part
    last = first + 2 * (across - 1)
    swap = send(half_out, half_in, pre_sems, last, partner)
    swap.start()
    swap.wait()
    enter_ref[:, my_lanes(core, inner)] = half_out[...]
    enter_ref[:, my_lanes(1 - core, inner)] = half_in[...]
    for j in range(inner // LANES):
        cols = pl.ds(j * LANES, LANES)
        rate = decay_ref[:, cols] * power16
        chip = enter_ref[:, cols]
        second = jnp.exp(-rate * pair_s[j : j + 1]) * chip + f32(pair_h[:, cols])
        enter_ref[:, cols] = jnp.where(first_core, chip, second)

    row_of = lax.broadcasted_iota(jnp.int32, (16, LANES), 0)
    from_of = lax.broadcasted_iota(jnp.int32, (16, LANES), 1)
    near_at = jnp.full((16, LANES), -1, jnp.int32)
    far_at = jnp.full((16, LANES), -1, jnp.int32)
    for r in range(requests):
        _, _, high, _, ends = marks[r]
        size = info[r]
        for j in range(EDGE):
            lag = EDGE - 1 - j
            near = jnp.where(ends & (size > lag), high + 15 - lag, -1)
            far = jnp.where(ends & (size <= lag), r * EDGE + EDGE + size - 1 - lag, -1)
            near_at = jnp.where(row_of == r * EDGE + j, near, near_at)
            far_at = jnp.where(row_of == r * EDGE + j, far, far_at)

    def hot_rows(at, count):
        return (from_of[:, :count] == at[:, :count]).astype(jnp.float32).astype(jnp.bfloat16)

    for first in range(0, inner, width):
        cols = pl.ds(first, width)
        last_edge_ref[:, cols] = (
            jnp.dot(hot_rows(near_at - 16, rows), x_ref[:, cols], preferred_element_type=jnp.float32)
            + jnp.dot(hot_rows(near_at, 16), halo_ref[:, cols], preferred_element_type=jnp.float32)
            + jnp.dot(hot_rows(far_at, 16), edge_ref[:, cols], preferred_element_type=jnp.float32)
        )
    keep_mixed.wait()
    keep_step.wait()


def front_call(devices, info, args, rows, inner, proj_width, requests):
    f32, bf16 = jnp.float32, jnp.bfloat16
    across, depth = layout_of(devices)
    half = half_width(inner)
    s_rows = -(-(inner // LANES) // 8) * 8
    return pl.pallas_call(
        functools.partial(front_stage, devices),
        out_shape=(
            jax.ShapeDtypeStruct((rows, inner), f32),
            jax.ShapeDtypeStruct((rows, inner), f32),
            jax.ShapeDtypeStruct((rows, proj_width), f32),
            jax.ShapeDtypeStruct((STATE, inner), f32),
            jax.ShapeDtypeStruct((16, inner), f32),
            jax.ShapeDtypeStruct((requests, STATE, inner), bf16),
            jax.ShapeDtypeStruct((16, inner), f32),
        ),
        in_specs=[sspec()] + [vspec()] * 6 + [hspec()] * (len(args) - 6),
        out_specs=tuple([hspec()] * 2 + [vspec()] * 5),
        scratch_shapes=[
            VMEM((rows, inner), f32),
            VMEM((rows, inner), f32),
            pltpu.SemaphoreType.DMA((2,)),
            VMEM((1, inner), f32),
            VMEM((rows, inner), bf16),
            VMEM((STATE, inner), f32),
            VMEM((EDGE, inner), bf16),
            VMEM((proj_width, inner), bf16),
            VMEM((proj_width - 2 * STATE, inner), bf16),
            pltpu.SemaphoreType.DMA((5,)),
            VMEM((rows + 16, inner), f32),
            VMEM((rows, inner), bf16),
            VMEM((rows, inner), f32),
            VMEM((STATE, rows, LANES), f32),
            VMEM((16, inner), bf16),
            VMEM((1, 16, inner), bf16),
            VMEM((STATE, inner), f32),
            VMEM((1, inner), f32),
            pltpu.SemaphoreType.DMA((2, 1)),
            VMEM((STATE, inner), bf16),
            VMEM((s_rows, LANES), f32),
            VMEM((STATE, inner), bf16),
            VMEM((s_rows, LANES), f32),
            VMEM((depth, STATE, half), bf16),
            VMEM((depth, 16, LANES), f32),
            VMEM((across, STATE, half), bf16),
            VMEM((across, 16, LANES), f32),
            VMEM((STATE, half), f32),
            VMEM((STATE, half), f32),
            pltpu.SemaphoreType.DMA((2, 3 + 2 * (depth + across - 2))),
        ]
        + Spread.scratch(devices, inner, 1, False)
        + Spread.scratch(devices, inner, requests, True),
        compiler_params=pltpu.CompilerParams(
            vmem_limit_bytes=61 << 20, collective_id=0, has_side_effects=True
        ),
        cost_estimate=pl.CostEstimate(
            flops=400_000_000, bytes_accessed=8_000_000, transcendentals=2_000_000
        ),
        name="front_stage",
    )(info, *args)


def row_sums(parts):
    row = lax.broadcasted_iota(jnp.int32, parts[0].shape, 0)
    for step in (4, 2, 1):
        odd = (row // step) % 2 == 1
        joined = []
        for i in range(step):
            a, b = parts[i], parts[i + step]
            keep, move = jnp.where(odd, b, a), jnp.where(odd, a, b)
            moved = pltpu.roll(move, step, 0)
            if step < 4:
                moved = jnp.where(odd, moved, pltpu.roll(move, 8 - step, 0))
            joined.append(keep + moved)
        parts = joined
    return parts[0]


def scan_stage(
    info,
    mixed_hbm,
    step_hbm,
    proj_ref,
    enter_ref,
    start_ref,
    param_ref,
    hidden_hbm,
    out_w_hbm,
    middle_ref,
    normed_ref,
    final_hbm,
    mixed_ref,
    step_ref,
    final_ref,
    block_sems,
    final_sem,
    bc_wide,
    y_ref,
    ssm_b,
    out_w,
    hidden_ref,
    w_sem,
    hidden_sem,
):
    rows, inner = mixed_ref.shape
    width = col_block(inner)
    tiles = width // LANES
    rank = proj_ref.shape[1] - 2 * STATE
    width = col_block(step_ref.shape[1])

    def block_copies(g):
        cols = pl.ds(pl.multiple_of(g * width, LANES), width)
        return (
            pltpu.make_async_copy(
                mixed_hbm.at[:, cols], mixed_ref.at[:, cols], block_sems.at[0, g]
            ),
            pltpu.make_async_copy(step_hbm.at[:, cols], step_ref.at[:, cols], block_sems.at[1, g]),
        )

    for g in range(step_ref.shape[1] // width):
        for copy in block_copies(g):
            copy.start()
    fetch = pltpu.make_async_copy(out_w_hbm, out_w, w_sem)
    fetch.start()
    fetch_hidden = pltpu.make_async_copy(hidden_hbm, hidden_ref, hidden_sem)
    fetch_hidden.start()
    model = hidden_ref.shape[0]
    decay_ref = param_ref.at[pl.ds(6, 1)]
    skip_ref = param_ref.at[pl.ds(7, 1)]

    turned = jnp.transpose(proj_ref[:, rank : rank + 2 * STATE])
    for t in range(rows):
        bc_wide[t] = jnp.broadcast_to(turned[:, t : t + 1], (2 * STATE, LANES))
    final_ref[...] = jnp.zeros_like(final_ref)
    power = (lax.broadcasted_iota(jnp.int32, (8, LANES), 0) + 1).astype(jnp.float32)

    def wide_step(t, i, step, push, fade8, state, rates):
        b_low, b_high = bc_wide[t, 0:8], bc_wide[t, 8:16]
        c_low, c_high = bc_wide[t, 16:24], bc_wide[t, 24:32]
        outs, new = [], []
        for j in range(tiles):
            s_row, p_row, f_row = (
                jnp.broadcast_to(part[j][i : i + 1], (8, LANES)) for part in (step, push, fade8)
            )
            d_low = jnp.exp(s_row * rates[j])
            d_high = d_low * f_row
            low = d_low * state[2 * j] + b_low * p_row
            high = d_high * state[2 * j + 1] + b_high * p_row
            new += [low, high]
            outs.append(c_low * low + c_high * high)
        return outs, tuple(new)

    def one_block(g, carry):
        for copy in block_copies(g):
            copy.wait()
        base = pl.multiple_of(g * width, LANES)
        tile_cols = [pl.ds(pl.multiple_of(base + j * LANES, LANES), LANES) for j in range(tiles)]
        rates = [-decay_ref[:, c] * power for c in tile_cols]
        decays = [decay_ref[:, c] for c in tile_cols]

        def load(row, count):
            step = [step_ref[pl.ds(row, count), c] for c in tile_cols]
            push = [s * mixed_ref[pl.ds(row, count), c] for s, c in zip(step, tile_cols)]
            fade8 = [jnp.exp(-8.0 * (s * d)) for s, d in zip(step, decays)]
            return step, push, fade8

        def eight(block, state, limits=None):
            row = pl.multiple_of(block * 8, 8)
            step, push, fade8 = load(row, 8)
            kept = [[] for _ in range(tiles)]
            for i in range(8):
                outs, new = wide_step(row + i, i, step, push, fade8, state, rates)
                if limits is not None:
                    active = (row + i >= limits[0]) & (row + i < limits[1])
                    new = tuple(jnp.where(active, a, b) for a, b in zip(new, state))
                state = new
                for j in range(tiles):
                    kept[j].append(outs[j])
            for j in range(tiles):
                y = row_sums(kept[j])
                if limits is not None:
                    at = row + lax.broadcasted_iota(jnp.int32, (8, LANES), 0)
                    y = jnp.where(
                        (at >= limits[0]) & (at < limits[1]), y, y_ref[pl.ds(row, 8), tile_cols[j]]
                    )
                y_ref[pl.ds(row, 8), tile_cols[j]] = y
            return state

        for r in range(final_ref.shape[0]):
            _, begin, end, new, ends = segment(info, r, rows)

            @pl.when(end > begin)
            def _():
                state = []
                for c in tile_cols:
                    for half in (pl.ds(0, 8), pl.ds(8, 8)):
                        old = enter_ref[half, c]
                        seed = start_ref[r, half, c].astype(jnp.float32)
                        state.append(jnp.where(new, seed, old))
                state = tuple(state)
                part = functools.partial(eight, limits=(begin, end))
                low, low_up, high = begin // 8, (begin + 7) // 8, end // 8
                state = lax.fori_loop(low, low_up, part, state)
                state = lax.fori_loop(low_up, jnp.maximum(high, low_up), eight, state)
                tail = jnp.where((high >= low_up) & (end % 8 > 0), high + 1, high)
                state = lax.fori_loop(high, tail, part, state)

                @pl.when(ends)
                def _():
                    for j, c in enumerate(tile_cols):
                        final_ref[r, pl.ds(0, 8), c] = state[2 * j]
                        final_ref[r, pl.ds(8, 8), c] = state[2 * j + 1]

        y = y_ref[:, pl.ds(base, width)]
        y = y + skip_ref[:, pl.ds(base, width)] * mixed_ref[:, pl.ds(base, width)]
        ssm_b[:, pl.ds(base, width)] = y.astype(jnp.bfloat16)
        return carry

    lax.fori_loop(0, inner // width, one_block, 0)
    keep_final = pltpu.make_async_copy(final_ref, final_hbm, final_sem)
    keep_final.start()
    fetch.wait()
    fetch_hidden.wait()
    middle = jnp.transpose(hidden_ref[...].astype(jnp.float32))
    for first in range(0, inner, width):
        middle = middle + lax.dot_general(
            ssm_b[:, first : first + width],
            out_w[:, first : first + width],
            (((1,), (1,)), ((), ())),
            preferred_element_type=jnp.float32,
        )
    middle_ref[...] = middle
    scale = lax.rsqrt(jnp.mean(middle * middle, axis=1, keepdims=True) + NORM_EPS)
    normed = (middle * scale * param_ref[8:9, :model]).astype(jnp.bfloat16)
    if normed_ref.shape[1] > model:
        normed_ref[...] = jnp.zeros_like(normed_ref)
    normed_ref[:, :model] = normed
    keep_final.wait()


def scan_call(info, args, out_w, rows, inner, model, requests):
    f32 = jnp.float32
    return pl.pallas_call(
        scan_stage,
        out_shape=(
            jax.ShapeDtypeStruct((rows, model), f32),
            jax.ShapeDtypeStruct((rows, padded(model)), jnp.bfloat16),
            jax.ShapeDtypeStruct((requests, STATE, inner), f32),
        ),
        in_specs=[sspec()] + [hspec()] * 2 + [vspec()] * (len(args) - 3) + [hspec()] * 2,
        out_specs=tuple([vspec()] * 2 + [hspec()]),
        scratch_shapes=[
            VMEM((rows, inner), f32),
            VMEM((rows, inner), f32),
            VMEM((requests, STATE, inner), f32),
            pltpu.SemaphoreType.DMA((2, inner // col_block(inner))),
            pltpu.SemaphoreType.DMA,
            VMEM((rows, 2 * STATE, LANES), f32),
            VMEM((rows, inner), f32),
            VMEM((rows, inner), jnp.bfloat16),
            VMEM((model, inner), jnp.bfloat16),
            VMEM((model, rows), jnp.bfloat16),
            pltpu.SemaphoreType.DMA,
            pltpu.SemaphoreType.DMA,
        ],
        compiler_params=pltpu.CompilerParams(vmem_limit_bytes=61 << 20),
        cost_estimate=pl.CostEstimate(
            flops=1_400_000_000, bytes_accessed=18_000_000, transcendentals=4_000_000
        ),
        name="scan_stage",
    )(info, *args, out_w)


def mlp_stage(
    devices,
    info,
    normed_hbm,
    middle_hbm,
    final_hbm,
    last_edge_hbm,
    gate_hbm,
    up_hbm,
    down_hbm,
    out_ref,
    new_state_ref,
    new_edge_ref,
    normed_ref,
    middle_ref,
    final_ref,
    last_edge_ref,
    gate_w,
    up_w,
    down_w,
    fetch_sems,
    near1,
    near2,
    far,
    out1,
    out2,
    far_out,
    own_out,
    low_in,
    high_in,
    far_in,
    ring_sems,
    full,
    full_edge,
    *spread_refs,
):
    rows, model = middle_ref.shape
    half = rows // 2
    inner = final_ref.shape[2]
    requests = final_ref.shape[0]
    me, _, _, _, partner, z_peers, x_peers = near_devices(devices)
    ring = lax.axis_size("req")
    here = lax.axis_index("req")
    above, below = (here + 1) % ring, (here + ring - 1) % ring
    fetches = [
        pltpu.make_async_copy(src, dst, fetch_sems.at[i])
        for i, (src, dst) in enumerate(
            (
                (normed_hbm, normed_ref),
                (final_hbm, final_ref),
                (last_edge_hbm, last_edge_ref),
                (gate_hbm, gate_w),
                (up_hbm, up_w),
                (down_hbm, down_w),
                (middle_hbm, middle_ref),
            )
        )
    ]
    for copy in fetches:
        copy.start()
    greet(
        [("req", above), ("req", below)] + [("seq", p) for p in [partner] + z_peers + x_peers]
    )

    def hop(src, dst, index, peer):
        return pltpu.make_async_remote_copy(
            src_ref=src,
            dst_ref=dst,
            send_sem=ring_sems.at[0, index],
            recv_sem=ring_sems.at[1, index],
            device_id={"req": peer},
            device_id_type=MESH_ID,
        )

    piece = [pl.ds(i * (half // 2), half // 2) for i in range(4)]
    first, second = pl.ds(0, half), pl.ds(half, half)
    toward = [above, above, below, below]
    out_hops = [hop(normed_ref.at[piece[i]], near1.at[piece[i]], i, toward[i]) for i in range(4)]
    on_hops = [hop(near1.at[piece[i]], far.at[piece[i]], 4 + i, toward[i]) for i in range(4)]
    up_b = hop(normed_ref.at[second], near2.at[first], 8, above)
    down_a = hop(normed_ref.at[first], near2.at[second], 9, below)
    far_hops = [hop(far_out.at[piece[i]], far_in.at[piece[i]], 10 + i, toward[i]) for i in range(4)]
    back_down = hop(out1.at[first], high_in.at[first], 14, below)
    back_up = hop(out1.at[second], low_in.at[second], 15, above)
    swap = [2, 3, 0, 1]
    last_hops = [
        hop(
            out2.at[piece[swap[i]]],
            (low_in if i < 2 else high_in).at[piece[i]],
            16 + i,
            toward[i],
        )
        for i in range(4)
    ]
    order = (0, 2, 1, 3)
    fetches[0].wait()
    for i in order:
        out_hops[i].start()
    per = len(Spread.scratch(devices, inner, 1, False))
    finals = Spread(devices, inner, requests, True, spread_refs[:per])
    edges = Spread(devices, inner, 1, False, spread_refs[per:])
    fetches[1].wait()
    for r in range(requests):
        finals.mine[r] = final_ref[r].astype(jnp.bfloat16)
    finals.start_core()
    fetches[2].wait()
    edges.mine[0] = last_edge_ref[...].astype(jnp.bfloat16)
    edges.start_core()

    def hidden_units(value):
        gate = jnp.dot(value, gate_w[...], preferred_element_type=jnp.float32)
        up = jnp.dot(value, up_w[...], preferred_element_type=jnp.float32)
        hidden = (gate / (1.0 + jnp.exp(-gate)) * up).astype(jnp.bfloat16)
        return lax.dot_general(
            hidden, down_w[...], (((1,), (1,)), ((), ())), preferred_element_type=jnp.float32
        )

    finals.finish_core()
    finals.start_z()
    edges.finish_core()
    for i in order:
        out_hops[i].wait_recv()
        on_hops[i].start()
    up_b.start()
    down_a.start()
    for copy in fetches[3:]:
        copy.wait()
    out1[:, :model] = hidden_units(near1[:, :model]).astype(jnp.bfloat16)
    for i in order:
        on_hops[i].wait_recv()
    far_out[:, :model] = hidden_units(far[:, :model]).astype(jnp.bfloat16)
    for i in order:
        far_hops[i].start()
    finals.finish_z()
    finals.start_x()
    edges.start_z()
    up_b.wait_recv()
    down_a.wait_recv()
    own_out[...] = hidden_units(near2[:, :model])
    for i in order:
        far_hops[i].wait_recv()
        rows_at = piece[swap[i]]
        joined = own_out[rows_at] + far_in[piece[i], :model].astype(jnp.float32)
        out2[rows_at, :model] = joined.astype(jnp.bfloat16)
        last_hops[i].start()
        if i == 2:
            back_down.start()
            back_up.start()
    finals.finish_x()
    finals.start_z2()
    edges.finish_z()
    edges.start_x()
    own_out[...] = hidden_units(normed_ref[:, :model]) + middle_ref[...]
    finals.finish_z2()
    finals.start_core2()
    edges.finish_x()
    edges.start_core2()
    finals.finish_core2(full)
    state = jnp.zeros((STATE, inner), jnp.float32)
    for r in range(requests):
        state = jnp.where(info[12 + r] == me, full[r].astype(jnp.float32), state)
    new_state_ref[...] = state
    edges.finish_core2(full_edge)
    gathered = full_edge[0].astype(jnp.float32)
    edge = jnp.zeros((EDGE, inner), jnp.float32)
    for r in range(requests):
        owned = info[12 + r] == me
        edge = jnp.where(owned, gathered[r * EDGE : (r + 1) * EDGE], edge)
    new_edge_ref[...] = edge.astype(jnp.bfloat16)
    for i in order:
        last_hops[i].wait_recv()
    back_down.wait_recv()
    back_up.wait_recv()
    total = own_out[...] + low_in[:, :model].astype(jnp.float32)
    total = total + high_in[:, :model].astype(jnp.float32)
    out_ref[...] = jnp.transpose(total).astype(jnp.bfloat16)
    for copy in out_hops + on_hops + far_hops + last_hops + [up_b, down_a, back_down, back_up]:
        copy.wait_send()


def mlp_call(devices, info, args, weights, rows, model, inner, requests):
    f32, bf16 = jnp.float32, jnp.bfloat16
    hidden = weights[0].shape[1]
    wide = padded(model)
    return pl.pallas_call(
        functools.partial(mlp_stage, devices),
        out_shape=(
            jax.ShapeDtypeStruct((model, rows), bf16),
            jax.ShapeDtypeStruct((STATE, inner), f32),
            jax.ShapeDtypeStruct((EDGE, inner), bf16),
        ),
        in_specs=[sspec()] + [hspec()] * (len(args) + len(weights)),
        out_specs=tuple([vspec()] * 3),
        scratch_shapes=[
            VMEM((rows, wide), bf16),
            VMEM((rows, model), f32),
            VMEM((requests, STATE, inner), f32),
            VMEM((16, inner), f32),
            VMEM((model, hidden), bf16),
            VMEM((model, hidden), bf16),
            VMEM((model, hidden), bf16),
            pltpu.SemaphoreType.DMA((7,)),
            VMEM((rows, wide), bf16),
            VMEM((rows, wide), bf16),
            VMEM((rows, wide), bf16),
            VMEM((rows, wide), bf16),
            VMEM((rows, wide), bf16),
            VMEM((rows, wide), bf16),
            VMEM((rows, model), f32),
            VMEM((rows, wide), bf16),
            VMEM((rows, wide), bf16),
            VMEM((rows, wide), bf16),
            pltpu.SemaphoreType.DMA((2, 20)),
            VMEM((requests, 16, inner), bf16),
            VMEM((1, 16, inner), bf16),
        ]
        + Spread.scratch(devices, inner, requests, True)
        + Spread.scratch(devices, inner, 1, False),
        compiler_params=pltpu.CompilerParams(
            vmem_limit_bytes=61 << 20, collective_id=1, has_side_effects=True
        ),
        cost_estimate=pl.CostEstimate(
            flops=7_000_000_000, bytes_accessed=16_000_000, transcendentals=1_000_000
        ),
        name="mlp_stage",
    )(info, *args, *weights)


def handing_stage(*refs):
    count = len(refs) // 2
    for i in range(count):
        refs[count + i][...] = refs[i][...]


def handed(*arrays):
    return pl.pallas_call(
        handing_stage,
        out_shape=tuple(jax.ShapeDtypeStruct(a.shape, a.dtype) for a in arrays),
        in_specs=[vspec()] * len(arrays),
        out_specs=tuple([vspec()] * len(arrays)),
        name="handing_stage",
    )(*arrays)


def shards(
    hidden_in,
    mamba_in,
    conv_weight,
    conv_bias,
    x_proj,
    dt_proj,
    dt_bias,
    decay_rate,
    skip_gain,
    out_proj,
    norm_gain,
    mlp_gate,
    mlp_up,
    mlp_down,
    cache_state,
    cache_edge,
    req_lengths,
    cont_flag,
    cache_source,
    owner_slot,
):
    rows, inner = mamba_in.shape[1:]
    model = hidden_in.shape[2]
    requests = req_lengths.shape[1]
    devices = lax.axis_size("seq")
    place = lax.axis_index("seq")
    info = jnp.concatenate(
        [
            req_lengths[0],
            cont_flag[0],
            cache_source[0],
            owner_slot[0],
            jnp.reshape(place * rows, (1,)).astype(jnp.int32),
        ]
    )
    mixed, step, proj, enter, last_edge, start_state, params = front_call(
        devices,
        info,
        (
            conv_weight,
            conv_bias,
            dt_bias,
            decay_rate,
            skip_gain,
            norm_gain,
            mamba_in[0],
            cache_state[0, 0],
            cache_edge[0, 0],
            x_proj.T,
            dt_proj,
        ),
        rows,
        inner,
        x_proj.shape[1],
        requests,
    )
    middle, normed, finals = scan_call(
        info,
        (mixed, step, proj, enter, start_state, params, hidden_in[0].T),
        out_proj.T,
        rows,
        inner,
        model,
        requests,
    )
    block_out, new_state, new_edge = handed(
        *mlp_call(
            devices,
            info,
            (normed, middle, finals, last_edge),
            (mlp_gate, mlp_up, mlp_down.T),
            rows,
            model,
            inner,
            requests,
        )
    )
    return block_out.T[None], new_state[None, None], new_edge[None, None]


def solution(mesh):
    grouped = P("req", "seq", None)
    slots = P("req", "seq", None, None)
    return jax.shard_map(
        shards,
        mesh=mesh,
        in_specs=(grouped, grouped)
        + (P(),) * 9
        + (P(None, "req"), P(None, "req"), P("req", None), slots, slots)
        + (P("req", None),) * 4,
        out_specs=(grouped, slots, slots),
        check_vma=False,
    )
```

```python
import functools

import jax
import jax.numpy as jnp
from jax import lax
from jax.experimental import pallas as pl
from jax.experimental.pallas import tpu as pltpu
from jax.sharding import PartitionSpec as P

STATE = 16
EDGE = 3
NORM_EPS = 1e-06
LANES = 128
FAR = 1e30
HIGHEST_PREC = lax.Precision.HIGHEST
VMEM = pltpu.VMEM
SMEM = pltpu.SMEM


def vspec():
    return pl.BlockSpec(memory_space=VMEM)


def hspec():
    return pl.BlockSpec(memory_space=pltpu.HBM)


def sspec():
    return pl.BlockSpec(memory_space=SMEM)


def col_block(width):
    return 640 if width % 640 == 0 else LANES


MESH_ID = pl.DeviceIdType.MESH


def layout_of(devices):
    depth = 4 if devices >= 32 else 2
    return devices // (2 * depth), depth


def padded(width):
    return -(-width // LANES) * LANES


def half_width(inner):
    return -(-inner // (2 * LANES)) * LANES


def near_devices(devices):
    across, depth = layout_of(devices)
    me = lax.axis_index("seq")
    core, z, x = me % 2, (me // 2) % depth, me // (2 * depth)
    partner = me + 1 - 2 * core
    z_peers = [x * 2 * depth + ((z + d) % depth) * 2 + core for d in range(1, depth)]
    x_peers = [((x + d) % across) * 2 * depth + z * 2 + core for d in range(1, across)]
    return me, core, z, x, partner, z_peers, x_peers


def my_lanes(core, inner):
    half = half_width(inner)
    return pl.ds(pl.multiple_of(core * (inner - half), LANES), half)


def send(src, dst, sems, index, peer):
    return pltpu.make_async_remote_copy(
        src_ref=src,
        dst_ref=dst,
        send_sem=sems.at[0, index],
        recv_sem=sems.at[1, index],
        device_id={"seq": peer},
        device_id_type=MESH_ID,
    )


def greet(axis_peers):
    barrier = pltpu.get_barrier_semaphore()
    for axis, peer in axis_peers:
        pl.semaphore_signal(barrier, inc=1, device_id={axis: peer}, device_id_type=MESH_ID)
    pl.semaphore_wait(barrier, len(axis_peers))


class Spread:
    def __init__(self, devices, inner, count, split, refs):
        self.devices, self.inner, self.count, self.split = devices, inner, count, split
        self.across, self.depth = layout_of(devices)
        self.part = count // self.depth if split else count
        (
            self.mine,
            self.from_core,
            self.acc,
            self.from_z,
            self.from_x,
            self.from_z2,
            self.other,
            self.sems,
        ) = refs
        _, self.core, self.z, self.x, self.partner, self.z_peers, self.x_peers = near_devices(
            devices
        )
        self.lanes = my_lanes(self.core, inner)
        self.far_lanes = my_lanes(1 - self.core, inner)
        self.copies = []

    @staticmethod
    def scratch(devices, inner, count, split):
        across, depth = layout_of(devices)
        part = count // depth if split else count
        half = half_width(inner)
        b = jnp.bfloat16
        return [
            VMEM((count, 16, inner), b),
            VMEM((count, 16, half), b),
            VMEM((count, 16, half), b),
            VMEM((depth - 1, part, 16, half), b),
            VMEM((across - 1, part, 16, half), b),
            VMEM((depth - 1, part, 16, half), b),
            VMEM((count, 16, half), b),
            pltpu.SemaphoreType.DMA((2, 2 + 2 * (depth - 1) + (across - 1))),
        ]

    def own_part(self, shift=0):
        if not self.split:
            return pl.ds(0, self.part)
        return pl.ds(((self.z + shift) % self.depth) * self.part, self.part)

    def begin(self, copies):
        self.copies = copies
        for copy in copies:
            copy.start()

    def end(self):
        for copy in self.copies:
            copy.wait()

    def start_core(self):
        self.begin(
            [send(self.mine.at[:, :, self.far_lanes], self.from_core, self.sems, 0, self.partner)]
        )

    def finish_core(self):
        self.end()
        total = self.mine[:, :, self.lanes].astype(jnp.float32) + self.from_core[...].astype(
            jnp.float32
        )
        self.acc[...] = total.astype(jnp.bfloat16)

    def start_z(self):
        self.begin(
            [
                send(self.acc.at[self.own_part(d + 1)], self.from_z.at[d], self.sems, 1 + d, peer)
                for d, peer in enumerate(self.z_peers)
            ]
        )

    def finish_z(self):
        self.end()
        here = self.own_part()
        total = self.acc[here].astype(jnp.float32)
        for d in range(self.depth - 1):
            total = total + self.from_z[d].astype(jnp.float32)
        self.acc[here] = total.astype(jnp.bfloat16)

    def start_x(self):
        base = self.depth
        self.begin(
            [
                send(self.acc.at[self.own_part()], self.from_x.at[d], self.sems, base + d, peer)
                for d, peer in enumerate(self.x_peers)
            ]
        )

    def finish_x(self):
        self.end()
        here = self.own_part()
        total = self.acc[here].astype(jnp.float32)
        for d in range(self.across - 1):
            total = total + self.from_x[d].astype(jnp.float32)
        self.acc[here] = total.astype(jnp.bfloat16)

    def start_z2(self):
        if not self.split:
            return
        base = self.depth + self.across - 1
        self.begin(
            [
                send(self.acc.at[self.own_part()], self.from_z2.at[d], self.sems, base + d, peer)
                for d, peer in enumerate(self.z_peers)
            ]
        )

    def finish_z2(self):
        if not self.split:
            return
        self.end()
        for d in range(self.depth - 1):
            self.acc[self.own_part(-(d + 1))] = self.from_z2[d]

    def start_core2(self):
        last = 2 * (self.depth - 1) + self.across
        self.begin([send(self.acc, self.other, self.sems, last, self.partner)])

    def finish_core2(self, out_ref):
        self.end()
        out_ref[:, :, self.lanes] = self.acc[...]
        out_ref[:, :, self.far_lanes] = self.other[...]


def segment(info, r, rows):
    begin = jnp.int32(0)
    for q in range(r):
        begin = begin + info[q]
    end = begin + info[r]
    first = info[16]
    low = jnp.clip(begin - first, 0, rows)
    high = jnp.clip(end - first, 0, rows)
    fresh = begin >= first
    ends = (end > first) & (end <= first + rows)
    return begin, low, high, fresh, ends


def front_stage(
    devices,
    info,
    taps_ref,
    conv_b_flat,
    dt_bias_flat,
    decay_flat,
    skip_flat,
    gain_flat,
    x_hbm,
    cache_hbm,
    cache_edge_hbm,
    x_proj_hbm,
    dt_proj_hbm,
    mixed_hbm,
    step_hbm,
    proj_ref,
    enter_ref,
    last_edge_ref,
    start_ref,
    param_ref,
    mixed_ref,
    step_ref,
    keep_sems,
    since_ref,
    x_ref,
    cache_ref,
    cache_edge_ref,
    x_proj_ref,
    dt_proj_ref,
    fetch_sems,
    ext,
    mixed_b,
    suffix,
    b_wide,
    halo_ref,
    edge3_ref,
    end_ref,
    sum_ref,
    halo_sems,
    pair_h,
    pair_s,
    own_h,
    own_s,
    z_h,
    z_s,
    x_h,
    x_s,
    half_out,
    half_in,
    pre_sems,
    *spread_refs,
):
    fetches = [
        pltpu.make_async_copy(src, dst, fetch_sems.at[i])
        for i, (src, dst) in enumerate(
            (
                (x_hbm, x_ref),
                (cache_edge_hbm, cache_edge_ref),
                (cache_hbm, cache_ref),
                (x_proj_hbm, x_proj_ref),
                (dt_proj_hbm, dt_proj_ref),
            )
        )
    ]
    for copy in fetches:
        copy.start()
    param_ref[pl.ds(0, 4), :] = taps_ref[...]
    for i, flat in enumerate((conv_b_flat, dt_bias_flat, decay_flat, skip_flat, gain_flat)):
        size = flat.shape[0]
        param_ref[pl.ds(4 + i, 1), pl.ds(0, size)] = flat[...].reshape(1, size)
    conv_w_ref = param_ref.at[pl.ds(0, 4)]
    conv_b_ref = param_ref.at[pl.ds(4, 1)]
    dt_bias_ref = param_ref.at[pl.ds(5, 1)]
    decay_ref = param_ref.at[pl.ds(6, 1)]
    rows, inner = x_ref.shape
    requests = start_ref.shape[0]
    me, core, z, x, partner, z_peers, x_peers = near_devices(devices)
    after, before = (me + 1) % devices, (me + devices - 1) % devices
    greet([("seq", p) for p in [partner, after, before] + z_peers + x_peers])
    halo_copy = send(x_ref.at[pl.ds(rows - 16, 16)], halo_ref, halo_sems, 0, after)
    fetches[0].wait()
    halo_copy.start()
    fetches[1].wait()
    per = len(Spread.scratch(devices, inner, 1, False))
    edge_sum = Spread(devices, inner, 1, False, spread_refs[:per])
    state_sum = Spread(devices, inner, requests, True, spread_refs[per:])
    spot = lax.broadcasted_iota(jnp.int32, (16, inner), 0)
    edge_rows = cache_edge_ref[...].astype(jnp.float32)
    placed = jnp.zeros((16, inner), jnp.float32)
    for r in range(requests):
        take = (info[8 + r] == me) & (info[4 + r] > 0)
        for j in range(EDGE):
            placed = jnp.where((spot == r * EDGE + j) & take, edge_rows[j : j + 1], placed)
    edge_sum.mine[0] = placed.astype(jnp.bfloat16)
    edge_sum.start_core()
    fetches[2].wait()
    for r in range(requests):
        take = (info[8 + r] == me) & (info[4 + r] > 0)
        state_sum.mine[r] = jnp.where(take, cache_ref[...], 0.0).astype(jnp.bfloat16)
    state_sum.start_core()
    ext[pl.ds(16, rows), :] = x_ref[...].astype(jnp.float32)
    fetches[3].wait()
    fetches[4].wait()
    edge_sum.finish_core()
    edge_sum.start_z()
    state_sum.finish_core()
    edge_sum.finish_z()
    edge_sum.start_x()
    state_sum.start_z()
    halo_copy.wait()
    ext[pl.ds(0, 16), :] = halo_ref[...].astype(jnp.float32)
    width = col_block(inner)
    rank = dt_proj_ref.shape[0]
    first_pos = info[16]
    position = first_pos + lax.broadcasted_iota(jnp.int32, (rows, LANES), 0)
    marks = [segment(info, r, rows) for r in range(requests)]
    begin = jnp.zeros((rows, LANES), jnp.int32)
    request = jnp.zeros((rows, LANES), jnp.int32)
    last_begin, last_req = jnp.int32(0), jnp.int32(0)
    for r in range(1, requests):
        reached = position >= marks[r][0]
        begin = jnp.where(reached, marks[r][0], begin)
        request = jnp.where(reached, r, request)
        inside = first_pos + rows - 1 >= marks[r][0]
        last_begin = jnp.where(inside, marks[r][0], last_begin)
        last_req = jnp.where(inside, r, last_req)
    offset = position - begin
    in_last = (position >= last_begin).astype(jnp.float32)
    edge_id = lax.broadcasted_iota(jnp.int32, (rows, 16), 1)
    hots = []
    for lag in (1, 2, 3):
        want = request * EDGE + EDGE + offset - lag
        hit = (edge_id == want[:, :16]) & (offset[:, :16] < lag)
        hots.append(hit.astype(jnp.float32).astype(jnp.bfloat16))

    keep = {}
    for lag in (1, 2, 3):
        keep[lag] = jnp.concatenate([offset] * (width // LANES), axis=1) >= lag
    for first in range(0, inner, width):
        cols = pl.ds(first, width)
        total = conv_b_ref[:, cols] + conv_w_ref[pl.ds(3, 1), cols] * ext[pl.ds(16, rows), cols]
        for lag in (1, 2, 3):
            near = ext[pl.ds(16 - lag, rows), cols]
            row = jnp.where(keep[lag], near, 0.0)
            total = total + conv_w_ref[pl.ds(3 - lag, 1), cols] * row
        suffix[:, cols] = total
    edge_sum.finish_x()
    edge_sum.start_core2()
    state_sum.finish_z()
    state_sum.start_x()
    edge_sum.finish_core2(edge3_ref)
    edge_ref = edge3_ref.at[0]
    hot = jnp.concatenate(hots * 3, axis=1)
    for first in range(0, inner, width):
        cols = pl.ds(first, width)
        edges = edge_ref[:, cols].astype(jnp.float32)
        far = jnp.concatenate(
            [conv_w_ref[pl.ds(3 - lag, 1), cols] * edges for lag in (1, 2, 3)], axis=0
        )
        high = far.astype(jnp.bfloat16)
        rest = far - high.astype(jnp.float32)
        mid = rest.astype(jnp.bfloat16)
        low = (rest - mid.astype(jnp.float32)).astype(jnp.bfloat16)
        far = jnp.concatenate([high, mid, low], axis=0)
        total = suffix[:, cols] + jnp.dot(hot, far, preferred_element_type=jnp.float32)
        mixed = (total / (1.0 + jnp.exp(-total))).astype(jnp.bfloat16)
        mixed_b[:, cols] = mixed
        mixed_ref[:, cols] = mixed.astype(jnp.float32)

    keep_mixed = pltpu.make_async_copy(mixed_ref, mixed_hbm, keep_sems.at[0])
    keep_mixed.start()
    proj = lax.dot_general(
        mixed_b[...],
        x_proj_ref[...],
        (((1,), (1,)), ((), ())),
        preferred_element_type=jnp.float32,
    )
    proj_ref[...] = proj
    for s in range(STATE):
        b_wide[s] = jnp.broadcast_to(proj[:, rank + s : rank + s + 1], (rows, LANES))
    dt_low = proj[:, :rank].astype(jnp.bfloat16)
    row_id = lax.broadcasted_iota(jnp.int32, (rows, rows), 0)
    col_id = lax.broadcasted_iota(jnp.int32, (rows, rows), 1)
    later = (col_id > row_id).astype(jnp.bfloat16)
    for first in range(0, inner, width):
        cols = pl.ds(first, width)
        v = jnp.dot(dt_low, dt_proj_ref[:, cols], preferred_element_type=jnp.float32)
        v = v + dt_bias_ref[:, cols]
        step = jnp.maximum(v, 0.0) + jnp.log1p(jnp.exp(-jnp.abs(v)))
        step_ref[:, cols] = step
        high = step.astype(jnp.bfloat16)
        rest = step - high.astype(jnp.float32)
        mid = rest.astype(jnp.bfloat16)
        low = (rest - mid.astype(jnp.float32)).astype(jnp.bfloat16)
        after = (
            jnp.dot(later, high, preferred_element_type=jnp.float32)
            + jnp.dot(later, mid, preferred_element_type=jnp.float32)
            + jnp.dot(later, low, preferred_element_type=jnp.float32)
        )
        suffix[:, cols] = after

    keep_step = pltpu.make_async_copy(step_ref, step_hbm, keep_sems.at[1])
    keep_step.start()
    state_sum.finish_x()
    state_sum.start_z2()
    starts_here = (last_begin >= first_pos).astype(jnp.int32)
    flag = jnp.full((1, LANES), starts_here, jnp.int32).astype(jnp.float32)
    power = (lax.broadcasted_iota(jnp.int32, (STATE, LANES), 0) + 1).astype(jnp.float32)

    def one_tile(j, carry):
        cols = pl.ds(pl.multiple_of(j * LANES, LANES), LANES)
        rate = decay_ref[:, cols]
        acc = [jnp.zeros((8, LANES), jnp.float32) for _ in range(STATE)]
        since = jnp.zeros((8, LANES), jnp.float32)
        for tile in range(rows // 8):
            here = pl.ds(tile * 8, 8)
            fade = jnp.exp(-rate * suffix[here, cols])
            step = step_ref[here, cols] * in_last[tile * 8 : tile * 8 + 8]
            since = since + step
            push = step * mixed_ref[here, cols]
            for s in range(STATE):
                push = push * fade
                acc[s] = acc[s] + push * b_wide[s, here, :]
        ends = jnp.concatenate([jnp.sum(a, axis=0, keepdims=True) for a in acc], axis=0)
        end_ref[:, cols] = ends
        since = jnp.sum(since, axis=0, keepdims=True)
        since_ref[:, cols] = since
        sum_ref[:, cols] = jnp.where(flag > 0.5, FAR, since)
        return carry

    def one_seed(j, carry):
        cols = pl.ds(pl.multiple_of(j * LANES, LANES), LANES)
        rate = decay_ref[:, cols]
        since = since_ref[:, cols]
        seed = jnp.exp(-(rate * since) * power) * start_ref[last_req, :, cols].astype(jnp.float32)
        end_ref[:, cols] = end_ref[:, cols] + flag * seed
        return carry

    lax.fori_loop(0, inner // LANES, one_tile, 0)
    state_sum.finish_z2()
    state_sum.start_core2()
    state_sum.finish_core2(start_ref)
    lax.fori_loop(0, inner // LANES, one_seed, 0)
    power16 = (lax.broadcasted_iota(jnp.int32, (STATE, LANES), 0) + 1).astype(jnp.float32)
    half = half_width(inner)
    tiles = half // LANES
    base = core * (inner - half)
    own_h[...] = end_ref[...].astype(jnp.bfloat16)
    for j in range(inner // LANES):
        own_s[pl.ds(j, 1), :] = sum_ref[:, pl.ds(j * LANES, LANES)]
    pair = [
        send(own_h, pair_h, pre_sems, 0, partner),
        send(own_s, pair_s, pre_sems, 1, partner),
    ]
    for copy in pair:
        copy.start()
    across, depth = layout_of(devices)
    first_core = core == 0

    def lane(j):
        return pl.ds(pl.multiple_of(base + j * LANES, LANES), LANES)

    def f32(value):
        return value.astype(jnp.float32)

    for copy in pair:
        copy.wait()
    z_sum = []
    for j in range(tiles):
        rate = decay_ref[:, lane(j)] * power16
        mine, theirs = own_h[:, lane(j)], pair_h[:, lane(j)]
        shift = (inner - half) // LANES
        s_mine = jnp.where(first_core, own_s[j : j + 1], own_s[j + shift : j + shift + 1])
        s_pair = jnp.where(first_core, pair_s[j : j + 1], pair_s[j + shift : j + shift + 1])
        h0 = f32(jnp.where(first_core, f32(mine), f32(theirs)))
        h1 = f32(jnp.where(first_core, f32(theirs), f32(mine)))
        s1 = jnp.where(first_core, s_pair, s_mine)
        z_h[0, :, pl.ds(j * LANES, LANES)] = (jnp.exp(-rate * s1) * h0 + h1).astype(jnp.bfloat16)
        z_s[0, pl.ds(j, 1), :] = s_mine + s_pair
    copies = []
    for d, peer in enumerate(z_peers):
        copies.append(send(z_h.at[0], z_h.at[d + 1], pre_sems, 2 + 2 * d, peer))
        copies.append(send(z_s.at[0], z_s.at[d + 1], pre_sems, 3 + 2 * d, peer))
    for copy in copies:
        copy.start()
    for copy in copies:
        copy.wait()
    prefix = []
    for j in range(tiles):
        cols = pl.ds(j * LANES, LANES)
        rate = decay_ref[:, lane(j)] * power16
        total = jnp.zeros((STATE, LANES), jnp.float32)
        part = jnp.zeros((STATE, LANES), jnp.float32)
        total_s = jnp.zeros((1, LANES), jnp.float32)
        part_s = jnp.zeros((1, LANES), jnp.float32)
        for k in range(depth):
            slot = (z - k + depth) % depth
            s_k = z_s[slot, pl.ds(j, 1), :]
            h_k = f32(z_h[slot, :, cols])
            fade = jnp.exp(-rate * s_k)
            total = fade * total + h_k
            part = jnp.where(k < z, fade * part + h_k, part)
            total_s = total_s + s_k
            part_s = jnp.where(k < z, part_s + s_k, part_s)
        x_h[0, :, cols] = total.astype(jnp.bfloat16)
        x_s[0, pl.ds(j, 1), :] = total_s
        prefix.append((part, part_s))
    copies = []
    first = 2 + 2 * (depth - 1)
    for d, peer in enumerate(x_peers):
        copies.append(send(x_h.at[0], x_h.at[d + 1], pre_sems, first + 2 * d, peer))
        copies.append(send(x_s.at[0], x_s.at[d + 1], pre_sems, first + 1 + 2 * d, peer))
    for copy in copies:
        copy.start()
    for copy in copies:
        copy.wait()
    for j in range(tiles):
        cols = pl.ds(j * LANES, LANES)
        rate = decay_ref[:, lane(j)] * power16
        part = jnp.zeros((STATE, LANES), jnp.float32)
        for k in range(across):
            slot = (x - k + across) % across
            value = jnp.exp(-rate * x_s[slot, pl.ds(j, 1), :]) * part + f32(x_h[slot, :, cols])
            part = jnp.where(k < x, value, part)
        inner_part, inner_s = prefix[j]
        half_out[:, cols] = jnp.exp(-rate * inner_s) * part + inner_part
    last = first + 2 * (across - 1)
    swap = send(half_out, half_in, pre_sems, last, partner)
    swap.start()
    swap.wait()
    enter_ref[:, my_lanes(core, inner)] = half_out[...]
    enter_ref[:, my_lanes(1 - core, inner)] = half_in[...]
    for j in range(inner // LANES):
        cols = pl.ds(j * LANES, LANES)
        rate = decay_ref[:, cols] * power16
        chip = enter_ref[:, cols]
        second = jnp.exp(-rate * pair_s[j : j + 1]) * chip + f32(pair_h[:, cols])
        enter_ref[:, cols] = jnp.where(first_core, chip, second)

    row_of = lax.broadcasted_iota(jnp.int32, (16, LANES), 0)
    from_of = lax.broadcasted_iota(jnp.int32, (16, LANES), 1)
    near_at = jnp.full((16, LANES), -1, jnp.int32)
    far_at = jnp.full((16, LANES), -1, jnp.int32)
    for r in range(requests):
        _, _, high, _, ends = marks[r]
        size = info[r]
        for j in range(EDGE):
            lag = EDGE - 1 - j
            near = jnp.where(ends & (size > lag), high + 15 - lag, -1)
            far = jnp.where(ends & (size <= lag), r * EDGE + EDGE + size - 1 - lag, -1)
            near_at = jnp.where(row_of == r * EDGE + j, near, near_at)
            far_at = jnp.where(row_of == r * EDGE + j, far, far_at)

    def hot_rows(at, count):
        return (from_of[:, :count] == at[:, :count]).astype(jnp.float32).astype(jnp.bfloat16)

    for first in range(0, inner, width):
        cols = pl.ds(first, width)
        last_edge_ref[:, cols] = (
            jnp.dot(hot_rows(near_at - 16, rows), x_ref[:, cols], preferred_element_type=jnp.float32)
            + jnp.dot(hot_rows(near_at, 16), halo_ref[:, cols], preferred_element_type=jnp.float32)
            + jnp.dot(hot_rows(far_at, 16), edge_ref[:, cols], preferred_element_type=jnp.float32)
        )
    keep_mixed.wait()
    keep_step.wait()


def front_call(devices, info, args, rows, inner, proj_width, requests):
    f32, bf16 = jnp.float32, jnp.bfloat16
    across, depth = layout_of(devices)
    half = half_width(inner)
    s_rows = -(-(inner // LANES) // 8) * 8
    return pl.pallas_call(
        functools.partial(front_stage, devices),
        out_shape=(
            jax.ShapeDtypeStruct((rows, inner), f32),
            jax.ShapeDtypeStruct((rows, inner), f32),
            jax.ShapeDtypeStruct((rows, proj_width), f32),
            jax.ShapeDtypeStruct((STATE, inner), f32),
            jax.ShapeDtypeStruct((16, inner), f32),
            jax.ShapeDtypeStruct((requests, STATE, inner), bf16),
            jax.ShapeDtypeStruct((16, inner), f32),
        ),
        in_specs=[sspec()] + [vspec()] * 6 + [hspec()] * (len(args) - 6),
        out_specs=tuple([hspec()] * 2 + [vspec()] * 5),
        scratch_shapes=[
            VMEM((rows, inner), f32),
            VMEM((rows, inner), f32),
            pltpu.SemaphoreType.DMA((2,)),
            VMEM((1, inner), f32),
            VMEM((rows, inner), bf16),
            VMEM((STATE, inner), f32),
            VMEM((EDGE, inner), bf16),
            VMEM((proj_width, inner), bf16),
            VMEM((proj_width - 2 * STATE, inner), bf16),
            pltpu.SemaphoreType.DMA((5,)),
            VMEM((rows + 16, inner), f32),
            VMEM((rows, inner), bf16),
            VMEM((rows, inner), f32),
            VMEM((STATE, rows, LANES), f32),
            VMEM((16, inner), bf16),
            VMEM((1, 16, inner), bf16),
            VMEM((STATE, inner), f32),
            VMEM((1, inner), f32),
            pltpu.SemaphoreType.DMA((2, 1)),
            VMEM((STATE, inner), bf16),
            VMEM((s_rows, LANES), f32),
            VMEM((STATE, inner), bf16),
            VMEM((s_rows, LANES), f32),
            VMEM((depth, STATE, half), bf16),
            VMEM((depth, 16, LANES), f32),
            VMEM((across, STATE, half), bf16),
            VMEM((across, 16, LANES), f32),
            VMEM((STATE, half), f32),
            VMEM((STATE, half), f32),
            pltpu.SemaphoreType.DMA((2, 3 + 2 * (depth + across - 2))),
        ]
        + Spread.scratch(devices, inner, 1, False)
        + Spread.scratch(devices, inner, requests, True),
        compiler_params=pltpu.CompilerParams(
            vmem_limit_bytes=61 << 20, collective_id=0, has_side_effects=True
        ),
        cost_estimate=pl.CostEstimate(
            flops=400_000_000, bytes_accessed=8_000_000, transcendentals=2_000_000
        ),
        name="front_stage",
    )(info, *args)


def row_sums(parts):
    row = lax.broadcasted_iota(jnp.int32, parts[0].shape, 0)
    for step in (4, 2, 1):
        odd = (row // step) % 2 == 1
        joined = []
        for i in range(step):
            a, b = parts[i], parts[i + step]
            keep, move = jnp.where(odd, b, a), jnp.where(odd, a, b)
            moved = pltpu.roll(move, step, 0)
            if step < 4:
                moved = jnp.where(odd, moved, pltpu.roll(move, 8 - step, 0))
            joined.append(keep + moved)
        parts = joined
    return parts[0]


def scan_stage(
    info,
    mixed_hbm,
    step_hbm,
    proj_ref,
    enter_hbm,
    start_hbm,
    param_ref,
    hidden_hbm,
    out_w_hbm,
    middle_ref,
    normed_ref,
    final_hbm,
    mixed_ref,
    step_ref,
    final_ref,
    enter_ref,
    start_ref,
    seed_sems,
    block_sems,
    final_sem,
    bc_wide,
    y_ref,
    ssm_b,
    out_w,
    hidden_ref,
    w_sem,
    hidden_sem,
):
    rows, inner = mixed_ref.shape
    width = col_block(inner)
    tiles = width // LANES
    rank = proj_ref.shape[1] - 2 * STATE
    seeds = (
        pltpu.make_async_copy(enter_hbm, enter_ref, seed_sems.at[0]),
        pltpu.make_async_copy(start_hbm, start_ref, seed_sems.at[1]),
    )
    for copy in seeds:
        copy.start()
    width = col_block(step_ref.shape[1])

    def block_copies(g):
        cols = pl.ds(pl.multiple_of(g * width, LANES), width)
        return (
            pltpu.make_async_copy(
                mixed_hbm.at[:, cols], mixed_ref.at[:, cols], block_sems.at[0, g]
            ),
            pltpu.make_async_copy(step_hbm.at[:, cols], step_ref.at[:, cols], block_sems.at[1, g]),
        )

    for g in range(step_ref.shape[1] // width):
        for copy in block_copies(g):
            copy.start()
    fetch = pltpu.make_async_copy(out_w_hbm, out_w, w_sem)
    fetch.start()
    fetch_hidden = pltpu.make_async_copy(hidden_hbm, hidden_ref, hidden_sem)
    fetch_hidden.start()
    model = hidden_ref.shape[0]
    decay_ref = param_ref.at[pl.ds(6, 1)]
    skip_ref = param_ref.at[pl.ds(7, 1)]

    turned = jnp.transpose(proj_ref[:, rank : rank + 2 * STATE])
    for t in range(rows):
        bc_wide[t] = jnp.broadcast_to(turned[:, t : t + 1], (2 * STATE, LANES))
    final_ref[...] = jnp.zeros_like(final_ref)
    power = (lax.broadcasted_iota(jnp.int32, (8, LANES), 0) + 1).astype(jnp.float32)

    def wide_step(t, i, step, push, fade8, state, rates):
        b_low, b_high = bc_wide[t, 0:8], bc_wide[t, 8:16]
        c_low, c_high = bc_wide[t, 16:24], bc_wide[t, 24:32]
        outs, new = [], []
        for j in range(tiles):
            s_row, p_row, f_row = (
                jnp.broadcast_to(part[j][i : i + 1], (8, LANES)) for part in (step, push, fade8)
            )
            d_low = jnp.exp(s_row * rates[j])
            d_high = d_low * f_row
            low = d_low * state[2 * j] + b_low * p_row
            high = d_high * state[2 * j + 1] + b_high * p_row
            new += [low, high]
            outs.append(c_low * low + c_high * high)
        return outs, tuple(new)

    def one_block(g, carry):
        for copy in block_copies(g):
            copy.wait()
        base = pl.multiple_of(g * width, LANES)
        tile_cols = [pl.ds(pl.multiple_of(base + j * LANES, LANES), LANES) for j in range(tiles)]
        rates = [-decay_ref[:, c] * power for c in tile_cols]
        decays = [decay_ref[:, c] for c in tile_cols]

        def load(row, count):
            step = [step_ref[pl.ds(row, count), c] for c in tile_cols]
            push = [s * mixed_ref[pl.ds(row, count), c] for s, c in zip(step, tile_cols)]
            fade8 = [jnp.exp(-8.0 * (s * d)) for s, d in zip(step, decays)]
            return step, push, fade8

        def eight(block, state, limits=None):
            row = pl.multiple_of(block * 8, 8)
            step, push, fade8 = load(row, 8)
            kept = [[] for _ in range(tiles)]
            for i in range(8):
                outs, new = wide_step(row + i, i, step, push, fade8, state, rates)
                if limits is not None:
                    active = (row + i >= limits[0]) & (row + i < limits[1])
                    new = tuple(jnp.where(active, a, b) for a, b in zip(new, state))
                state = new
                for j in range(tiles):
                    kept[j].append(outs[j])
            for j in range(tiles):
                y = row_sums(kept[j])
                if limits is not None:
                    at = row + lax.broadcasted_iota(jnp.int32, (8, LANES), 0)
                    y = jnp.where(
                        (at >= limits[0]) & (at < limits[1]), y, y_ref[pl.ds(row, 8), tile_cols[j]]
                    )
                y_ref[pl.ds(row, 8), tile_cols[j]] = y
            return state

        for r in range(final_ref.shape[0]):
            _, begin, end, new, ends = segment(info, r, rows)

            @pl.when(end > begin)
            def _():
                state = []
                for c in tile_cols:
                    for half in (pl.ds(0, 8), pl.ds(8, 8)):
                        old = enter_ref[half, c]
                        seed = start_ref[r, half, c].astype(jnp.float32)
                        state.append(jnp.where(new, seed, old))
                state = tuple(state)
                part = functools.partial(eight, limits=(begin, end))
                low, low_up, high = begin // 8, (begin + 7) // 8, end // 8
                state = lax.fori_loop(low, low_up, part, state)
                state = lax.fori_loop(low_up, jnp.maximum(high, low_up), eight, state)
                tail = jnp.where((high >= low_up) & (end % 8 > 0), high + 1, high)
                state = lax.fori_loop(high, tail, part, state)

                @pl.when(ends)
                def _():
                    for j, c in enumerate(tile_cols):
                        final_ref[r, pl.ds(0, 8), c] = state[2 * j]
                        final_ref[r, pl.ds(8, 8), c] = state[2 * j + 1]

        y = y_ref[:, pl.ds(base, width)]
        y = y + skip_ref[:, pl.ds(base, width)] * mixed_ref[:, pl.ds(base, width)]
        ssm_b[:, pl.ds(base, width)] = y.astype(jnp.bfloat16)
        return carry

    for copy in seeds:
        copy.wait()
    lax.fori_loop(0, inner // width, one_block, 0)
    keep_final = pltpu.make_async_copy(final_ref, final_hbm, final_sem)
    keep_final.start()
    fetch.wait()
    fetch_hidden.wait()
    middle = jnp.transpose(hidden_ref[...].astype(jnp.float32))
    for first in range(0, inner, width):
        middle = middle + lax.dot_general(
            ssm_b[:, first : first + width],
            out_w[:, first : first + width],
            (((1,), (1,)), ((), ())),
            preferred_element_type=jnp.float32,
        )
    middle_ref[...] = middle
    scale = lax.rsqrt(jnp.mean(middle * middle, axis=1, keepdims=True) + NORM_EPS)
    normed = (middle * scale * param_ref[8:9, :model]).astype(jnp.bfloat16)
    if normed_ref.shape[1] > model:
        normed_ref[...] = jnp.zeros_like(normed_ref)
    normed_ref[:, :model] = normed
    keep_final.wait()


def scan_call(info, args, out_w, rows, inner, model, requests):
    f32 = jnp.float32
    return pl.pallas_call(
        scan_stage,
        out_shape=(
            jax.ShapeDtypeStruct((rows, model), f32),
            jax.ShapeDtypeStruct((rows, padded(model)), jnp.bfloat16),
            jax.ShapeDtypeStruct((requests, STATE, inner), f32),
        ),
        in_specs=[sspec()]
        + [hspec()] * 2
        + [vspec()]
        + [hspec()] * 2
        + [vspec()] * (len(args) - 6)
        + [hspec()] * 2,
        out_specs=tuple([vspec()] * 2 + [hspec()]),
        scratch_shapes=[
            VMEM((rows, inner), f32),
            VMEM((rows, inner), f32),
            VMEM((requests, STATE, inner), f32),
            VMEM((STATE, inner), f32),
            VMEM((requests, STATE, inner), jnp.bfloat16),
            pltpu.SemaphoreType.DMA((2,)),
            pltpu.SemaphoreType.DMA((2, inner // col_block(inner))),
            pltpu.SemaphoreType.DMA,
            VMEM((rows, 2 * STATE, LANES), f32),
            VMEM((rows, inner), f32),
            VMEM((rows, inner), jnp.bfloat16),
            VMEM((model, inner), jnp.bfloat16),
            VMEM((model, rows), jnp.bfloat16),
            pltpu.SemaphoreType.DMA,
            pltpu.SemaphoreType.DMA,
        ],
        compiler_params=pltpu.CompilerParams(vmem_limit_bytes=61 << 20),
        cost_estimate=pl.CostEstimate(
            flops=1_400_000_000, bytes_accessed=18_000_000, transcendentals=4_000_000
        ),
        name="scan_stage",
    )(info, *args, out_w)


def mlp_stage(
    devices,
    info,
    normed_hbm,
    middle_hbm,
    final_hbm,
    last_edge_hbm,
    gate_hbm,
    up_hbm,
    down_hbm,
    out_ref,
    new_state_ref,
    new_edge_ref,
    normed_ref,
    middle_ref,
    final_ref,
    last_edge_ref,
    gate_w,
    up_w,
    down_w,
    fetch_sems,
    near1,
    near2,
    far,
    out1,
    out2,
    far_out,
    own_out,
    low_in,
    high_in,
    far_in,
    ring_sems,
    full,
    full_edge,
    *spread_refs,
):
    rows, model = middle_ref.shape
    half = rows // 2
    inner = final_ref.shape[2]
    requests = final_ref.shape[0]
    me, _, _, _, partner, z_peers, x_peers = near_devices(devices)
    ring = lax.axis_size("req")
    here = lax.axis_index("req")
    above, below = (here + 1) % ring, (here + ring - 1) % ring
    fetches = [
        pltpu.make_async_copy(src, dst, fetch_sems.at[i])
        for i, (src, dst) in enumerate(
            (
                (normed_hbm, normed_ref),
                (final_hbm, final_ref),
                (last_edge_hbm, last_edge_ref),
                (gate_hbm, gate_w),
                (up_hbm, up_w),
                (down_hbm, down_w),
                (middle_hbm, middle_ref),
            )
        )
    ]
    for copy in fetches:
        copy.start()
    greet(
        [("req", above), ("req", below)] + [("seq", p) for p in [partner] + z_peers + x_peers]
    )

    def hop(src, dst, index, peer):
        return pltpu.make_async_remote_copy(
            src_ref=src,
            dst_ref=dst,
            send_sem=ring_sems.at[0, index],
            recv_sem=ring_sems.at[1, index],
            device_id={"req": peer},
            device_id_type=MESH_ID,
        )

    piece = [pl.ds(i * (half // 2), half // 2) for i in range(4)]
    first, second = pl.ds(0, half), pl.ds(half, half)
    toward = [above, above, below, below]
    out_hops = [hop(normed_ref.at[piece[i]], near1.at[piece[i]], i, toward[i]) for i in range(4)]
    on_hops = [hop(near1.at[piece[i]], far.at[piece[i]], 4 + i, toward[i]) for i in range(4)]
    up_b = hop(normed_ref.at[second], near2.at[first], 8, above)
    down_a = hop(normed_ref.at[first], near2.at[second], 9, below)
    far_hops = [hop(far_out.at[piece[i]], far_in.at[piece[i]], 10 + i, toward[i]) for i in range(4)]
    back_down = hop(out1.at[first], high_in.at[first], 14, below)
    back_up = hop(out1.at[second], low_in.at[second], 15, above)
    swap = [2, 3, 0, 1]
    last_hops = [
        hop(
            out2.at[piece[swap[i]]],
            (low_in if i < 2 else high_in).at[piece[i]],
            16 + i,
            toward[i],
        )
        for i in range(4)
    ]
    order = (0, 2, 1, 3)
    fetches[0].wait()
    for i in order:
        out_hops[i].start()
    per = len(Spread.scratch(devices, inner, 1, False))
    finals = Spread(devices, inner, requests, True, spread_refs[:per])
    edges = Spread(devices, inner, 1, False, spread_refs[per:])
    fetches[1].wait()
    for r in range(requests):
        finals.mine[r] = final_ref[r].astype(jnp.bfloat16)
    finals.start_core()
    fetches[2].wait()
    edges.mine[0] = last_edge_ref[...].astype(jnp.bfloat16)
    edges.start_core()

    def hidden_units(value):
        gate = jnp.dot(value, gate_w[...], preferred_element_type=jnp.float32)
        up = jnp.dot(value, up_w[...], preferred_element_type=jnp.float32)
        hidden = (gate / (1.0 + jnp.exp(-gate)) * up).astype(jnp.bfloat16)
        return lax.dot_general(
            hidden, down_w[...], (((1,), (1,)), ((), ())), preferred_element_type=jnp.float32
        )

    finals.finish_core()
    finals.start_z()
    edges.finish_core()
    for i in order:
        out_hops[i].wait_recv()
        on_hops[i].start()
    up_b.start()
    down_a.start()
    for copy in fetches[3:]:
        copy.wait()
    out1[:, :model] = hidden_units(near1[:, :model]).astype(jnp.bfloat16)
    for i in order:
        on_hops[i].wait_recv()
    far_out[:, :model] = hidden_units(far[:, :model]).astype(jnp.bfloat16)
    for i in order:
        far_hops[i].start()
    finals.finish_z()
    finals.start_x()
    edges.start_z()
    up_b.wait_recv()
    down_a.wait_recv()
    own_out[...] = hidden_units(near2[:, :model])
    for i in order:
        far_hops[i].wait_recv()
        rows_at = piece[swap[i]]
        joined = own_out[rows_at] + far_in[piece[i], :model].astype(jnp.float32)
        out2[rows_at, :model] = joined.astype(jnp.bfloat16)
        last_hops[i].start()
        if i == 2:
            back_down.start()
            back_up.start()
    finals.finish_x()
    finals.start_z2()
    edges.finish_z()
    edges.start_x()
    own_out[...] = hidden_units(normed_ref[:, :model]) + middle_ref[...]
    finals.finish_z2()
    finals.start_core2()
    edges.finish_x()
    edges.start_core2()
    finals.finish_core2(full)
    state = jnp.zeros((STATE, inner), jnp.float32)
    for r in range(requests):
        state = jnp.where(info[12 + r] == me, full[r].astype(jnp.float32), state)
    new_state_ref[...] = state
    edges.finish_core2(full_edge)
    gathered = full_edge[0].astype(jnp.float32)
    edge = jnp.zeros((EDGE, inner), jnp.float32)
    for r in range(requests):
        owned = info[12 + r] == me
        edge = jnp.where(owned, gathered[r * EDGE : (r + 1) * EDGE], edge)
    new_edge_ref[...] = edge.astype(jnp.bfloat16)
    for i in order:
        last_hops[i].wait_recv()
    back_down.wait_recv()
    back_up.wait_recv()
    total = own_out[...] + low_in[:, :model].astype(jnp.float32)
    total = total + high_in[:, :model].astype(jnp.float32)
    out_ref[...] = jnp.transpose(total).astype(jnp.bfloat16)
    for copy in out_hops + on_hops + far_hops + last_hops + [up_b, down_a, back_down, back_up]:
        copy.wait_send()


def mlp_call(devices, info, args, weights, rows, model, inner, requests):
    f32, bf16 = jnp.float32, jnp.bfloat16
    hidden = weights[0].shape[1]
    wide = padded(model)
    return pl.pallas_call(
        functools.partial(mlp_stage, devices),
        out_shape=(
            jax.ShapeDtypeStruct((model, rows), bf16),
            jax.ShapeDtypeStruct((STATE, inner), f32),
            jax.ShapeDtypeStruct((EDGE, inner), bf16),
        ),
        in_specs=[sspec()] + [hspec()] * (len(args) + len(weights)),
        out_specs=tuple([vspec()] * 3),
        scratch_shapes=[
            VMEM((rows, wide), bf16),
            VMEM((rows, model), f32),
            VMEM((requests, STATE, inner), f32),
            VMEM((16, inner), f32),
            VMEM((model, hidden), bf16),
            VMEM((model, hidden), bf16),
            VMEM((model, hidden), bf16),
            pltpu.SemaphoreType.DMA((7,)),
            VMEM((rows, wide), bf16),
            VMEM((rows, wide), bf16),
            VMEM((rows, wide), bf16),
            VMEM((rows, wide), bf16),
            VMEM((rows, wide), bf16),
            VMEM((rows, wide), bf16),
            VMEM((rows, model), f32),
            VMEM((rows, wide), bf16),
            VMEM((rows, wide), bf16),
            VMEM((rows, wide), bf16),
            pltpu.SemaphoreType.DMA((2, 20)),
            VMEM((requests, 16, inner), bf16),
            VMEM((1, 16, inner), bf16),
        ]
        + Spread.scratch(devices, inner, requests, True)
        + Spread.scratch(devices, inner, 1, False),
        compiler_params=pltpu.CompilerParams(
            vmem_limit_bytes=61 << 20, collective_id=1, has_side_effects=True
        ),
        cost_estimate=pl.CostEstimate(
            flops=7_000_000_000, bytes_accessed=16_000_000, transcendentals=1_000_000
        ),
        name="mlp_stage",
    )(info, *args, *weights)


def handing_stage(*refs):
    count = len(refs) // 2
    for i in range(count):
        refs[count + i][...] = refs[i][...]


def handed(*arrays):
    return pl.pallas_call(
        handing_stage,
        out_shape=tuple(jax.ShapeDtypeStruct(a.shape, a.dtype) for a in arrays),
        in_specs=[vspec()] * len(arrays),
        out_specs=tuple([vspec()] * len(arrays)),
        name="handing_stage",
    )(*arrays)


def shards(
    hidden_in,
    mamba_in,
    conv_weight,
    conv_bias,
    x_proj,
    dt_proj,
    dt_bias,
    decay_rate,
    skip_gain,
    out_proj,
    norm_gain,
    mlp_gate,
    mlp_up,
    mlp_down,
    cache_state,
    cache_edge,
    req_lengths,
    cont_flag,
    cache_source,
    owner_slot,
):
    rows, inner = mamba_in.shape[1:]
    model = hidden_in.shape[2]
    requests = req_lengths.shape[1]
    devices = lax.axis_size("seq")
    place = lax.axis_index("seq")
    info = jnp.concatenate(
        [
            req_lengths[0],
            cont_flag[0],
            cache_source[0],
            owner_slot[0],
            jnp.reshape(place * rows, (1,)).astype(jnp.int32),
        ]
    )
    mixed, step, proj, enter, last_edge, start_state, params = front_call(
        devices,
        info,
        (
            conv_weight,
            conv_bias,
            dt_bias,
            decay_rate,
            skip_gain,
            norm_gain,
            mamba_in[0],
            cache_state[0, 0],
            cache_edge[0, 0],
            x_proj.T,
            dt_proj,
        ),
        rows,
        inner,
        x_proj.shape[1],
        requests,
    )
    middle, normed, finals = scan_call(
        info,
        (mixed, step, proj, enter, start_state, params, hidden_in[0].T),
        out_proj.T,
        rows,
        inner,
        model,
        requests,
    )
    block_out, new_state, new_edge = handed(
        *mlp_call(
            devices,
            info,
            (normed, middle, finals, last_edge),
            (mlp_gate, mlp_up, mlp_down.T),
            rows,
            model,
            inner,
            requests,
        )
    )
    return block_out.T[None], new_state[None, None], new_edge[None, None]


def solution(mesh):
    grouped = P("req", "seq", None)
    slots = P("req", "seq", None, None)
    return jax.shard_map(
        shards,
        mesh=mesh,
        in_specs=(grouped, grouped)
        + (P(),) * 9
        + (P(None, "req"), P(None, "req"), P("req", None), slots, slots)
        + (P("req", None),) * 4,
        out_specs=(grouped, slots, slots),
        check_vma=False,
    )
```
